32 devices in a mesh: slides: 2 (over x), cols: 8 (over z, y), rows: 2 (over core).
Axes of the slice: x: 2, y: 2, z: 4, core: 2. Of those that a mesh axis runs over, the one named last changes fastest.
Arguments:
- pixels: bfloat16 [3, 256, 8192], P(None, 'rows', ('slides', 'cols')), parts along dimension 2, may hold values from -6 to 6
- patch_weight: bfloat16 [24, 24, 3, 768], replicated, may hold values from -0.15625 to 0.15625
- patch_bias: float32 [768], replicated, may hold values from -3 to 3
- norm_gain: float32 [768], replicated, may hold values from 0.1 to 1.9
- gate_weight: bfloat16 [768, 1536], replicated, may hold values from -0.21875 to 0.21875
- mix_weight: bfloat16 [768, 1664], replicated, may hold values from -0.21875 to 0.21875
- step_weight: bfloat16 [768, 24], replicated, may hold values from -0.21875 to 0.21875
- step_bias: float32 [24], replicated, may hold values from -5 to -2
- log_rate: float32 [24], replicated, may hold values from -11 to 2
- conv_weight: float32 [4, 1664], replicated, may hold values from -3 to 3
- conv_bias: float32 [1664], replicated, may hold values from -3 to 3
- skip_gain: float32 [24], replicated, may hold values from 0.25 to 2
- out_gain: float32 [1536], replicated, may hold values from 0.1 to 1.9
- out_weight: bfloat16 [1536, 768], replicated, may hold values from -0.15625 to 0.15625
Outputs:
- layer_out: bfloat16 [8192, 768], P(('slides', 'cols', 'rows')), parts along dimension 0
The draws below stay inside these ranges and needn't reach their ends.
There are 2 independent parts, one for each index of `slides`. The reference program is written for one: setup_inputs(seed, part) draws one part's arguments, and reference() takes and returns one part's arrays. A program takes and returns all parts, laid end to end along the dimension named above; an argument that names none is the same for every part. Nothing has to cross between parts.
All inputs are finite; a program needn't handle non-finite values.
Results may differ from the reference program's by a relative error of at most 0.011.
Values may be sent and summed in bfloat16 or wider, within the bound.
No kernel may reach another device: no remote copies, remote signals or barrier semaphores. Data moves between devices by JAX's collectives and lax.ppermute only.
A program may use at most 192 MiB of HBM per device.

```python
from functools import partial
import jax
import jax.numpy as jnp
from jax import lax

D = 768
E = 1536
HDIM = 64
NSTATE = 64
CONVK = 4
CHAN = 3
PATCH = 16
KERNEL = 24
BAND = 256
SPAN = 256
HEADS = 24
TOKENS = 4096
WIDTH_PX = 4096


def head_rates(key):
    folded = jax.random.fold_in(key, 4242)
    key_base, key_order, key_slow, key_fast = jax.random.split(folded, 4)
    base_step = jnp.exp(jax.random.uniform(key_base, (HEADS,), jnp.float32, jnp.log(0.01), jnp.log(0.1)))
    slow_count = HEADS // 2
    ranking = jax.random.permutation(key_order, HEADS)
    slow_rate = jnp.exp(jax.random.uniform(key_slow, (HEADS,), jnp.float32, jnp.log(0.3 / TOKENS), jnp.log(1.5 / TOKENS)))
    fast_rate = jnp.exp(jax.random.uniform(key_fast, (HEADS,), jnp.float32, jnp.log(1.0 / 50.0), jnp.log(1.0 / 20.0)))
    head_rate = jnp.where(ranking < slow_count, slow_rate, fast_rate)
    return (base_step, head_rate)


def draw_step_bias(key, part):
    return jnp.log(jnp.expm1(head_rates(key)[0]))


def draw_log_rate(key, part):
    base_step, head_rate = head_rates(key)
    return jnp.log(head_rate / base_step)


def levels(own_key, extent, cuts, least, high):
    def one(position, blocks):
        steps = jax.random.uniform(jax.random.fold_in(jax.random.fold_in(own_key, 6), position), (blocks,), jnp.float32, least / len(cuts), high / len(cuts))
        return jnp.repeat(jnp.exp(steps), extent[position] // blocks).reshape((-1,) + (1,) * (len(extent) - position - 1))

    level = one(*cuts[0])
    for cut in cuts[1:]:
        level = level * one(*cut)
    return level


def noise(rng, dims, spread, reach, shards=(), held_as=jnp.bfloat16):
    values = spread * jax.random.normal(rng, dims, jnp.float32)
    if shards:
        values = values * levels(rng, dims, shards, -0.22, 0.18)
    return jnp.clip(values, -reach, reach).astype(held_as)


def setup_inputs(seed: int = 0, part: int = 0) -> dict:
    keys = jax.random.split(jax.random.key(seed), 15)
    part_splits = jax.random.split(jax.random.fold_in(keys[14], part), 15)
    pixels = noise(part_splits[0], (CHAN, BAND, WIDTH_PX), 1.0, 6.0, ((1, 2), (2, 8)))
    patch_weight = noise(keys[1], (KERNEL, KERNEL, CHAN, D), (KERNEL * KERNEL * CHAN) ** -0.5, 0.15625)
    patch_bias = noise(keys[2], (D,), 0.5, 3.0, (), jnp.float32)
    norm_gain = jnp.clip(1.0 + 0.18 * jax.random.normal(keys[3], (D,), jnp.float32), 0.1, 1.9)
    gate_weight = noise(keys[4], (D, E), D ** -0.5, 0.21875)
    mix_weight = noise(keys[5], (D, E + 2 * NSTATE), D ** -0.5, 0.21875)
    step_weight = noise(keys[6], (D, HEADS), D ** -0.5, 0.21875)
    step_bias = draw_step_bias(jax.random.fold_in(keys[14], 71), part)
    log_rate = draw_log_rate(jax.random.fold_in(keys[14], 71), part)
    conv_weight = noise(keys[9], (CONVK, E + 2 * NSTATE), CONVK ** -0.5, 3.0, (), jnp.float32)
    conv_bias = noise(keys[10], (E + 2 * NSTATE,), 0.5, 3.0, (), jnp.float32)
    skip_gain = jnp.clip(jax.random.uniform(keys[11], (HEADS,), jnp.float32, 0.25, 2.0), 0.25, 2.0)
    out_gain = jnp.clip(1.0 + 0.18 * jax.random.normal(keys[12], (E,), jnp.float32), 0.1, 1.9)
    out_weight = noise(keys[13], (E, D), E ** -0.5, 0.15625)
    return dict(pixels=pixels, patch_weight=patch_weight, patch_bias=patch_bias, norm_gain=norm_gain, gate_weight=gate_weight, mix_weight=mix_weight, step_weight=step_weight, step_bias=step_bias, log_rate=log_rate, conv_weight=conv_weight, conv_bias=conv_bias, skip_gain=skip_gain, out_gain=out_gain, out_weight=out_weight)


def rms_scale(values, gains):
    mean_sq = lax.optimization_barrier(jnp.mean(values * values, axis=-1, keepdims=True))
    return values * lax.rsqrt(mean_sq + 1e-05) * gains.astype(jnp.float32)

def block_step(carry_state, pieces, skip_vec):
    head_in, b_mat, c_mat, step_size, log_decay = pieces
    cum_decay = jnp.cumsum(log_decay, axis=0)
    scores = jnp.dot(c_mat, b_mat.T, preferred_element_type=jnp.float32)
    cum_heads = cum_decay.T
    decay_gap = cum_heads[:, :, None] - cum_heads[:, None, :]
    causal = jnp.arange(SPAN)[:, None] >= jnp.arange(SPAN)[None, :]
    decay_w = jnp.where(causal, jnp.exp(jnp.where(causal, decay_gap, 0.0)), 0.0)
    weights = (scores[None] * decay_w * step_size.T[:, None, :]).astype(jnp.bfloat16)
    inputs_f = head_in.astype(jnp.float32)
    y_intra = jnp.einsum('hts,shp->thp', weights.astype(jnp.float32), inputs_f)
    y_state = jnp.exp(cum_decay)[:, :, None] * jnp.einsum('hpn,tn->thp', carry_state, c_mat.astype(jnp.float32), precision=lax.Precision.HIGHEST)
    to_end = jnp.exp(cum_decay[-1:] - cum_decay) * step_size
    fresh_state = jnp.einsum('thp,tn->hpn', inputs_f * to_end[:, :, None], b_mat.astype(jnp.float32), precision=lax.Precision.HIGHEST)
    next_state = jnp.exp(cum_decay[-1])[:, None, None] * carry_state + fresh_state
    result = y_intra + y_state + skip_vec[None, :, None] * inputs_f
    return (next_state, result)

def reference(pixels, patch_weight, patch_bias, norm_gain, gate_weight, mix_weight, step_weight, step_bias, log_rate, conv_weight, conv_bias, skip_gain, out_gain, out_weight):
    margin = (KERNEL - PATCH) // 2
    embed_grid = lax.conv_general_dilated(pixels[None], patch_weight, (PATCH, PATCH), ((margin, margin), (margin, margin)), dimension_numbers=('NCHW', 'HWIO', 'NHWC'), preferred_element_type=jnp.float32)[0]
    embedded = (embed_grid + patch_bias.astype(jnp.float32)).astype(jnp.bfloat16).reshape(TOKENS, D)
    resid = embedded.astype(jnp.float32)
    normed = rms_scale(resid, norm_gain).astype(jnp.bfloat16)
    gate_proj = jnp.dot(normed, gate_weight, preferred_element_type=jnp.float32).astype(jnp.bfloat16)
    mixed_raw = jnp.dot(normed, mix_weight, preferred_element_type=jnp.float32).astype(jnp.bfloat16)
    step_raw = jnp.dot(normed, step_weight, preferred_element_type=jnp.float32)
    window = jnp.concatenate([jnp.zeros((CONVK - 1, E + 2 * NSTATE), jnp.bfloat16), mixed_raw], 0).astype(jnp.float32)
    conv_sum = conv_bias.astype(jnp.float32)
    for offset in range(CONVK):
        conv_sum = conv_sum + conv_weight[offset].astype(jnp.float32) * window[offset:offset + TOKENS]
    mixed = jax.nn.silu(conv_sum).astype(jnp.bfloat16)
    step_size = jax.nn.softplus(step_raw + step_bias.astype(jnp.float32))
    log_decay = -step_size * jnp.exp(log_rate.astype(jnp.float32))
    blocks = TOKENS // SPAN
    head_in = mixed[:, :E].reshape(blocks, SPAN, HEADS, HDIM)
    b_mat = mixed[:, E:E + NSTATE].reshape(blocks, SPAN, NSTATE)
    c_mat = mixed[:, E + NSTATE:].reshape(blocks, SPAN, NSTATE)
    start_state = jnp.zeros((HEADS, HDIM, NSTATE), jnp.float32)
    stepper = partial(block_step, skip_vec=skip_gain.astype(jnp.float32))
    unused_state, head_out = lax.scan(stepper, start_state, (head_in, b_mat, c_mat, step_size.reshape(blocks, SPAN, HEADS), log_decay.reshape(blocks, SPAN, HEADS)))
    gated = head_out.reshape(TOKENS, E) * jax.nn.silu(gate_proj.astype(jnp.float32))
    hidden = rms_scale(gated, out_gain).astype(jnp.bfloat16)
    return (jnp.dot(hidden, out_weight, preferred_element_type=jnp.float32) + resid).astype(jnp.bfloat16)
```

```python
from functools import partial

import jax
import jax.numpy as jnp
from jax import lax
from jax.experimental import pallas as pl
from jax.experimental.pallas import tpu as pltpu
from jax.sharding import PartitionSpec as P

E = 1536
D = 768
HDIM = 64
NSTATE = 64
PATCH = 16
KERNEL = 24
SPAN = 256
HEADS = 24
CHAN = 3
MARGIN = (KERNEL - PATCH) // 2
WIN = CHAN * KERNEL
LEAD = 8
F32 = jnp.float32
BF16 = jnp.bfloat16


def vmem():
    return pl.BlockSpec(memory_space=pltpu.VMEM)


def call(kernel, inputs, outs, scratch=(), limit=24, flops=0, moved=0, name=None):
    return pl.pallas_call(
        kernel,
        out_shape=outs,
        in_specs=[vmem()] * len(inputs),
        out_specs=jax.tree.map(lambda _: vmem(), outs),
        scratch_shapes=scratch,
        compiler_params=pltpu.CompilerParams(vmem_limit_bytes=limit << 20),
        cost_estimate=pl.CostEstimate(flops=flops, bytes_accessed=moved, transcendentals=0),
        name=name,
    )(*inputs)


def shape(dims, kind=BF16):
    return jax.ShapeDtypeStruct(dims, kind)


def pack_kernel(own, partner, *refs):
    outs, rows = refs[:-1], refs[-1]
    col, row = lax.axis_index("cols"), lax.axis_index("rows")
    local = own.shape[1]
    width = own.shape[2]
    edge = jnp.zeros((CHAN, 32, width), BF16)
    rows[:, 0:32, :] = edge
    rows[:, 32 + 2 * local : 64 + 2 * local, :] = edge
    rows[:, pl.ds(pl.multiple_of(32 + local * row, 32), local), :] = own[...]
    rows[:, pl.ds(pl.multiple_of(32 + local * (1 - row), 32), local), :] = partner[...]
    for step, out in enumerate(outs):
        token_row = 2 * (col ^ step) + row
        first = pl.multiple_of(PATCH * token_row, PATCH)
        pieces, tails = [], []
        for channel in range(CHAN):
            block = rows[channel, pl.ds(first, 64), :].astype(F32)
            pieces.append(block[28:52])
            before = block[12:28, width - 64 :]
            tails += [before[:8], before[8:]]
        tails.append(jnp.zeros((8, width - 64 * len(tails)), F32))
        pieces.append(jnp.concatenate(tails, axis=1))
        out[...] = jnp.concatenate(pieces, axis=0).astype(BF16)


def embed_kernel(*refs):
    blocks, (weight, bias, out, strip, tail, wide) = refs[:-6], refs[-6:]
    col = lax.axis_index("cols")
    width = blocks[0].shape[1]
    count = len(blocks)
    strip[0:LEAD, :] = jnp.zeros((LEAD, 128), F32)
    strip[LEAD + count * width :, :] = jnp.zeros((LEAD, 128), F32)
    blank = jnp.zeros((128 - WIN, width), F32)
    for step, block in enumerate(blocks):
        source = col ^ step
        values = block[0:WIN, :].astype(F32)
        flipped = jnp.concatenate([values, blank], axis=0).T
        strip[pl.ds(pl.multiple_of(LEAD + source * width, 8), width), :] = flipped

        @pl.when(source == count - 1)
        def _():
            whole = block[...].astype(F32)
            extra = whole[WIN : WIN + 8]
            pieces = []
            for channel in range(CHAN):
                pieces += [extra[:, 128 * channel : 128 * channel + 64]]
                pieces += [extra[:, 128 * channel + 64 : 128 * channel + 128]]
                pieces += [whole[KERNEL * channel : KERNEL * channel + 8, width - 64 :]]
            pieces.append(jnp.zeros((128 - WIN, 64), F32))
            last = jnp.concatenate(pieces, axis=0)
            last = jnp.concatenate([last, jnp.zeros((128, 64), F32)], axis=1).T
            tail[0:72, :] = jnp.zeros((72, 128), F32)
            tail[72:136, :] = last[:64]
            tail[136:144, :] = jnp.zeros((8, 128), F32)

    tokens = count * width // PATCH
    for offset in range(KERNEL):
        start = LEAD - MARGIN + offset
        lanes = pl.ds(offset * 128, 128)
        part = jnp.concatenate(
            [tail[pl.ds(start, LEAD, stride=PATCH), :], strip[pl.ds(start, tokens, stride=PATCH), :]], axis=0
        )
        wide[:, lanes] = part.astype(BF16)
    grid = jnp.dot(wide[...], weight[...], preferred_element_type=F32)
    out[...] = (grid + bias[...]).astype(BF16)


def spread_matrix():
    head = lax.broadcasted_iota(jnp.int32, (HEADS, E), 0)
    lane = lax.broadcasted_iota(jnp.int32, (HEADS, E), 1)
    return ((lane >= head * HDIM) & (lane < (head + 1) * HDIM)).astype(BF16)


def halves(values):
    high = values.astype(BF16)
    return high, (values - high.astype(F32)).astype(BF16)


def spread(values, matrix):
    high, low = halves(values)
    return jnp.dot(high, matrix, preferred_element_type=F32) + jnp.dot(low, matrix, preferred_element_type=F32)


def softplus(values):
    small = jnp.exp(-jnp.abs(values))
    return jnp.maximum(values, 0.0) + jnp.log1p(small)


def mix_kernel(
    embedded, norm_gain, mix_weight, step_weight, step_bias, log_rate, conv_weight, conv_bias,
    normed_out, x_out, b_out, c_out, step_out, cum_out, keep_out, send_out, raw, state,
):
    col, row = lax.axis_index("cols"), lax.axis_index("rows")
    resid = embedded[...].astype(F32)
    mean_sq = jnp.mean(resid * resid, axis=-1, keepdims=True)
    normed_f = resid * lax.rsqrt(mean_sq + 1e-05) * norm_gain[...]
    normed = normed_f.astype(BF16)
    normed_out[...] = normed_f[LEAD:].astype(BF16)
    length = embedded.shape[0] - LEAD
    raw[...] = jnp.dot(normed, mix_weight[...], preferred_element_type=F32).astype(BF16).astype(F32)

    @pl.when((col == 0) & (row == 0))
    def _():
        raw[0:LEAD, :] = jnp.zeros((LEAD, raw.shape[1]), F32)

    step_raw = jnp.dot(normed, step_weight[...], preferred_element_type=F32)[LEAD:]
    step = softplus(step_raw + step_bias[...])
    log_decay = -step * jnp.exp(log_rate[...])
    lower = (
        lax.broadcasted_iota(jnp.int32, (length, length), 0) >= lax.broadcasted_iota(jnp.int32, (length, length), 1)
    ).astype(BF16)
    high = log_decay.astype(BF16)
    middle = (log_decay - high.astype(F32)).astype(BF16)
    cum = jnp.dot(lower, high, preferred_element_type=F32)
    cum = cum + jnp.dot(lower, middle, preferred_element_type=F32)
    low = (log_decay - high.astype(F32) - middle.astype(F32)).astype(BF16)
    cum = cum + jnp.dot(lower, low, preferred_element_type=F32)
    step_out[...] = step
    cum_out[...] = cum
    matrix = spread_matrix()
    last = cum[length - 1 :]
    to_end = spread(jnp.exp(last - cum) * step, matrix)
    decay = spread(jnp.broadcast_to(jnp.exp(last), (8, HEADS)), matrix)
    taps = conv_weight.shape[0]
    chunk = 64
    scaled = []
    maps = []
    for first in range(0, length, chunk):
        total = jnp.broadcast_to(conv_bias[...], (chunk, raw.shape[1]))
        for tap in range(taps):
            total = total + conv_weight[tap : tap + 1, :] * raw[pl.ds(LEAD - taps + 1 + tap + first, chunk), :]
        mixed = (total * jax.nn.sigmoid(total)).astype(BF16)
        x_out[pl.ds(first, chunk), :] = mixed[:, :E]
        mixed_f = mixed[:, E:].astype(F32)
        b_out[pl.ds(first, chunk), :] = mixed_f[:, :NSTATE].astype(BF16)
        c_out[pl.ds(first, chunk), :] = mixed_f[:, NSTATE:].astype(BF16)
        maps.append(mixed_f[:, :NSTATE])
        scaled.append((mixed[:, :E].astype(F32) * to_end[first : first + chunk]).astype(BF16))
    b_t = jnp.concatenate(maps, axis=0).T.astype(BF16)
    state[0:NSTATE, :] = jnp.dot(b_t, jnp.concatenate(scaled, axis=0), preferred_element_type=F32)
    state[NSTATE : NSTATE + 8, :] = decay
    half = E // 2
    mine = pl.ds(pl.multiple_of(row * half, 128), half)
    theirs = pl.ds(pl.multiple_of((1 - row) * half, 128), half)
    keep_out[...] = state[:, mine]
    send_out[...] = wire(state[0:NSTATE, theirs], state[NSTATE : NSTATE + 8, theirs])


def wire(values, decay):
    high = decay.astype(BF16).astype(F32)
    rest = decay - high
    place = lax.broadcasted_iota(jnp.int32, decay.shape, 0)
    return jnp.concatenate([values, jnp.where(place == 0, high, rest)], axis=0).astype(BF16)


def unwire(message):
    values = message[0:NSTATE, :].astype(F32)
    rows = message[NSTATE : NSTATE + 8, :].astype(F32)
    return values, jnp.broadcast_to(rows[0:1] + rows[1:2], rows.shape)


def scale(decay, values):
    return decay[0:1] * values


def pair_kernel(keep, received, total_out, message_out):
    row = lax.axis_index("rows")
    own, own_decay = keep[0:NSTATE, :], keep[NSTATE : NSTATE + 8, :]
    other, other_decay = unwire(received)
    upper = row == 1
    last_decay = jnp.where(upper, own_decay, other_decay)
    values = scale(last_decay, jnp.where(upper, other, own)) + jnp.where(upper, own, other)
    decay = own_decay * other_decay
    total_out[0:NSTATE, :] = values
    total_out[NSTATE : NSTATE + 8, :] = decay
    message_out[...] = wire(values, decay)


def join_kernel(bit, total, before, received, total_out, before_out, message_out):
    col = lax.axis_index("cols")
    later = (col & bit) != 0
    values, decay = total[0:NSTATE, :], total[NSTATE : NSTATE + 8, :]
    came, came_decay = unwire(received)
    last_decay = jnp.where(later, decay, came_decay)
    joined = scale(last_decay, jnp.where(later, came, values)) + jnp.where(later, values, came)
    total_out[0:NSTATE, :] = joined
    total_out[NSTATE : NSTATE + 8, :] = decay * came_decay
    message_out[...] = wire(joined, decay * came_decay)
    if before is None:
        before_out[0:NSTATE, :] = jnp.where(later, came, 0.0)
        before_out[NSTATE : NSTATE + 8, :] = jnp.where(later, came_decay, 1.0)
    else:
        ahead, ahead_decay = before[0:NSTATE, :], before[NSTATE : NSTATE + 8, :]
        before_out[0:NSTATE, :] = jnp.where(later, scale(ahead_decay, came) + ahead, ahead)
        before_out[NSTATE : NSTATE + 8, :] = jnp.where(later, ahead_decay * came_decay, ahead_decay)


def enter_kernel(bit, before, last, keep, received, mine_out, theirs_out):
    col, row = lax.axis_index("cols"), lax.axis_index("rows")
    later = (col & bit) != 0
    ahead, ahead_decay = before[0:NSTATE, :], before[NSTATE : NSTATE + 8, :]
    came, came_decay = unwire(last)
    ahead = jnp.where(later, scale(ahead_decay, came) + ahead, ahead)
    other, other_decay = unwire(received)
    upper = row == 1
    low = jnp.where(upper, other, keep[0:NSTATE, :])
    low_decay = jnp.where(upper, other_decay, keep[NSTATE : NSTATE + 8, :])
    second = scale(low_decay, ahead) + low
    mine_out[...] = jnp.where(upper, second, ahead).astype(BF16)
    theirs_out[...] = jnp.where(upper, ahead, second).astype(BF16)


def gate_kernel(normed, gate_weight, out):
    gate = jnp.dot(normed[...], gate_weight[...], preferred_element_type=F32).astype(BF16).astype(F32)
    out[...] = gate * jax.nn.sigmoid(gate)


def intra_kernel(x, b_mat, c_mat, step, cum, skip, out):
    length = x.shape[0]
    half = length // 2
    scores = lax.dot_general(c_mat[...], b_mat[...], (((1,), (1,)), ((), ())), preferred_element_type=F32)
    causal = lax.broadcasted_iota(jnp.int32, (length, length), 0) >= lax.broadcasted_iota(
        jnp.int32, (length, length), 1
    )
    scores = jnp.where(causal, scores, 0.0)
    wide = jnp.zeros((length, 128 - HEADS), F32)
    cum_v = cum[...]
    cum_t = jnp.concatenate([cum_v, wide], axis=1).T
    step_t = jnp.concatenate([step[...], wide], axis=1).T
    for pair in range(HEADS // 2):
        x_pair = x[:, pair * 128 : (pair + 1) * 128]
        tops, bottoms = [], []
        for member in range(2):
            head = 2 * pair + member
            column = cum_v[:, head : head + 1]
            cum_row = cum_t[head : head + 1, :]
            step_row = step_t[head : head + 1, :]

            def weights(rows, span):
                gap = jnp.minimum(column[rows] - cum_row[:, span], 0.0)
                return (scores[rows, span] * jnp.exp(gap) * step_row[:, span]).astype(BF16)

            inputs = x_pair[:, member * HDIM : (member + 1) * HDIM]
            top = jnp.dot(weights(slice(0, half), slice(0, half)), inputs[:half], preferred_element_type=F32)
            bottom = jnp.dot(weights(slice(half, length), slice(0, length)), inputs, preferred_element_type=F32)
            tops.append(top)
            bottoms.append(bottom)
        direct = skip[:, pair * 128 : (pair + 1) * 128] * x_pair.astype(F32)
        out[0:half, pair * 128 : (pair + 1) * 128] = jnp.concatenate(tops, axis=1) + direct[:half]
        out[half:length, pair * 128 : (pair + 1) * 128] = jnp.concatenate(bottoms, axis=1) + direct[half:]


def finish_kernel(local, gate, c_mat, cum, mine, theirs, embedded, out_gain, out_weight, out, state):
    row = lax.axis_index("rows")
    half = E // 2
    state[:, pl.ds(pl.multiple_of(row * half, 128), half)] = mine[...]
    state[:, pl.ds(pl.multiple_of((1 - row) * half, 128), half)] = theirs[...]
    carried = jnp.dot(c_mat[...], state[...], preferred_element_type=F32)
    carried = carried * spread(jnp.exp(cum[...]), spread_matrix())
    gated = (local[...] + carried) * gate[...]
    mean_sq = jnp.mean(gated * gated, axis=-1, keepdims=True)
    hidden = (gated * lax.rsqrt(mean_sq + 1e-05) * out_gain[...]).astype(BF16)
    result = jnp.dot(hidden, out_weight[...], preferred_element_type=F32)
    out[...] = (result + embedded[...].astype(F32)[LEAD:]).astype(BF16)


def swap(block, axis, bit):
    return lax.ppermute(block, axis, [(i, i ^ bit) for i in range(lax.axis_size(axis))])


def embed_by_rows(pixels, patch_weight, patch_bias):
    col_count = lax.axis_size("cols")
    width = pixels.shape[2]
    partner = swap(pixels, "rows", 1)
    block = shape((WIN + 8, width))
    scratch = [pltpu.VMEM((CHAN, 2 * pixels.shape[1] + 64, width), BF16)]
    blocks = call(pack_kernel, (pixels, partner), [block] * col_count, scratch, name="pack")
    came = [blocks[0]] + [swap(blocks[s], "cols", s) for s in range(1, col_count)]
    weight = patch_weight.transpose(1, 2, 0, 3).reshape(KERNEL, WIN, D)
    weight = jnp.pad(weight, ((0, 0), (0, 128 - WIN), (0, 0))).reshape(KERNEL * 128, D)
    tokens = col_count * width // PATCH
    scratch = [
        pltpu.VMEM((2 * LEAD + col_count * width, 128), F32),
        pltpu.VMEM((144, 128), F32),
        pltpu.VMEM((LEAD + tokens, KERNEL * 128), BF16),
    ]
    flops = 2 * tokens * KERNEL * 128 * D
    return call(
        embed_kernel, (*came, weight, patch_bias.reshape(1, -1)), shape((LEAD + tokens, D)), scratch,
        flops=flops, moved=6 << 20, name="embed",
    )


def extended(block, sides, width):
    for axis, dim in sides:
        count = lax.axis_size(axis)
        forward = [(i, i + 1) for i in range(count - 1)]
        backward = [(target, source) for source, target in forward]
        low = lax.ppermute(
            lax.slice_in_dim(block, block.shape[dim] - width, None, axis=dim), axis, forward
        )
        high = lax.ppermute(lax.slice_in_dim(block, 0, width, axis=dim), axis, backward)
        block = jnp.concatenate([low, block, high], axis=dim)
    return block


def shifted(block, axis, distance):
    devices = range(lax.axis_size(axis))
    route = [(i - distance, i) for i in devices if i - distance in devices]
    return lax.ppermute(block, axis, route)


def embed_by_blocks(pixels, patch_weight, patch_bias):
    padded = extended(pixels, (("cols", 2), ("rows", 1)), MARGIN)
    embed_grid = lax.conv_general_dilated(
        padded[None],
        patch_weight,
        (PATCH, PATCH),
        "VALID",
        dimension_numbers=("NCHW", "HWIO", "NHWC"),
        preferred_element_type=jnp.float32,
    )[0]
    embed_grid = (embed_grid + patch_bias).astype(jnp.bfloat16)
    row_local, col_local, feature_width = embed_grid.shape
    devices = lax.axis_size(("cols", "rows"))
    row_count = lax.axis_size("rows")
    col_count = lax.axis_size("cols")
    groups = col_count // row_local
    piece_len = col_local * feature_width // devices
    outgoing = embed_grid.reshape(row_local, devices, piece_len)
    spread = lax.all_to_all(outgoing, ("cols", "rows"), split_axis=1, concat_axis=1, tiled=True)
    spread = spread.reshape(row_local, groups, row_local, row_count, piece_len).transpose(
        3, 0, 1, 2, 4
    )
    landed = lax.all_to_all(
        spread.reshape(devices, row_local, piece_len),
        ("cols", "rows"),
        split_axis=0,
        concat_axis=0,
        tiled=True,
    )
    tokens = landed.transpose(1, 0, 2).reshape(row_local * col_local, feature_width)
    tail = shifted(tokens[tokens.shape[0] - LEAD :], ("cols", "rows"), 1)
    return jnp.concatenate([tail, tokens], axis=0)


def body(
    pixels,
    patch_weight,
    patch_bias,
    norm_gain,
    gate_weight,
    mix_weight,
    step_weight,
    step_bias,
    log_rate,
    conv_weight,
    conv_bias,
    skip_gain,
    out_gain,
    out_weight,
):
    col_count = lax.axis_size("cols")
    row_local = pixels.shape[1] // PATCH
    if col_count == row_local:
        embedded = embed_by_rows(pixels, patch_weight, patch_bias)
    else:
        embedded = embed_by_blocks(pixels, patch_weight, patch_bias)
    length = embedded.shape[0] - LEAD
    line = lambda a: a.reshape(1, -1)
    mixed_width = mix_weight.shape[1]
    half = E // 2
    packed = NSTATE + 8
    normed, x, b_mat, c_mat, step, cum, keep, send = call(
        mix_kernel,
        (
            embedded, line(norm_gain), mix_weight, step_weight, line(step_bias), line(log_rate),
            conv_weight, line(conv_bias),
        ),
        [
            shape((length, D)), shape((length, E)), shape((length, NSTATE)), shape((length, NSTATE)),
            shape((length, HEADS), F32), shape((length, HEADS), F32), shape((packed, half), F32),
            shape((packed, half)),
        ],
        [pltpu.VMEM((LEAD + length, mixed_width), F32), pltpu.VMEM((packed, E), F32)],
        flops=2 * length * D * mixed_width, moved=4 << 20, name="mix",
    )
    came = swap(send, "rows", 1)
    summary, message = shape((packed, half), F32), shape((packed, half))
    total, out = call(pair_kernel, (keep, came), [summary, message], name="pair")
    skip = line(jnp.repeat(skip_gain, HDIM))
    gate = call(
        gate_kernel, (normed, gate_weight), shape((length, E), F32),
        flops=2 * length * D * E, moved=4 << 20, name="gate",
    )
    local = call(
        intra_kernel, (x, b_mat, c_mat, step, cum, skip), shape((length, E), F32),
        flops=HEADS * length * length * 256, moved=4 << 20, name="intra",
    )
    before, bit = None, 1
    while 2 * bit < col_count:
        arrived = swap(out, "cols", bit)
        if before is None:
            kernel = lambda t, r, *outs, bit=bit: join_kernel(bit, t, None, r, *outs)
            total, before, out = call(kernel, (total, arrived), [summary, summary, message], name="join")
        else:
            total, before, out = call(
                partial(join_kernel, bit), (total, before, arrived), [summary, summary, message], name="join"
            )
        bit *= 2
    arrived = swap(out, "cols", bit)
    entering = shape((NSTATE, half))
    mine, theirs = call(partial(enter_kernel, bit), (before, arrived, keep, came), [entering, entering], name="enter")
    theirs = swap(theirs, "rows", 1)
    return call(
        finish_kernel,
        (local, gate, c_mat, cum, mine, theirs, embedded, line(out_gain), out_weight),
        shape((length, D)),
        [pltpu.VMEM((NSTATE, E), BF16)],
        flops=2 * length * D * E, moved=4 << 20, name="finish",
    )


def solution(mesh):
    placed = (
        P(None, "rows", ("slides", "cols")),
        P(),
        P(),
        P(),
        P(),
        P(),
        P(),
        P(),
        P(),
        P(),
        P(),
        P(),
        P(),
        P(),
    )
    return jax.shard_map(
        body,
        mesh=mesh,
        in_specs=placed,
        out_specs=P(("slides", "cols", "rows"), None),
        check_vma=False,
    )
```

```python
from functools import partial

import jax
import jax.numpy as jnp
from jax import lax
from jax.experimental import pallas as pl
from jax.experimental.pallas import tpu as pltpu
from jax.sharding import PartitionSpec as P


E = 1536
D = 768
HDIM = 64
NSTATE = 64
PATCH = 16
KERNEL = 24
HEADS = 24
CHAN = 3
MARGIN = (KERNEL - PATCH) // 2
WIN = CHAN * KERNEL
LEAD = 8
F32 = jnp.float32
BF16 = jnp.bfloat16


def vmem():
    return pl.BlockSpec(memory_space=pltpu.VMEM)


def call(kernel, inputs, outs, scratch=(), limit=4, flops=0, moved=0, scalars=0):
    return pl.pallas_call(
        kernel,
        out_shape=outs,
        in_specs=[pl.BlockSpec(memory_space=pltpu.SMEM)] * scalars + [vmem()] * (len(inputs) - scalars),
        out_specs=jax.tree.map(lambda _: vmem(), outs),
        scratch_shapes=scratch,
        compiler_params=pltpu.CompilerParams(vmem_limit_bytes=limit << 20),
        cost_estimate=pl.CostEstimate(flops=flops, bytes_accessed=moved, transcendentals=0),
    )(*inputs)


def shape(dims, kind=BF16):
    return jax.ShapeDtypeStruct(dims, kind)


def pack_kernel(own, partner, *refs):
    outs, rows = refs[:-1], refs[-1]
    col, row = lax.axis_index("cols"), lax.axis_index("rows")
    local = own.shape[1]
    width = own.shape[2]
    edge = jnp.zeros((CHAN, 32, width), BF16)
    rows[:, 0:32, :] = edge
    rows[:, 32 + 2 * local : 64 + 2 * local, :] = edge
    rows[:, pl.ds(pl.multiple_of(32 + local * row, 32), local), :] = own[...]
    rows[:, pl.ds(pl.multiple_of(32 + local * (1 - row), 32), local), :] = partner[...]
    for step, out in enumerate(outs):
        token_row = 2 * (col ^ step) + row
        first = pl.multiple_of(PATCH * token_row, PATCH)
        pieces, tails = [], []
        for channel in range(CHAN):
            block = rows[channel, pl.ds(first, 64), :].astype(F32)
            pieces.append(block[28:52])
            before = block[12:28, width - 64 :]
            tails += [before[:8], before[8:]]
        tails.append(jnp.zeros((8, width - 64 * len(tails)), F32))
        pieces.append(jnp.concatenate(tails, axis=1))
        out[...] = jnp.concatenate(pieces, axis=0).astype(BF16)


def stage_kernel(pixels, out):
    out[...] = pixels[...]


def embed_kernel(*refs):
    blocks, (weight, bias, out, strip, tail, wide) = refs[:-6], refs[-6:]
    col = lax.axis_index("cols")
    width = blocks[0].shape[1]
    count = len(blocks)
    strip[0:LEAD, :] = jnp.zeros((LEAD, 128), F32)
    strip[LEAD + count * width :, :] = jnp.zeros((LEAD, 128), F32)
    blank = jnp.zeros((128 - WIN, width), F32)
    for step, block in enumerate(blocks):
        source = col ^ step
        values = block[0:WIN, :].astype(F32)
        flipped = jnp.concatenate([values, blank], axis=0).T
        strip[pl.ds(pl.multiple_of(LEAD + source * width, 8), width), :] = flipped

        @pl.when(source == count - 1)
        def _():
            whole = block[...].astype(F32)
            extra = whole[WIN : WIN + 8]
            pieces = []
            for channel in range(CHAN):
                pieces += [extra[:, 128 * channel : 128 * channel + 64]]
                pieces += [extra[:, 128 * channel + 64 : 128 * channel + 128]]
                pieces += [whole[KERNEL * channel : KERNEL * channel + 8, width - 64 :]]
            pieces.append(jnp.zeros((128 - WIN, 64), F32))
            last = jnp.concatenate(pieces, axis=0)
            last = jnp.concatenate([last, jnp.zeros((128, 64), F32)], axis=1).T
            tail[0:72, :] = jnp.zeros((72, 128), F32)
            tail[72:136, :] = last[:64]
            tail[136:144, :] = jnp.zeros((8, 128), F32)

    tokens = count * width // PATCH
    for offset in range(KERNEL):
        start = LEAD - MARGIN + offset
        lanes = pl.ds(offset * 128, 128)
        part = jnp.concatenate(
            [tail[pl.ds(start, LEAD, stride=PATCH), :], strip[pl.ds(start, tokens, stride=PATCH), :]], axis=0
        )
        wide[:, lanes] = part.astype(BF16)
    grid = jnp.dot(wide[...], weight[...], preferred_element_type=F32)
    out[...] = (grid + bias[...]).astype(BF16)


def spread_matrix():
    head = lax.broadcasted_iota(jnp.int32, (HEADS, E), 0)
    lane = lax.broadcasted_iota(jnp.int32, (HEADS, E), 1)
    return ((lane >= head * HDIM) & (lane < (head + 1) * HDIM)).astype(BF16)


def halves(values):
    high = values.astype(BF16)
    return high, (values - high.astype(F32)).astype(BF16)


def spread(values, matrix):
    high, low = halves(values)
    return jnp.dot(high, matrix, preferred_element_type=F32) + jnp.dot(low, matrix, preferred_element_type=F32)


def softplus(values):
    small = jnp.exp(-jnp.abs(values))
    return jnp.maximum(values, 0.0) + jnp.log1p(small)


def mix_kernel(
    embedded, norm_gain, mix_weight, step_weight, step_bias, log_rate, conv_weight, conv_bias,
    normed_out, x_out, b_out, c_out, step_out, cum_out, keep_out, send_out, raw, state,
):
    col, row = lax.axis_index("cols"), lax.axis_index("rows")
    resid = embedded[...].astype(F32)
    mean_sq = jnp.mean(resid * resid, axis=-1, keepdims=True)
    normed_f = resid * lax.rsqrt(mean_sq + 1e-05) * norm_gain[...]
    normed = normed_f.astype(BF16)
    normed_out[...] = normed_f[LEAD:].astype(BF16)
    length = embedded.shape[0] - LEAD
    raw[...] = jnp.dot(normed, mix_weight[...], preferred_element_type=F32).astype(BF16).astype(F32)

    @pl.when((col == 0) & (row == 0))
    def _():
        raw[0:LEAD, :] = jnp.zeros((LEAD, raw.shape[1]), F32)

    step_raw = lax.dot_general(
        normed, step_weight[...], (((1,), (1,)), ((), ())), preferred_element_type=F32
    )[LEAD:]
    step = softplus(step_raw + step_bias[...])
    log_decay = -step * jnp.exp(log_rate[...])
    lower = (
        lax.broadcasted_iota(jnp.int32, (length, length), 0) >= lax.broadcasted_iota(jnp.int32, (length, length), 1)
    ).astype(BF16)
    high = log_decay.astype(BF16)
    middle = (log_decay - high.astype(F32)).astype(BF16)
    cum = jnp.dot(lower, high, preferred_element_type=F32)
    cum = cum + jnp.dot(lower, middle, preferred_element_type=F32)
    low = (log_decay - high.astype(F32) - middle.astype(F32)).astype(BF16)
    cum = cum + jnp.dot(lower, low, preferred_element_type=F32)
    step_out[...] = step
    cum_out[...] = cum
    matrix = spread_matrix()
    last = cum[length - 1 :]
    to_end = spread(jnp.exp(last - cum) * step, matrix)
    decay = spread(jnp.broadcast_to(jnp.exp(last), (8, HEADS)), matrix)
    taps = conv_weight.shape[0]
    chunk = 64
    scaled = []
    maps = []
    for first in range(0, length, chunk):
        total = jnp.broadcast_to(conv_bias[...], (chunk, raw.shape[1]))
        for tap in range(taps):
            total = total + conv_weight[tap : tap + 1, :] * raw[pl.ds(LEAD - taps + 1 + tap + first, chunk), :]
        mixed = (total * jax.nn.sigmoid(total)).astype(BF16)
        x_out[pl.ds(first, chunk), :] = mixed[:, :E]
        mixed_f = mixed[:, E:].astype(F32)
        b_out[pl.ds(first, chunk), :] = mixed_f[:, :NSTATE].astype(BF16)
        c_out[pl.ds(first, chunk), :] = mixed_f[:, NSTATE:].astype(BF16)
        maps.append(mixed_f[:, :NSTATE])
        scaled.append((mixed[:, :E].astype(F32) * to_end[first : first + chunk]).astype(BF16))
    b_t = jnp.concatenate(maps, axis=0).T.astype(BF16)
    state[0:NSTATE, :] = jnp.dot(b_t, jnp.concatenate(scaled, axis=0), preferred_element_type=F32)
    state[NSTATE : NSTATE + 8, :] = decay
    half = E // 2
    mine = pl.ds(pl.multiple_of(row * half, 128), half)
    theirs = pl.ds(pl.multiple_of((1 - row) * half, 128), half)
    keep_out[...] = state[:, mine]
    send_out[...] = wire(state[0:NSTATE, theirs], state[NSTATE : NSTATE + 8, theirs])


def wire(values, decay):
    high = decay.astype(BF16).astype(F32)
    rest = decay - high
    place = lax.broadcasted_iota(jnp.int32, decay.shape, 0)
    return jnp.concatenate([values, jnp.where(place == 0, high, rest)], axis=0).astype(BF16)


def unwire(message):
    values = message[0:NSTATE, :].astype(F32)
    rows = message[NSTATE : NSTATE + 8, :].astype(F32)
    return values, jnp.broadcast_to(rows[0:1] + rows[1:2], rows.shape)


def scale(decay, values):
    return decay[0:1] * values


def pair_kernel(keep, received, total_out, message_out):
    row = lax.axis_index("rows")
    own, own_decay = keep[0:NSTATE, :], keep[NSTATE : NSTATE + 8, :]
    other, other_decay = unwire(received)
    upper = row == 1
    last_decay = jnp.where(upper, own_decay, other_decay)
    values = scale(last_decay, jnp.where(upper, other, own)) + jnp.where(upper, own, other)
    decay = own_decay * other_decay
    total_out[0:NSTATE, :] = values
    total_out[NSTATE : NSTATE + 8, :] = decay
    message_out[...] = wire(values, decay)


def join_kernel(bit, total, before, received, total_out, before_out, message_out):
    col = lax.axis_index("cols")
    later = (col & bit) != 0
    values, decay = total[0:NSTATE, :], total[NSTATE : NSTATE + 8, :]
    came, came_decay = unwire(received)
    last_decay = jnp.where(later, decay, came_decay)
    joined = scale(last_decay, jnp.where(later, came, values)) + jnp.where(later, values, came)
    total_out[0:NSTATE, :] = joined
    total_out[NSTATE : NSTATE + 8, :] = decay * came_decay
    message_out[...] = wire(joined, decay * came_decay)
    if before is None:
        before_out[0:NSTATE, :] = jnp.where(later, came, 0.0)
        before_out[NSTATE : NSTATE + 8, :] = jnp.where(later, came_decay, 1.0)
    else:
        ahead, ahead_decay = before[0:NSTATE, :], before[NSTATE : NSTATE + 8, :]
        before_out[0:NSTATE, :] = jnp.where(later, scale(ahead_decay, came) + ahead, ahead)
        before_out[NSTATE : NSTATE + 8, :] = jnp.where(later, ahead_decay * came_decay, ahead_decay)


def enter_kernel(bit, before, last, keep, received, mine_out, theirs_out):
    col, row = lax.axis_index("cols"), lax.axis_index("rows")
    later = (col & bit) != 0
    ahead, ahead_decay = before[0:NSTATE, :], before[NSTATE : NSTATE + 8, :]
    came, _ = unwire(last)
    ahead = jnp.where(later, scale(ahead_decay, came) + ahead, ahead)
    other, other_decay = unwire(received)
    upper = row == 1
    low = jnp.where(upper, other, keep[0:NSTATE, :])
    low_decay = jnp.where(upper, other_decay, keep[NSTATE : NSTATE + 8, :])
    second = scale(low_decay, ahead) + low
    mine_out[...] = jnp.where(upper, second, ahead).astype(BF16)
    theirs_out[...] = jnp.where(upper, ahead, second).astype(BF16)


def gate_kernel(normed, gate_weight, out):
    gate = jnp.dot(normed[...], gate_weight[...], preferred_element_type=F32).astype(BF16).astype(F32)
    out[...] = gate * jax.nn.sigmoid(gate)


def intra_kernel(first, skip, x, b_mat, c_mat, step, cum, out):
    length = x.shape[0]
    half = length // 2
    scores = lax.dot_general(c_mat[...], b_mat[...], (((1,), (1,)), ((), ())), preferred_element_type=F32)
    causal = lax.broadcasted_iota(jnp.int32, (length, length), 0) >= lax.broadcasted_iota(
        jnp.int32, (length, length), 1
    )
    scores = jnp.where(causal, scores, 0.0)
    wide = jnp.zeros((length, 128 - HEADS), F32)
    cum_v = cum[...]
    cum_t = jnp.concatenate([cum_v, wide], axis=1).T
    step_t = jnp.concatenate([step[...], wide], axis=1).T
    for place in range(out.shape[1] // 128):
        pair = first + place
        x_pair = x[:, pair * 128 : (pair + 1) * 128]
        tops, bottoms = [], []
        for member in range(2):
            head = 2 * pair + member
            column = cum_v[:, head : head + 1]
            cum_row = cum_t[head : head + 1, :]
            step_row = step_t[head : head + 1, :]

            def weights(rows, span):
                gap = jnp.minimum(column[rows] - cum_row[:, span], 0.0)
                return (scores[rows, span] * jnp.exp(gap) * step_row[:, span]).astype(BF16)

            inputs = x_pair[:, member * HDIM : (member + 1) * HDIM]
            top = jnp.dot(weights(slice(0, half), slice(0, half)), inputs[:half], preferred_element_type=F32)
            bottom = jnp.dot(weights(slice(half, length), slice(0, length)), inputs, preferred_element_type=F32)
            tops.append(top)
            bottoms.append(bottom)
        lane = lax.broadcasted_iota(jnp.int32, x_pair.shape, 1)
        direct = jnp.where(lane < HDIM, skip[2 * pair], skip[2 * pair + 1]) * x_pair.astype(F32)
        lanes = slice(place * 128, (place + 1) * 128)
        out[0:half, lanes] = jnp.concatenate(tops, axis=1) + direct[:half]
        out[half:length, lanes] = jnp.concatenate(bottoms, axis=1) + direct[half:]


def finish_kernel(local_a, local_b, gate, c_mat, cum, mine, theirs, embedded, out_gain, out_weight, out, state):
    row = lax.axis_index("rows")
    half = E // 2
    state[:, pl.ds(pl.multiple_of(row * half, 128), half)] = mine[...]
    state[:, pl.ds(pl.multiple_of((1 - row) * half, 128), half)] = theirs[...]
    carried = jnp.dot(c_mat[...], state[...], preferred_element_type=F32)
    carried = carried * spread(jnp.exp(cum[...]), spread_matrix())
    local = jnp.concatenate([local_a[...], local_b[...]], axis=1)
    gated = (local + carried) * gate[...]
    mean_sq = jnp.mean(gated * gated, axis=-1, keepdims=True)
    hidden = (gated * lax.rsqrt(mean_sq + 1e-05) * out_gain[...]).astype(BF16)
    result = jnp.dot(hidden, out_weight[...], preferred_element_type=F32)
    out[...] = (result + embedded[...].astype(F32)[LEAD:]).astype(BF16)


def swap(block, axis, bit):
    return lax.ppermute(block, axis, [(i, i ^ bit) for i in range(lax.axis_size(axis))])


def sending_order(count):
    return (1, *range(count // 2, count), *range(2, count // 2))


def embed_by_rows(pixels, patch_weight, patch_bias):
    col_count = lax.axis_size("cols")
    width = pixels.shape[2]
    partner = swap(pixels, "rows", 1)
    pixels = call(stage_kernel, (pixels,), shape(pixels.shape))
    block = shape((WIN + 8, width))
    scratch = [pltpu.VMEM((CHAN, 2 * pixels.shape[1] + 64, width), BF16)]
    blocks = call(pack_kernel, (pixels, partner), [block] * col_count, scratch, limit=8)
    came = [blocks[0]] + [None] * (col_count - 1)
    for step in sending_order(col_count):
        came[step] = swap(blocks[step], "cols", step)
    weight = patch_weight.transpose(1, 2, 0, 3).reshape(KERNEL, WIN, D)
    weight = jnp.pad(weight, ((0, 0), (0, 128 - WIN), (0, 0))).reshape(KERNEL * 128, D)
    tokens = col_count * width // PATCH
    scratch = [
        pltpu.VMEM((2 * LEAD + col_count * width, 128), F32),
        pltpu.VMEM((144, 128), F32),
        pltpu.VMEM((LEAD + tokens, KERNEL * 128), BF16),
    ]
    flops = 2 * tokens * KERNEL * 128 * D
    return call(
        embed_kernel, (*came, weight, patch_bias.reshape(1, -1)), shape((LEAD + tokens, D)), scratch,
        flops=flops, moved=6 << 20, limit=16,
    )


def extended(block, sides, width):
    for axis, dim in sides:
        count = lax.axis_size(axis)
        forward = [(i, i + 1) for i in range(count - 1)]
        backward = [(target, source) for source, target in forward]
        low = lax.ppermute(
            lax.slice_in_dim(block, block.shape[dim] - width, None, axis=dim), axis, forward
        )
        high = lax.ppermute(lax.slice_in_dim(block, 0, width, axis=dim), axis, backward)
        block = jnp.concatenate([low, block, high], axis=dim)
    return block


def shifted(block, axis, distance):
    devices = range(lax.axis_size(axis))
    route = [(i - distance, i) for i in devices if i - distance in devices]
    return lax.ppermute(block, axis, route)


def embed_by_blocks(pixels, patch_weight, patch_bias):
    padded = extended(pixels, (("cols", 2), ("rows", 1)), MARGIN)
    embed_grid = lax.conv_general_dilated(
        padded[None],
        patch_weight,
        (PATCH, PATCH),
        "VALID",
        dimension_numbers=("NCHW", "HWIO", "NHWC"),
        preferred_element_type=jnp.float32,
    )[0]
    embed_grid = (embed_grid + patch_bias).astype(jnp.bfloat16)
    row_local, col_local, feature_width = embed_grid.shape
    devices = lax.axis_size(("cols", "rows"))
    row_count = lax.axis_size("rows")
    col_count = lax.axis_size("cols")
    groups = col_count // row_local
    piece_len = col_local * feature_width // devices
    outgoing = embed_grid.reshape(row_local, devices, piece_len)
    spread = lax.all_to_all(outgoing, ("cols", "rows"), split_axis=1, concat_axis=1, tiled=True)
    spread = spread.reshape(row_local, groups, row_local, row_count, piece_len).transpose(
        3, 0, 1, 2, 4
    )
    landed = lax.all_to_all(
        spread.reshape(devices, row_local, piece_len),
        ("cols", "rows"),
        split_axis=0,
        concat_axis=0,
        tiled=True,
    )
    tokens = landed.transpose(1, 0, 2).reshape(row_local * col_local, feature_width)
    tail = shifted(tokens[tokens.shape[0] - LEAD :], ("cols", "rows"), 1)
    return jnp.concatenate([tail, tokens], axis=0)


def body(
    pixels,
    patch_weight,
    patch_bias,
    norm_gain,
    gate_weight,
    mix_weight,
    step_weight,
    step_bias,
    log_rate,
    conv_weight,
    conv_bias,
    skip_gain,
    out_gain,
    out_weight,
):
    col_count = lax.axis_size("cols")
    row_local = pixels.shape[1] // PATCH
    if col_count == row_local:
        embedded = embed_by_rows(pixels, patch_weight, patch_bias)
    else:
        embedded = embed_by_blocks(pixels, patch_weight, patch_bias)
    length = embedded.shape[0] - LEAD
    line = lambda a: a.reshape(1, -1)
    mixed_width = mix_weight.shape[1]
    half = E // 2
    packed = NSTATE + 8
    normed, x, b_mat, c_mat, step, cum, keep, send = call(
        mix_kernel,
        (
            embedded, line(norm_gain), mix_weight, step_weight.T, line(step_bias), line(log_rate),
            conv_weight, line(conv_bias),
        ),
        [
            shape((length, D)), shape((length, E)), shape((length, NSTATE)), shape((length, NSTATE)),
            shape((length, HEADS), F32), shape((length, HEADS), F32), shape((packed, half), F32),
            shape((packed, half)),
        ],
        [pltpu.VMEM((LEAD + length, mixed_width), F32), pltpu.VMEM((packed, E), F32)],
        flops=2 * length * D * mixed_width, moved=4 << 20, limit=16,
    )
    came = swap(send, "rows", 1)
    summary, message = shape((packed, half), F32), shape((packed, half))
    total, out = call(pair_kernel, (keep, came), [summary, message])
    gate = call(
        gate_kernel, (normed, gate_weight), shape((length, E), F32),
        flops=2 * length * D * E, moved=4 << 20, limit=8,
    )
    locals_ = []
    for part in range(2):
        locals_.append(
            call(
                partial(intra_kernel, part * HEADS // 4), (skip_gain, x, b_mat, c_mat, step, cum),
                shape((length, half), F32), scalars=1,
                flops=HEADS * length * length * 128, moved=2 << 20, limit=8,
            )
        )
    before, bit = None, 1
    while 2 * bit < col_count:
        arrived = swap(out, "cols", bit)
        if before is None:
            kernel = lambda t, r, *outs, bit=bit: join_kernel(bit, t, None, r, *outs)
            total, before, out = call(kernel, (total, arrived), [summary, summary, message])
        else:
            total, before, out = call(partial(join_kernel, bit), (total, before, arrived), [summary, summary, message])
        bit *= 2
    arrived = swap(out, "cols", bit)
    entering = shape((NSTATE, half))
    mine, theirs = call(partial(enter_kernel, bit), (before, arrived, keep, came), [entering, entering])
    theirs = swap(theirs, "rows", 1)
    return call(
        finish_kernel,
        (*locals_, gate, c_mat, cum, mine, theirs, embedded, line(out_gain), out_weight),
        shape((length, D)),
        [pltpu.VMEM((NSTATE, E), BF16)],
        flops=2 * length * D * E, moved=4 << 20, limit=16,
    )


def solution(mesh):
    placed = (
        P(None, "rows", ("slides", "cols")),
        P(),
        P(),
        P(),
        P(),
        P(),
        P(),
        P(),
        P(),
        P(),
        P(),
        P(),
        P(),
        P(),
    )
    return jax.shard_map(
        body,
        mesh=mesh,
        in_specs=placed,
        out_specs=P(("slides", "cols", "rows"), None),
        check_vma=False,
    )
```

```python
from functools import partial

import jax
import jax.numpy as jnp
from jax import lax
from jax.experimental import pallas as pl
from jax.experimental.pallas import tpu as pltpu
from jax.sharding import PartitionSpec as P


E = 1536
D = 768
HDIM = 64
NSTATE = 64
PATCH = 16
KERNEL = 24
HEADS = 24
CHAN = 3
MARGIN = (KERNEL - PATCH) // 2
WIN = CHAN * KERNEL
LEAD = 8
F32 = jnp.float32
BF16 = jnp.bfloat16


def vmem():
    return pl.BlockSpec(memory_space=pltpu.VMEM)


def call(kernel, inputs, outs, scratch=(), limit=4, flops=0, moved=0, scalars=0):
    return pl.pallas_call(
        kernel,
        out_shape=outs,
        in_specs=[pl.BlockSpec(memory_space=pltpu.SMEM)] * scalars + [vmem()] * (len(inputs) - scalars),
        out_specs=jax.tree.map(lambda _: vmem(), outs),
        scratch_shapes=scratch,
        compiler_params=pltpu.CompilerParams(vmem_limit_bytes=limit << 20),
        cost_estimate=pl.CostEstimate(flops=flops, bytes_accessed=moved, transcendentals=0),
    )(*inputs)


def shape(dims, kind=BF16):
    return jax.ShapeDtypeStruct(dims, kind)


def pack_kernel(own, partner, *refs):
    outs, rows = refs[:-1], refs[-1]
    col, row = lax.axis_index("cols"), lax.axis_index("rows")
    local = own.shape[1]
    width = own.shape[2]
    edge = jnp.zeros((CHAN, 32, width), BF16)
    rows[:, 0:32, :] = edge
    rows[:, 32 + 2 * local : 64 + 2 * local, :] = edge
    rows[:, pl.ds(pl.multiple_of(32 + local * row, 32), local), :] = own[...]
    rows[:, pl.ds(pl.multiple_of(32 + local * (1 - row), 32), local), :] = partner[...]
    for step, out in enumerate(outs):
        token_row = 2 * (col ^ step) + row
        first = pl.multiple_of(PATCH * token_row, PATCH)
        pieces, tails = [], []
        for channel in range(CHAN):
            block = rows[channel, pl.ds(first, 64), :].astype(F32)
            pieces.append(block[28:52])
            before = block[12:28, width - 64 :]
            tails += [before[:8], before[8:]]
        tails.append(jnp.zeros((8, width - 64 * len(tails)), F32))
        pieces.append(jnp.concatenate(tails, axis=1))
        out[...] = jnp.concatenate(pieces, axis=0).astype(BF16)


def stage_kernel(pixels, out):
    out[...] = pixels[...]


def pick_matrix():
    row = lax.broadcasted_iota(jnp.int32, (256, 256), 0)
    pixel = lax.broadcasted_iota(jnp.int32, (256, 256), 1)
    return (pixel == (row & 15) * PATCH + (row >> 4)).astype(BF16)


def turned(pick, values):
    return lax.dot_general(pick, values, (((1,), (1,)), ((), ())), preferred_element_type=F32)


def embed_kernel(*refs):
    blocks, (weight, bias, out, picked, tail, wide) = refs[:-6], refs[-6:]
    col = lax.axis_index("cols")
    width = blocks[0].shape[1]
    count = len(blocks)
    tokens = count * width // PATCH
    local = width // PATCH
    zeros = jnp.zeros((PATCH, LEAD, 128), F32)
    picked[:, 0:LEAD, :] = zeros
    picked[:, LEAD + tokens :, :] = zeros
    blank = jnp.zeros((128 - WIN, width), BF16)
    pick = pick_matrix()
    for step, block in enumerate(blocks):
        source = col ^ step
        values = jnp.concatenate([block[0:WIN, :], blank], axis=0)
        for group in range(width // 256):
            found = turned(pick, values[:, 256 * group : 256 * (group + 1)])
            first = pl.multiple_of(LEAD + source * local + 16 * group, 8)
            picked[:, pl.ds(first, 16), :] = found.reshape(PATCH, 16, 128)

        @pl.when(source == count - 1)
        def _():
            whole = block[...].astype(F32)
            extra = whole[WIN : WIN + 8]
            pieces = []
            for channel in range(CHAN):
                pieces += [extra[:, 128 * channel : 128 * channel + 64]]
                pieces += [extra[:, 128 * channel + 64 : 128 * channel + 128]]
                pieces += [whole[KERNEL * channel : KERNEL * channel + 8, width - 64 :]]
            pieces.append(jnp.zeros((128 - WIN, 64), F32))
            last = jnp.concatenate(pieces, axis=0)
            last = jnp.concatenate([jnp.zeros((128, 64), F32), last, jnp.zeros((128, 128), F32)], axis=1)
            found = turned(pick, last.astype(BF16)).reshape(PATCH, 16, 128)
            tail[:, 0:8, :] = zeros
            tail[:, 8:24, :] = found

    for offset in range(KERNEL):
        place = offset - MARGIN + PATCH
        shift, pixel = place // PATCH - 1, place % PATCH
        ahead = tail[pixel, 8 + shift : 16 + shift, :]
        part = jnp.concatenate([ahead, picked[pixel, LEAD + shift : LEAD + shift + tokens, :]], axis=0)
        wide[:, offset * 128 : (offset + 1) * 128] = part.astype(BF16)
    grid = jnp.dot(wide[...], weight[...], preferred_element_type=F32)
    out[...] = (grid + bias[...]).astype(BF16)


def spread_matrix():
    head = lax.broadcasted_iota(jnp.int32, (HEADS, E), 0)
    lane = lax.broadcasted_iota(jnp.int32, (HEADS, E), 1)
    return ((lane >= head * HDIM) & (lane < (head + 1) * HDIM)).astype(BF16)


def halves(values):
    high = values.astype(BF16)
    return high, (values - high.astype(F32)).astype(BF16)


def spread(values, matrix):
    high, low = halves(values)
    return jnp.dot(high, matrix, preferred_element_type=F32) + jnp.dot(low, matrix, preferred_element_type=F32)


def silu(values):
    half = 0.5 * values
    return half + half * jnp.tanh(half)


def softplus(values):
    small = jnp.exp(-jnp.abs(values))
    return jnp.maximum(values, 0.0) + jnp.log1p(small)


def mix_kernel(
    embedded, norm_gain, mix_weight, step_weight, step_bias, log_rate, conv_weight, conv_bias,
    normed_out, x_out, b_out, c_out, step_out, cum_out, keep_out, send_out, raw, state,
):
    col, row = lax.axis_index("cols"), lax.axis_index("rows")
    resid = embedded[...].astype(F32)
    mean_sq = jnp.mean(resid * resid, axis=-1, keepdims=True)
    normed_f = resid * lax.rsqrt(mean_sq + 1e-05) * norm_gain[...]
    normed = normed_f.astype(BF16)
    normed_out[...] = normed_f[LEAD:].astype(BF16)
    length = embedded.shape[0] - LEAD
    raw[...] = jnp.dot(normed, mix_weight[...], preferred_element_type=F32).astype(BF16).astype(F32)

    @pl.when((col == 0) & (row == 0))
    def _():
        raw[0:LEAD, :] = jnp.zeros((LEAD, raw.shape[1]), F32)

    step_raw = lax.dot_general(
        normed, step_weight[...], (((1,), (1,)), ((), ())), preferred_element_type=F32
    )[LEAD:]
    step = softplus(step_raw + step_bias[...])
    log_decay = -step * jnp.exp(log_rate[...])
    lower = (
        lax.broadcasted_iota(jnp.int32, (length, length), 0) >= lax.broadcasted_iota(jnp.int32, (length, length), 1)
    ).astype(BF16)
    high = log_decay.astype(BF16)
    middle = (log_decay - high.astype(F32)).astype(BF16)
    cum = jnp.dot(lower, high, preferred_element_type=F32)
    cum = cum + jnp.dot(lower, middle, preferred_element_type=F32)
    low = (log_decay - high.astype(F32) - middle.astype(F32)).astype(BF16)
    cum = cum + jnp.dot(lower, low, preferred_element_type=F32)
    step_out[...] = step
    cum_out[...] = cum
    matrix = spread_matrix()
    last = cum[length - 1 :]
    to_end = spread(jnp.exp(last - cum) * step, matrix)
    decay = spread(jnp.broadcast_to(jnp.exp(last), (8, HEADS)), matrix)
    taps = conv_weight.shape[0]
    chunk = 64
    scaled = []
    maps = []
    for first in range(0, length, chunk):
        total = jnp.broadcast_to(conv_bias[...], (chunk, raw.shape[1]))
        for tap in range(taps):
            total = total + conv_weight[tap : tap + 1, :] * raw[pl.ds(LEAD - taps + 1 + tap + first, chunk), :]
        mixed = silu(total).astype(BF16)
        x_out[pl.ds(first, chunk), :] = mixed[:, :E]
        mixed_f = mixed[:, E:].astype(F32)
        b_out[pl.ds(first, chunk), :] = mixed_f[:, :NSTATE].astype(BF16)
        c_out[pl.ds(first, chunk), :] = mixed_f[:, NSTATE:].astype(BF16)
        maps.append(mixed_f[:, :NSTATE])
        scaled.append((mixed[:, :E].astype(F32) * to_end[first : first + chunk]).astype(BF16))
    b_t = jnp.concatenate(maps, axis=0).T.astype(BF16)
    state[0:NSTATE, :] = jnp.dot(b_t, jnp.concatenate(scaled, axis=0), preferred_element_type=F32)
    state[NSTATE : NSTATE + 8, :] = decay
    half = E // 2
    mine = pl.ds(pl.multiple_of(row * half, 128), half)
    theirs = pl.ds(pl.multiple_of((1 - row) * half, 128), half)
    keep_out[...] = state[:, mine]
    send_out[...] = wire(state[0:NSTATE, theirs], state[NSTATE : NSTATE + 8, theirs])


def wire(values, decay):
    high = decay.astype(BF16).astype(F32)
    rest = decay - high
    place = lax.broadcasted_iota(jnp.int32, decay.shape, 0)
    return jnp.concatenate([values, jnp.where(place == 0, high, rest)], axis=0).astype(BF16)


def unwire(message):
    values = message[0:NSTATE, :].astype(F32)
    rows = message[NSTATE : NSTATE + 8, :].astype(F32)
    return values, jnp.broadcast_to(rows[0:1] + rows[1:2], rows.shape)


def scale(decay, values):
    return decay[0:1] * values


def pair_kernel(keep, received, total_out, message_out):
    row = lax.axis_index("rows")
    own, own_decay = keep[0:NSTATE, :], keep[NSTATE : NSTATE + 8, :]
    other, other_decay = unwire(received)
    upper = row == 1
    last_decay = jnp.where(upper, own_decay, other_decay)
    values = scale(last_decay, jnp.where(upper, other, own)) + jnp.where(upper, own, other)
    decay = own_decay * other_decay
    total_out[0:NSTATE, :] = values
    total_out[NSTATE : NSTATE + 8, :] = decay
    message_out[...] = wire(values, decay)


def join_kernel(bit, first, final, *refs):
    refs = list(refs)
    total = refs.pop(0)
    before = None if first else refs.pop(0)
    received = refs.pop(0)
    col = lax.axis_index("cols")
    later = (col & bit) != 0
    values, decay = total[0:NSTATE, :], total[NSTATE : NSTATE + 8, :]
    came, came_decay = unwire(received)
    last_decay = jnp.where(later, decay, came_decay)
    joined = scale(last_decay, jnp.where(later, came, values)) + jnp.where(later, values, came)
    before_out, message_out = refs[:2]
    if not final:
        refs[2][0:NSTATE, :] = joined
        refs[2][NSTATE : NSTATE + 8, :] = decay * came_decay
    message_out[...] = wire(joined, decay * came_decay)
    if first:
        before_out[0:NSTATE, :] = jnp.where(later, came, 0.0)
        before_out[NSTATE : NSTATE + 8, :] = jnp.where(later, came_decay, 1.0)
    else:
        ahead, ahead_decay = before[0:NSTATE, :], before[NSTATE : NSTATE + 8, :]
        before_out[0:NSTATE, :] = jnp.where(later, scale(ahead_decay, came) + ahead, ahead)
        before_out[NSTATE : NSTATE + 8, :] = jnp.where(later, ahead_decay * came_decay, ahead_decay)


def enter_kernel(bit, before, last, keep, received, mine_out, theirs_out):
    col, row = lax.axis_index("cols"), lax.axis_index("rows")
    later = (col & bit) != 0
    ahead, ahead_decay = before[0:NSTATE, :], before[NSTATE : NSTATE + 8, :]
    came, _ = unwire(last)
    ahead = jnp.where(later, scale(ahead_decay, came) + ahead, ahead)
    other, other_decay = unwire(received)
    upper = row == 1
    low = jnp.where(upper, other, keep[0:NSTATE, :])
    low_decay = jnp.where(upper, other_decay, keep[NSTATE : NSTATE + 8, :])
    second = scale(low_decay, ahead) + low
    mine_out[...] = jnp.where(upper, second, ahead).astype(BF16)
    theirs_out[...] = jnp.where(upper, ahead, second).astype(BF16)


def gate_kernel(normed, gate_weight, local_a, local_b, cum, own_out, factor_out):
    gate = jnp.dot(normed[...], gate_weight[...], preferred_element_type=F32).astype(BF16).astype(F32)
    gate = silu(gate)
    half = local_a.shape[1]
    own_out[:, :half] = local_a[...] * gate[:, :half]
    own_out[:, half:] = local_b[...] * gate[:, half:]
    factor_out[...] = spread(jnp.exp(cum[...]), spread_matrix()) * gate


def intra_kernel(first, skip, x, b_mat, c_mat, step, cum, out):
    length = x.shape[0]
    half = length // 2
    scores = lax.dot_general(c_mat[...], b_mat[...], (((1,), (1,)), ((), ())), preferred_element_type=F32)
    causal = lax.broadcasted_iota(jnp.int32, (length, length), 0) >= lax.broadcasted_iota(
        jnp.int32, (length, length), 1
    )
    scores = jnp.where(causal, scores, 0.0)
    wide = jnp.zeros((length, 128 - HEADS), F32)
    cum_v = cum[...]
    cum_t = jnp.concatenate([cum_v, wide], axis=1).T
    step_t = jnp.concatenate([step[...], wide], axis=1).T
    for place in range(out.shape[1] // 128):
        pair = first + place
        x_pair = x[:, pair * 128 : (pair + 1) * 128]
        tops, bottoms = [], []
        for member in range(2):
            head = 2 * pair + member
            column = cum_v[:, head : head + 1]
            cum_row = cum_t[head : head + 1, :]
            step_row = step_t[head : head + 1, :]

            def weights(rows, span):
                gap = jnp.minimum(column[rows] - cum_row[:, span], 0.0)
                return (scores[rows, span] * jnp.exp(gap) * step_row[:, span]).astype(BF16)

            inputs = x_pair[:, member * HDIM : (member + 1) * HDIM]
            top = jnp.dot(weights(slice(0, half), slice(0, half)), inputs[:half], preferred_element_type=F32)
            bottom = jnp.dot(weights(slice(half, length), slice(0, length)), inputs, preferred_element_type=F32)
            tops.append(top)
            bottoms.append(bottom)
        lane = lax.broadcasted_iota(jnp.int32, x_pair.shape, 1)
        direct = jnp.where(lane < HDIM, skip[2 * pair], skip[2 * pair + 1]) * x_pair.astype(F32)
        lanes = slice(place * 128, (place + 1) * 128)
        out[0:half, lanes] = jnp.concatenate(tops, axis=1) + direct[:half]
        out[half:length, lanes] = jnp.concatenate(bottoms, axis=1) + direct[half:]


def half_product(which, state, own, factor, c_mat, out_gain, out_weight):
    half = own.shape[1] // 2
    lanes = pl.ds(pl.multiple_of(which * half, 128), half)
    carried = jnp.dot(c_mat[...], state[...], preferred_element_type=F32)
    gated = own[:, lanes] + carried * factor[:, lanes]
    squares = jnp.sum(gated * gated, axis=-1, keepdims=True)
    hidden = (gated * out_gain[:, lanes]).astype(BF16)
    return jnp.dot(hidden, out_weight[lanes, :], preferred_element_type=F32), squares


def first_kernel(mine, own, factor, c_mat, out_gain, out_weight, product_out, squares_out):
    product, squares = half_product(
        lax.axis_index("rows"), mine, own, factor, c_mat, out_gain, out_weight
    )
    product_out[...] = product
    squares_out[...] = jnp.broadcast_to(squares, squares_out.shape)


def finish_kernel(theirs, own, factor, c_mat, out_gain, out_weight, product, squares, embedded, out):
    rest, more = half_product(
        1 - lax.axis_index("rows"), theirs, own, factor, c_mat, out_gain, out_weight
    )
    mean_sq = (squares[:, 0:1] + more) / own.shape[1]
    result = (product[...] + rest) * lax.rsqrt(mean_sq + 1e-05)
    out[...] = (result + embedded[...].astype(F32)[LEAD:]).astype(BF16)


def swap(block, axis, bit):
    return lax.ppermute(block, axis, [(i, i ^ bit) for i in range(lax.axis_size(axis))])


def sending_order(count):
    return (1, *range(count // 2, count), *range(2, count // 2))


def embed_by_rows(pixels, patch_weight, patch_bias):
    col_count = lax.axis_size("cols")
    width = pixels.shape[2]
    partner = swap(pixels, "rows", 1)
    pixels = call(stage_kernel, (pixels,), shape(pixels.shape))
    block = shape((WIN + 8, width))
    scratch = [pltpu.VMEM((CHAN, 2 * pixels.shape[1] + 64, width), BF16)]
    blocks = call(pack_kernel, (pixels, partner), [block] * col_count, scratch, limit=8)
    came = [blocks[0]] + [None] * (col_count - 1)
    for step in sending_order(col_count):
        came[step] = swap(blocks[step], "cols", step)
    weight = patch_weight.transpose(1, 2, 0, 3).reshape(KERNEL, WIN, D)
    weight = jnp.pad(weight, ((0, 0), (0, 128 - WIN), (0, 0))).reshape(KERNEL * 128, D)
    tokens = col_count * width // PATCH
    scratch = [
        pltpu.VMEM((PATCH, 2 * LEAD + tokens, 128), F32),
        pltpu.VMEM((PATCH, 24, 128), F32),
        pltpu.VMEM((LEAD + tokens, KERNEL * 128), BF16),
    ]
    flops = 2 * tokens * KERNEL * 128 * D
    return call(
        embed_kernel, (*came, weight, patch_bias.reshape(1, -1)), shape((LEAD + tokens, D)), scratch,
        flops=flops, moved=6 << 20, limit=16,
    )


def extended(block, sides, width):
    for axis, dim in sides:
        count = lax.axis_size(axis)
        forward = [(i, i + 1) for i in range(count - 1)]
        backward = [(target, source) for source, target in forward]
        low = lax.ppermute(
            lax.slice_in_dim(block, block.shape[dim] - width, None, axis=dim), axis, forward
        )
        high = lax.ppermute(lax.slice_in_dim(block, 0, width, axis=dim), axis, backward)
        block = jnp.concatenate([low, block, high], axis=dim)
    return block


def shifted(block, axis, distance):
    devices = range(lax.axis_size(axis))
    route = [(i - distance, i) for i in devices if i - distance in devices]
    return lax.ppermute(block, axis, route)


def embed_by_blocks(pixels, patch_weight, patch_bias):
    padded = extended(pixels, (("cols", 2), ("rows", 1)), MARGIN)
    embed_grid = lax.conv_general_dilated(
        padded[None],
        patch_weight,
        (PATCH, PATCH),
        "VALID",
        dimension_numbers=("NCHW", "HWIO", "NHWC"),
        preferred_element_type=jnp.float32,
    )[0]
    embed_grid = (embed_grid + patch_bias).astype(jnp.bfloat16)
    row_local, col_local, feature_width = embed_grid.shape
    devices = lax.axis_size(("cols", "rows"))
    row_count = lax.axis_size("rows")
    col_count = lax.axis_size("cols")
    groups = col_count // row_local
    piece_len = col_local * feature_width // devices
    outgoing = embed_grid.reshape(row_local, devices, piece_len)
    spread = lax.all_to_all(outgoing, ("cols", "rows"), split_axis=1, concat_axis=1, tiled=True)
    spread = spread.reshape(row_local, groups, row_local, row_count, piece_len).transpose(
        3, 0, 1, 2, 4
    )
    landed = lax.all_to_all(
        spread.reshape(devices, row_local, piece_len),
        ("cols", "rows"),
        split_axis=0,
        concat_axis=0,
        tiled=True,
    )
    tokens = landed.transpose(1, 0, 2).reshape(row_local * col_local, feature_width)
    tail = shifted(tokens[tokens.shape[0] - LEAD :], ("cols", "rows"), 1)
    return jnp.concatenate([tail, tokens], axis=0)


def body(
    pixels,
    patch_weight,
    patch_bias,
    norm_gain,
    gate_weight,
    mix_weight,
    step_weight,
    step_bias,
    log_rate,
    conv_weight,
    conv_bias,
    skip_gain,
    out_gain,
    out_weight,
):
    col_count = lax.axis_size("cols")
    row_local = pixels.shape[1] // PATCH
    if col_count == row_local:
        embedded = embed_by_rows(pixels, patch_weight, patch_bias)
    else:
        embedded = embed_by_blocks(pixels, patch_weight, patch_bias)
    length = embedded.shape[0] - LEAD
    line = lambda a: a.reshape(1, -1)
    mixed_width = mix_weight.shape[1]
    half = E // 2
    packed = NSTATE + 8
    normed, x, b_mat, c_mat, step, cum, keep, send = call(
        mix_kernel,
        (
            embedded, line(norm_gain), mix_weight, step_weight.T, line(step_bias), line(log_rate),
            conv_weight, line(conv_bias),
        ),
        [
            shape((length, D)), shape((length, E)), shape((length, NSTATE)), shape((length, NSTATE)),
            shape((length, HEADS), F32), shape((length, HEADS), F32), shape((packed, half), F32),
            shape((packed, half)),
        ],
        [pltpu.VMEM((LEAD + length, mixed_width), F32), pltpu.VMEM((packed, E), F32)],
        flops=2 * length * D * mixed_width, moved=4 << 20, limit=16,
    )
    came = swap(send, "rows", 1)
    summary, message = shape((packed, half), F32), shape((packed, half))
    total, out = call(pair_kernel, (keep, came), [summary, message])
    locals_ = []
    for part in range(2):
        locals_.append(
            call(
                partial(intra_kernel, part * HEADS // 4), (skip_gain, x, b_mat, c_mat, step, cum),
                shape((length, half), F32), scalars=1,
                flops=HEADS * length * length * 128, moved=2 << 20, limit=8,
            )
        )
    own, factor = call(
        gate_kernel, (normed, gate_weight, *locals_, cum), [shape((length, E), F32)] * 2,
        flops=2 * length * D * E, moved=4 << 20, limit=8,
    )
    before, bit = None, 1
    while 2 * bit < col_count:
        arrived = swap(out, "cols", bit)
        first, final = before is None, 4 * bit >= col_count
        inputs = (total, arrived) if first else (total, before, arrived)
        before, out, *total = call(
            partial(join_kernel, bit, first, final), inputs, [summary, message] + [summary] * (not final)
        )
        total = total[0] if total else None
        bit *= 2
    arrived = swap(out, "cols", bit)
    entering = shape((NSTATE, half))
    mine, theirs = call(partial(enter_kernel, bit), (before, arrived, keep, came), [entering, entering])
    theirs = swap(theirs, "rows", 1)
    common = (own, factor, c_mat, line(out_gain), out_weight)
    product, squares = call(
        first_kernel, (mine, *common), [shape((length, D), F32), shape((length, 128), F32)],
        flops=length * D * E, moved=4 << 20, limit=8,
    )
    return call(
        finish_kernel, (theirs, *common, product, squares, embedded), shape((length, D)),
        flops=length * D * E, moved=4 << 20, limit=8,
    )


def solution(mesh):
    placed = (
        P(None, "rows", ("slides", "cols")),
        P(),
        P(),
        P(),
        P(),
        P(),
        P(),
        P(),
        P(),
        P(),
        P(),
        P(),
        P(),
        P(),
    )
    return jax.shard_map(
        body,
        mesh=mesh,
        in_specs=placed,
        out_specs=P(("slides", "cols", "rows"), None),
        check_vma=False,
    )
```

```python
from functools import partial

import jax
import jax.numpy as jnp
from jax import lax
from jax.experimental import pallas as pl
from jax.experimental.pallas import tpu as pltpu
from jax.sharding import PartitionSpec as P


E = 1536
D = 768
HDIM = 64
NSTATE = 64
PATCH = 16
KERNEL = 24
HEADS = 24
CHAN = 3
MARGIN = (KERNEL - PATCH) // 2
WIN = CHAN * KERNEL
LEAD = 8
F32 = jnp.float32
BF16 = jnp.bfloat16


def vmem():
    return pl.BlockSpec(memory_space=pltpu.VMEM)


def call(kernel, inputs, outs, scratch=(), limit=4, flops=0, moved=0, scalars=0):
    return pl.pallas_call(
        kernel,
        out_shape=outs,
        in_specs=[pl.BlockSpec(memory_space=pltpu.SMEM)] * scalars + [vmem()] * (len(inputs) - scalars),
        out_specs=jax.tree.map(lambda _: vmem(), outs),
        scratch_shapes=scratch,
        compiler_params=pltpu.CompilerParams(vmem_limit_bytes=limit << 20),
        cost_estimate=pl.CostEstimate(flops=flops, bytes_accessed=moved, transcendentals=0),
    )(*inputs)


def shape(dims, kind=BF16):
    return jax.ShapeDtypeStruct(dims, kind)


def pack_kernel(own, partner, *refs):
    outs, rows = refs[:-1], refs[-1]
    col, row = lax.axis_index("cols"), lax.axis_index("rows")
    local = own.shape[1]
    width = own.shape[2]
    edge = jnp.zeros((CHAN, 32, width), BF16)
    rows[:, 0:32, :] = edge
    rows[:, 32 + 2 * local : 64 + 2 * local, :] = edge
    rows[:, pl.ds(pl.multiple_of(32 + local * row, 32), local), :] = own[...]
    rows[:, pl.ds(pl.multiple_of(32 + local * (1 - row), 32), local), :] = partner[...]
    for step, out in enumerate(outs):
        token_row = 2 * (col ^ step) + row
        first = pl.multiple_of(PATCH * token_row, PATCH)
        pieces, tails = [], []
        for channel in range(CHAN):
            block = rows[channel, pl.ds(first, 64), :].astype(F32)
            pieces.append(block[28:52])
            before = block[12:28, width - 64 :]
            tails += [before[:8], before[8:]]
        tails.append(jnp.zeros((8, width - 64 * len(tails)), F32))
        pieces.append(jnp.concatenate(tails, axis=1))
        out[...] = jnp.concatenate(pieces, axis=0).astype(BF16)


def stage_kernel(pixels, out):
    out[...] = pixels[...]


def pick_matrix():
    row = lax.broadcasted_iota(jnp.int32, (256, 256), 0)
    pixel = lax.broadcasted_iota(jnp.int32, (256, 256), 1)
    return (pixel == (row & 15) * PATCH + (row >> 4)).astype(BF16)


def turned(pick, values):
    return lax.dot_general(pick, values, (((1,), (1,)), ((), ())), preferred_element_type=F32)


def embed_kernel(*refs):
    blocks, (weight, bias, out, picked, tail, wide) = refs[:-6], refs[-6:]
    col = lax.axis_index("cols")
    width = blocks[0].shape[1]
    count = len(blocks)
    tokens = count * width // PATCH
    local = width // PATCH
    zeros = jnp.zeros((PATCH, LEAD, 128), F32)
    picked[:, 0:LEAD, :] = zeros
    picked[:, LEAD + tokens :, :] = zeros
    blank = jnp.zeros((128 - WIN, width), BF16)
    pick = pick_matrix()
    edge = jnp.zeros((WIN + 8, 128), F32)
    extra = jnp.zeros((8, 128 * CHAN), F32)
    for step, block in enumerate(blocks):
        source = col ^ step
        values = jnp.concatenate([block[0:WIN, :], blank], axis=0)
        for group in range(width // 256):
            found = turned(pick, values[:, 256 * group : 256 * (group + 1)])
            first = pl.multiple_of(LEAD + source * local + 16 * group, 8)
            picked[:, pl.ds(first, 16), :] = found.reshape(PATCH, 16, 128)
        last = source == count - 1
        edge = jnp.where(last, block[:, width - 128 :].astype(F32), edge)
        extra = jnp.where(last, block[WIN - 8 : WIN + 8, : 128 * CHAN].astype(F32)[8:], extra)
    pieces = []
    for channel in range(CHAN):
        pieces += [extra[:, 128 * channel : 128 * channel + 64]]
        pieces += [extra[:, 128 * channel + 64 : 128 * channel + 128]]
        pieces += [edge[KERNEL * channel : KERNEL * channel + 8, 64:]]
    pieces.append(jnp.zeros((128 - WIN, 64), F32))
    last = jnp.concatenate(pieces, axis=0)
    last = jnp.concatenate([jnp.zeros((128, 64), F32), last, jnp.zeros((128, 128), F32)], axis=1)
    tail[:, 0:8, :] = zeros
    tail[:, 8:24, :] = turned(pick, last.astype(BF16)).reshape(PATCH, 16, 128)

    for offset in range(KERNEL):
        place = offset - MARGIN + PATCH
        shift, pixel = place // PATCH - 1, place % PATCH
        ahead = tail[pixel, 8 + shift : 16 + shift, :]
        part = jnp.concatenate([ahead, picked[pixel, LEAD + shift : LEAD + shift + tokens, :]], axis=0)
        wide[:, offset * 128 : (offset + 1) * 128] = part.astype(BF16)
    grid = jnp.dot(wide[...], weight[...], preferred_element_type=F32)
    out[...] = (grid + bias[...]).astype(BF16)


def spread_matrix():
    head = lax.broadcasted_iota(jnp.int32, (HEADS, E), 0)
    lane = lax.broadcasted_iota(jnp.int32, (HEADS, E), 1)
    return ((lane >= head * HDIM) & (lane < (head + 1) * HDIM)).astype(BF16)


def halves(values):
    high = values.astype(BF16)
    return high, (values - high.astype(F32)).astype(BF16)


def spread(values, matrix):
    high, low = halves(values)
    return jnp.dot(high, matrix, preferred_element_type=F32) + jnp.dot(low, matrix, preferred_element_type=F32)


def silu(values):
    half = 0.5 * values
    return half + half * jnp.tanh(half)


def softplus(values):
    small = jnp.exp(-jnp.abs(values))
    return jnp.maximum(values, 0.0) + jnp.log1p(small)


def mix_kernel(
    embedded, norm_gain, mix_weight, step_weight, step_bias, log_rate, conv_weight, conv_bias,
    normed_out, x_out, b_out, c_out, step_out, cum_out, keep_out, send_out, state,
):
    col, row = lax.axis_index("cols"), lax.axis_index("rows")
    resid = embedded[...].astype(F32)
    mean_sq = jnp.mean(resid * resid, axis=-1, keepdims=True)
    normed_f = resid * lax.rsqrt(mean_sq + 1e-05) * norm_gain[...]
    rows = lax.broadcasted_iota(jnp.int32, normed_f.shape, 0)
    blank = (rows < LEAD) & (col == 0) & (row == 0)
    normed = jnp.where(blank, 0.0, normed_f).astype(BF16)
    normed_out[...] = normed_f[LEAD:].astype(BF16)
    length = embedded.shape[0] - LEAD
    step_raw = lax.dot_general(
        normed, step_weight[...], (((1,), (1,)), ((), ())), preferred_element_type=F32
    )[LEAD:]
    step = softplus(step_raw + step_bias[...])
    log_decay = -step * jnp.exp(log_rate[...])
    lower = (
        lax.broadcasted_iota(jnp.int32, (length, length), 0) >= lax.broadcasted_iota(jnp.int32, (length, length), 1)
    ).astype(BF16)
    high = log_decay.astype(BF16)
    middle = (log_decay - high.astype(F32)).astype(BF16)
    low = (log_decay - high.astype(F32) - middle.astype(F32)).astype(BF16)
    cum = jnp.dot(lower, high, preferred_element_type=F32)
    cum = cum + jnp.dot(lower, middle, preferred_element_type=F32)
    cum = cum + jnp.dot(lower, low, preferred_element_type=F32)
    step_out[...] = step
    cum_out[...] = cum
    matrix = spread_matrix()
    last = cum[length - 1 :]
    scales = (jnp.exp(last - cum) * step).astype(BF16)
    state[NSTATE : NSTATE + 8, :] = spread(jnp.broadcast_to(jnp.exp(last), (8, HEADS)), matrix)
    taps = conv_weight.shape[0]

    def project(lanes):
        return jnp.dot(normed, mix_weight[:, lanes], preferred_element_type=F32).astype(BF16)

    def mixed(raw, lanes):
        raw = raw.astype(F32)
        total = conv_weight[0:1, lanes] * raw
        for tap in range(1, taps):
            total = pltpu.roll(total, 1, 0) + conv_weight[tap : tap + 1, lanes] * raw
        return silu(total[LEAD:] + conv_bias[:, lanes]).astype(BF16)

    chunk = 512
    spans = [slice(E, E + 2 * NSTATE)] + [slice(first, first + chunk) for first in range(0, E, chunk)]
    ahead = project(spans[0])
    for place, lanes in enumerate(spans):
        raw = ahead
        if place + 1 < len(spans):
            ahead = project(spans[place + 1])
        part = mixed(raw, lanes)
        if place == 0:
            maps = part.astype(F32)
            b_out[...] = maps[:, :NSTATE].astype(BF16)
            c_out[...] = maps[:, NSTATE:].astype(BF16)
            b_t = maps.T[:NSTATE].astype(BF16)
            continue
        x_out[:, lanes] = part
        to_end = jnp.dot(scales, matrix[:, lanes], preferred_element_type=F32)
        scaled = (part.astype(F32) * to_end).astype(BF16)
        state[0:NSTATE, lanes] = jnp.dot(b_t, scaled, preferred_element_type=F32)
    half = E // 2
    mine = pl.ds(pl.multiple_of(row * half, 128), half)
    theirs = pl.ds(pl.multiple_of((1 - row) * half, 128), half)
    keep_out[...] = state[:, mine]
    send_out[...] = wire(state[0:NSTATE, theirs], state[NSTATE : NSTATE + 8, theirs])


def wire(values, decay):
    high = decay.astype(BF16).astype(F32)
    rest = decay - high
    place = lax.broadcasted_iota(jnp.int32, decay.shape, 0)
    return jnp.concatenate([values, jnp.where(place == 0, high, rest)], axis=0).astype(BF16)


def unwire(message):
    values = message[0:NSTATE, :].astype(F32)
    rows = message[NSTATE : NSTATE + 8, :].astype(F32)
    return values, jnp.broadcast_to(rows[0:1] + rows[1:2], rows.shape)


def product(factors):
    total = factors[0]
    for factor in factors[1:]:
        total = total * factor
    return total


def folded(place, pieces):
    places = [place ^ step for step in range(len(pieces))]
    steps = range(len(pieces))
    one = jnp.ones_like(pieces[0][1])
    all_values, ahead_values = None, None
    for step in steps:
        after = [jnp.where(places[k] > places[step], pieces[k][1], one) for k in steps if k != step]
        between = [
            jnp.where((places[k] > places[step]) & (places[k] < place), pieces[k][1], one)
            for k in steps
            if k not in (0, step)
        ]
        term = product(after)[0:1] * pieces[step][0]
        all_values = term if step == 0 else all_values + term
        if step:
            weight = jnp.where(places[step] < place, product([one, *between]), 0.0)
            term = weight[0:1] * pieces[step][0]
            ahead_values = term if ahead_values is None else ahead_values + term
    all_decay = product([decay for _, decay in pieces])
    ahead_decay = product([jnp.where(places[k] < place, pieces[k][1], one) for k in steps if k])
    return (all_values, all_decay), (ahead_values, ahead_decay)


def read(summary):
    return summary[0:NSTATE, :], summary[NSTATE : NSTATE + 8, :]


def write(summary, piece):
    summary[0:NSTATE, :] = piece[0]
    summary[NSTATE : NSTATE + 8, :] = piece[1]


def chained(earlier, latter):
    return latter[1][0:1] * earlier[0] + latter[0], earlier[1] * latter[1]


def pair_kernel(keep, received, total_out, message_out):
    total, _ = folded(lax.axis_index("rows"), [read(keep), unwire(received)])
    write(total_out, total)
    message_out[...] = wire(*total)


def join_kernel(low, count, first, *refs):
    refs = list(refs)
    total = read(refs.pop(0))
    before = None if first else read(refs.pop(0))
    pieces = [total] + [unwire(refs.pop(0)) for _ in range(count - 1)]
    place = (lax.axis_index("cols") // low) & (count - 1)
    total, ahead = folded(place, pieces)
    before_out, message_out = refs[:2]
    write(before_out, ahead if first else chained(ahead, before))
    message_out[...] = wire(*total)
    write(refs[2], total)


def enter_kernel(low, count, first, *refs):
    refs = list(refs)
    total = read(refs.pop(0))
    before = None if first else read(refs.pop(0))
    pieces = [total] + [unwire(refs.pop(0)) for _ in range(count - 1)]
    keep, received, mine_out, theirs_out = refs
    _, ahead = folded((lax.axis_index("cols") // low) & (count - 1), pieces)
    if not first:
        ahead = chained(ahead, before)
    own, other = read(keep), unwire(received)
    upper = lax.axis_index("rows") == 1
    low_piece = tuple(jnp.where(upper, b, a) for a, b in zip(own, other))
    second = chained(ahead, low_piece)[0]
    mine_out[...] = jnp.where(upper, second, ahead[0]).astype(BF16)
    theirs_out[...] = jnp.where(upper, ahead[0], second).astype(BF16)


def gate_kernel(normed, gate_weight, local_a, local_b, cum, own_out, factor_out):
    gate = jnp.dot(normed[...], gate_weight[...], preferred_element_type=F32).astype(BF16).astype(F32)
    gate = silu(gate)
    half = local_a.shape[1]
    own_out[:, :half] = local_a[...] * gate[:, :half]
    own_out[:, half:] = local_b[...] * gate[:, half:]
    factor_out[...] = spread(jnp.exp(cum[...]), spread_matrix()) * gate


def intra_kernel(first, skip, x, b_mat, c_mat, step, cum, out):
    length = x.shape[0]
    half = length // 2
    scores = lax.dot_general(c_mat[...], b_mat[...], (((1,), (1,)), ((), ())), preferred_element_type=F32)
    causal = lax.broadcasted_iota(jnp.int32, (length, length), 0) >= lax.broadcasted_iota(
        jnp.int32, (length, length), 1
    )
    scores = jnp.where(causal, scores, 0.0)
    wide = jnp.zeros((length, 128 - HEADS), F32)
    cum_v = cum[...]
    cum_t = jnp.concatenate([cum_v, wide], axis=1).T
    step_t = jnp.concatenate([step[...], wide], axis=1).T
    for place in range(out.shape[1] // 128):
        pair = first + place
        x_pair = x[:, pair * 128 : (pair + 1) * 128]
        tops, bottoms = [], []
        for member in range(2):
            head = 2 * pair + member
            column = cum_v[:, head : head + 1]
            cum_row = cum_t[head : head + 1, :]
            step_row = step_t[head : head + 1, :]

            def weights(rows, span):
                gap = jnp.minimum(column[rows] - cum_row[:, span], 0.0)
                return (scores[rows, span] * jnp.exp(gap) * step_row[:, span]).astype(BF16)

            inputs = x_pair[:, member * HDIM : (member + 1) * HDIM]
            top = jnp.dot(weights(slice(0, half), slice(0, half)), inputs[:half], preferred_element_type=F32)
            bottom = jnp.dot(weights(slice(half, length), slice(0, length)), inputs, preferred_element_type=F32)
            tops.append(top)
            bottoms.append(bottom)
        lane = lax.broadcasted_iota(jnp.int32, x_pair.shape, 1)
        direct = jnp.where(lane < HDIM, skip[2 * pair], skip[2 * pair + 1]) * x_pair.astype(F32)
        lanes = slice(place * 128, (place + 1) * 128)
        out[0:half, lanes] = jnp.concatenate(tops, axis=1) + direct[:half]
        out[half:length, lanes] = jnp.concatenate(bottoms, axis=1) + direct[half:]


def half_product(which, state, own, factor, c_mat, out_gain, out_weight):
    half = own.shape[1] // 2
    lanes = pl.ds(pl.multiple_of(which * half, 128), half)
    carried = jnp.dot(c_mat[...], state[...], preferred_element_type=F32)
    gated = own[:, lanes] + carried * factor[:, lanes]
    squares = jnp.sum(gated * gated, axis=-1, keepdims=True)
    hidden = (gated * out_gain[:, lanes]).astype(BF16)
    return jnp.dot(hidden, out_weight[lanes, :], preferred_element_type=F32), squares


def first_kernel(mine, own, factor, c_mat, out_gain, out_weight, product_out, squares_out):
    product, squares = half_product(
        lax.axis_index("rows"), mine, own, factor, c_mat, out_gain, out_weight
    )
    product_out[...] = product
    squares_out[...] = jnp.broadcast_to(squares, squares_out.shape)


def finish_kernel(theirs, own, factor, c_mat, out_gain, out_weight, product, squares, embedded, out):
    rest, more = half_product(
        1 - lax.axis_index("rows"), theirs, own, factor, c_mat, out_gain, out_weight
    )
    mean_sq = (squares[:, 0:1] + more) / own.shape[1]
    result = (product[...] + rest) * lax.rsqrt(mean_sq + 1e-05)
    out[...] = (result + embedded[...].astype(F32)[LEAD:]).astype(BF16)


def swap(block, axis, bit):
    return lax.ppermute(block, axis, [(i, i ^ bit) for i in range(lax.axis_size(axis))])


def sending_order(count):
    return (1, *range(count // 2, count), *range(2, count // 2))


def embed_by_rows(pixels, patch_weight, patch_bias):
    col_count = lax.axis_size("cols")
    width = pixels.shape[2]
    partner = swap(pixels, "rows", 1)
    pixels = call(stage_kernel, (pixels,), shape(pixels.shape))
    block = shape((WIN + 8, width))
    scratch = [pltpu.VMEM((CHAN, 2 * pixels.shape[1] + 64, width), BF16)]
    blocks = call(pack_kernel, (pixels, partner), [block] * col_count, scratch, limit=8)
    came = [blocks[0]] + [None] * (col_count - 1)
    for step in sending_order(col_count):
        came[step] = swap(blocks[step], "cols", step)
    weight = patch_weight.transpose(1, 2, 0, 3).reshape(KERNEL, WIN, D)
    weight = jnp.pad(weight, ((0, 0), (0, 128 - WIN), (0, 0))).reshape(KERNEL * 128, D)
    tokens = col_count * width // PATCH
    scratch = [
        pltpu.VMEM((PATCH, 2 * LEAD + tokens, 128), F32),
        pltpu.VMEM((PATCH, 24, 128), F32),
        pltpu.VMEM((LEAD + tokens, KERNEL * 128), BF16),
    ]
    flops = 2 * tokens * KERNEL * 128 * D
    return call(
        embed_kernel, (*came, weight, patch_bias.reshape(1, -1)), shape((LEAD + tokens, D)), scratch,
        flops=flops, moved=6 << 20, limit=16,
    )


def extended(block, sides, width):
    for axis, dim in sides:
        count = lax.axis_size(axis)
        forward = [(i, i + 1) for i in range(count - 1)]
        backward = [(target, source) for source, target in forward]
        low = lax.ppermute(
            lax.slice_in_dim(block, block.shape[dim] - width, None, axis=dim), axis, forward
        )
        high = lax.ppermute(lax.slice_in_dim(block, 0, width, axis=dim), axis, backward)
        block = jnp.concatenate([low, block, high], axis=dim)
    return block


def shifted(block, axis, distance):
    devices = range(lax.axis_size(axis))
    route = [(i - distance, i) for i in devices if i - distance in devices]
    return lax.ppermute(block, axis, route)


def embed_by_blocks(pixels, patch_weight, patch_bias):
    padded = extended(pixels, (("cols", 2), ("rows", 1)), MARGIN)
    embed_grid = lax.conv_general_dilated(
        padded[None],
        patch_weight,
        (PATCH, PATCH),
        "VALID",
        dimension_numbers=("NCHW", "HWIO", "NHWC"),
        preferred_element_type=jnp.float32,
    )[0]
    embed_grid = (embed_grid + patch_bias).astype(jnp.bfloat16)
    row_local, col_local, feature_width = embed_grid.shape
    devices = lax.axis_size(("cols", "rows"))
    row_count = lax.axis_size("rows")
    col_count = lax.axis_size("cols")
    groups = col_count // row_local
    piece_len = col_local * feature_width // devices
    outgoing = embed_grid.reshape(row_local, devices, piece_len)
    spread = lax.all_to_all(outgoing, ("cols", "rows"), split_axis=1, concat_axis=1, tiled=True)
    spread = spread.reshape(row_local, groups, row_local, row_count, piece_len).transpose(
        3, 0, 1, 2, 4
    )
    landed = lax.all_to_all(
        spread.reshape(devices, row_local, piece_len),
        ("cols", "rows"),
        split_axis=0,
        concat_axis=0,
        tiled=True,
    )
    tokens = landed.transpose(1, 0, 2).reshape(row_local * col_local, feature_width)
    tail = shifted(tokens[tokens.shape[0] - LEAD :], ("cols", "rows"), 1)
    return jnp.concatenate([tail, tokens], axis=0)


def body(
    pixels,
    patch_weight,
    patch_bias,
    norm_gain,
    gate_weight,
    mix_weight,
    step_weight,
    step_bias,
    log_rate,
    conv_weight,
    conv_bias,
    skip_gain,
    out_gain,
    out_weight,
):
    col_count = lax.axis_size("cols")
    row_local = pixels.shape[1] // PATCH
    if col_count == row_local:
        embedded = embed_by_rows(pixels, patch_weight, patch_bias)
    else:
        embedded = embed_by_blocks(pixels, patch_weight, patch_bias)
    length = embedded.shape[0] - LEAD
    line = lambda a: a.reshape(1, -1)
    mixed_width = mix_weight.shape[1]
    half = E // 2
    packed = NSTATE + 8
    normed, x, b_mat, c_mat, step, cum, keep, send = call(
        mix_kernel,
        (
            embedded, line(norm_gain), mix_weight, step_weight.T, line(step_bias), line(log_rate),
            conv_weight, line(conv_bias),
        ),
        [
            shape((length, D)), shape((length, E)), shape((length, NSTATE)), shape((length, NSTATE)),
            shape((length, HEADS), F32), shape((length, HEADS), F32), shape((packed, half), F32),
            shape((packed, half)),
        ],
        [pltpu.VMEM((packed, E), F32)],
        flops=2 * length * D * mixed_width, moved=4 << 20, limit=16,
    )
    came = swap(send, "rows", 1)
    summary, message = shape((packed, half), F32), shape((packed, half))
    total, out = call(pair_kernel, (keep, came), [summary, message])
    locals_ = []
    for part in range(2):
        locals_.append(
            call(
                partial(intra_kernel, part * HEADS // 4), (skip_gain, x, b_mat, c_mat, step, cum),
                shape((length, half), F32), scalars=1,
                flops=HEADS * length * length * 128, moved=2 << 20, limit=8,
            )
        )
    own, factor = call(
        gate_kernel, (normed, gate_weight, *locals_, cum), [shape((length, E), F32)] * 2,
        flops=2 * length * D * E, moved=4 << 20, limit=8,
    )
    groups, low = [], 1
    while low < col_count:
        count = min(4, col_count // low)
        groups.append((low, count))
        low *= count
    before = None
    for number, (low, count) in enumerate(groups):
        ending = number + 1 == len(groups)
        arrived = []
        for hop in range(1, count):
            arrived.append(swap(out, "cols", hop * low))
        first = before is None
        inputs = ([total] if first else [total, before]) + arrived
        if ending:
            entering = shape((NSTATE, half))
            mine, theirs = call(partial(enter_kernel, low, count, first), (*inputs, keep, came), [entering, entering])
        else:
            before, out, total = call(partial(join_kernel, low, count, first), inputs, [summary, message, summary])
    theirs = swap(theirs, "rows", 1)
    common = (own, factor, c_mat, line(out_gain), out_weight)
    partial_sum, squares = call(
        first_kernel, (mine, *common), [shape((length, D), F32), shape((length, 128), F32)],
        flops=length * D * E, moved=4 << 20, limit=8,
    )
    return call(
        finish_kernel, (theirs, *common, partial_sum, squares, embedded), shape((length, D)),
        flops=length * D * E, moved=4 << 20, limit=8,
    )


def solution(mesh):
    placed = (
        P(None, "rows", ("slides", "cols")),
        P(),
        P(),
        P(),
        P(),
        P(),
        P(),
        P(),
        P(),
        P(),
        P(),
        P(),
        P(),
        P(),
    )
    return jax.shard_map(
        body,
        mesh=mesh,
        in_specs=placed,
        out_specs=P(("slides", "cols", "rows"), None),
        check_vma=False,
    )
```

```python
from functools import partial

import jax
import jax.numpy as jnp
from jax import lax
from jax.experimental import pallas as pl
from jax.experimental.pallas import tpu as pltpu
from jax.sharding import PartitionSpec as P


E = 1536
D = 768
HDIM = 64
NSTATE = 64
PATCH = 16
KERNEL = 24
HEADS = 24
CHAN = 3
MARGIN = (KERNEL - PATCH) // 2
WIN = CHAN * KERNEL
LEAD = 8
F32 = jnp.float32
BF16 = jnp.bfloat16


def vmem():
    return pl.BlockSpec(memory_space=pltpu.VMEM)


def call(kernel, inputs, outs, scratch=(), limit=4, flops=0, moved=0, scalars=0):
    return pl.pallas_call(
        kernel,
        out_shape=outs,
        in_specs=[pl.BlockSpec(memory_space=pltpu.SMEM)] * scalars + [vmem()] * (len(inputs) - scalars),
        out_specs=jax.tree.map(lambda _: vmem(), outs),
        scratch_shapes=scratch,
        compiler_params=pltpu.CompilerParams(vmem_limit_bytes=limit << 20),
        cost_estimate=pl.CostEstimate(flops=flops, bytes_accessed=moved, transcendentals=0),
    )(*inputs)


def shape(dims, kind=BF16):
    return jax.ShapeDtypeStruct(dims, kind)


def pack_kernel(own, partner, *refs):
    outs, rows = refs[:-1], refs[-1]
    col, row = lax.axis_index("cols"), lax.axis_index("rows")
    local = own.shape[1]
    width = own.shape[2]
    edge = jnp.zeros((CHAN, 32, width), BF16)
    rows[:, 0:32, :] = edge
    rows[:, 32 + 2 * local : 64 + 2 * local, :] = edge
    rows[:, pl.ds(pl.multiple_of(32 + local * row, 32), local), :] = own[...]
    rows[:, pl.ds(pl.multiple_of(32 + local * (1 - row), 32), local), :] = partner[...]
    side = len(outs)
    for step, out in enumerate(outs):
        chip = side * row + ((col % side) ^ step)
        first = pl.multiple_of(2 * PATCH * chip, 32)
        blocks = [rows[channel, pl.ds(first, 80), :].astype(F32) for channel in range(CHAN)]
        pieces = [block[28 + 8 * group : 36 + 8 * group] for group in range(5) for block in blocks]
        tails = [block[12 + 8 * group : 20 + 8 * group, width - 64 :] for group in range(2) for block in blocks]
        tails.append(jnp.zeros((8, width - 64 * len(tails)), F32))
        out[...] = jnp.concatenate([*pieces, jnp.concatenate(tails, axis=1)], axis=0).astype(BF16)


def stage_kernel(pixels, out):
    out[...] = pixels[...]


def pick_matrix():
    row = lax.broadcasted_iota(jnp.int32, (256, 256), 0)
    pixel = lax.broadcasted_iota(jnp.int32, (256, 256), 1)
    return (pixel == (row & 15) * PATCH + (row >> 4)).astype(BF16)


def turned(pick, values):
    return lax.dot_general(pick, values, (((1,), (1,)), ((), ())), preferred_element_type=F32)


def embed_kernel(*refs):
    blocks, (weight, bias, out, picked, tail, wide) = refs[:-6], refs[-6:]
    col, row = lax.axis_index("cols"), lax.axis_index("rows")
    width = blocks[0].shape[1]
    count = len(blocks)
    side = count // 2
    tokens = count * width // PATCH
    local = width // PATCH
    zeros = jnp.zeros((PATCH, LEAD, 128), F32)
    picked[:, 0:LEAD, :] = zeros
    picked[:, LEAD + tokens :, :] = zeros
    blank = jnp.zeros((128 - WIN, width), BF16)
    pick = pick_matrix()
    window = pl.ds(pl.multiple_of(2 * KERNEL * row, 16), WIN)
    edge = jnp.zeros((WIN, 128), F32)
    extra = jnp.zeros((8, 128 * CHAN), F32)
    for place, block in enumerate(blocks):
        source = side * (row if place < side else 1 - row) + ((col % side) ^ (place % side))
        values = jnp.concatenate([block[window, :], blank], axis=0)
        for group in range(width // 256):
            found = turned(pick, values[:, 256 * group : 256 * (group + 1)])
            first = pl.multiple_of(LEAD + source * local + 16 * group, 8)
            picked[:, pl.ds(first, 16), :] = found.reshape(PATCH, 16, 128)
        last = source == count - 1
        edge = jnp.where(last, block[0:WIN, width - 128 :].astype(F32), edge)
        extra = jnp.where(last, block[5 * KERNEL - 8 : 5 * KERNEL + 8, : 128 * CHAN].astype(F32)[8:], extra)
    before = [extra[:, 64 * piece : 64 * (piece + 1)] for piece in range(2 * CHAN)] + [edge[:KERNEL, 64:]]
    last = jnp.where(row == 0, jnp.concatenate(before, axis=0), edge[:, 64:])
    last = jnp.concatenate([last, jnp.zeros((128 - WIN, 64), F32)], axis=0)
    last = jnp.concatenate([jnp.zeros((128, 64), F32), last, jnp.zeros((128, 128), F32)], axis=1)
    tail[:, 0:8, :] = zeros
    tail[:, 8:24, :] = turned(pick, last.astype(BF16)).reshape(PATCH, 16, 128)

    for offset in range(KERNEL):
        place = offset - MARGIN + PATCH
        shift, pixel = place // PATCH - 1, place % PATCH
        ahead = tail[pixel, 8 + shift : 16 + shift, :]
        part = jnp.concatenate([ahead, picked[pixel, LEAD + shift : LEAD + shift + tokens, :]], axis=0)
        wide[:, offset * 128 : (offset + 1) * 128] = part.astype(BF16)
    grid = jnp.dot(wide[...], weight[...], preferred_element_type=F32)
    out[...] = (grid + bias[...]).astype(BF16)


def spread_matrix():
    head = lax.broadcasted_iota(jnp.int32, (HEADS, E), 0)
    lane = lax.broadcasted_iota(jnp.int32, (HEADS, E), 1)
    return ((lane >= head * HDIM) & (lane < (head + 1) * HDIM)).astype(BF16)


def halves(values):
    high = values.astype(BF16)
    return high, (values - high.astype(F32)).astype(BF16)


def spread(values, matrix):
    high, low = halves(values)
    return jnp.dot(high, matrix, preferred_element_type=F32) + jnp.dot(low, matrix, preferred_element_type=F32)


def silu(values):
    half = 0.5 * values
    return half + half * jnp.tanh(half)


def softplus(values):
    small = jnp.exp(-jnp.abs(values))
    return jnp.maximum(values, 0.0) + jnp.log1p(small)


def mix_kernel(
    embedded, norm_gain, mix_weight, step_weight, step_bias, log_rate, conv_weight, conv_bias,
    normed_out, x_out, b_out, c_out, step_out, cum_out, keep_out, send_out, state,
):
    col, row = lax.axis_index("cols"), lax.axis_index("rows")
    resid = embedded[...].astype(F32)
    mean_sq = jnp.mean(resid * resid, axis=-1, keepdims=True)
    normed_f = resid * lax.rsqrt(mean_sq + 1e-05) * norm_gain[...]
    rows = lax.broadcasted_iota(jnp.int32, normed_f.shape, 0)
    blank = (rows < LEAD) & (col == 0) & (row == 0)
    normed = jnp.where(blank, 0.0, normed_f).astype(BF16)
    normed_out[...] = normed_f[LEAD:].astype(BF16)
    length = embedded.shape[0] - LEAD
    step_raw = lax.dot_general(
        normed, step_weight[...], (((1,), (1,)), ((), ())), preferred_element_type=F32
    )[LEAD:]
    step = softplus(step_raw + step_bias[...])
    log_decay = -step * jnp.exp(log_rate[...])
    lower = (
        lax.broadcasted_iota(jnp.int32, (length, length), 0) >= lax.broadcasted_iota(jnp.int32, (length, length), 1)
    ).astype(BF16)
    high = log_decay.astype(BF16)
    middle = (log_decay - high.astype(F32)).astype(BF16)
    low = (log_decay - high.astype(F32) - middle.astype(F32)).astype(BF16)
    cum = jnp.dot(lower, high, preferred_element_type=F32)
    cum = cum + jnp.dot(lower, middle, preferred_element_type=F32)
    cum = cum + jnp.dot(lower, low, preferred_element_type=F32)
    step_out[...] = step
    cum_out[...] = cum
    matrix = spread_matrix()
    last = cum[length - 1 :]
    scales = (jnp.exp(last - cum) * step).astype(BF16)
    state[NSTATE : NSTATE + 8, :] = spread(jnp.broadcast_to(jnp.exp(last), (8, HEADS)), matrix)
    taps = conv_weight.shape[0]

    def project(lanes):
        return jnp.dot(normed, mix_weight[:, lanes], preferred_element_type=F32).astype(BF16)

    def mixed(raw, lanes):
        raw = raw.astype(F32)
        total = conv_weight[0:1, lanes] * raw
        for tap in range(1, taps):
            total = pltpu.roll(total, 1, 0) + conv_weight[tap : tap + 1, lanes] * raw
        return silu(total[LEAD:] + conv_bias[:, lanes]).astype(BF16)

    chunk = 512
    spans = [slice(E, E + 2 * NSTATE)] + [slice(first, first + chunk) for first in range(0, E, chunk)]
    ahead = project(spans[0])
    for place, lanes in enumerate(spans):
        raw = ahead
        if place + 1 < len(spans):
            ahead = project(spans[place + 1])
        part = mixed(raw, lanes)
        if place == 0:
            maps = part.astype(F32)
            b_out[...] = maps[:, :NSTATE].astype(BF16)
            c_out[...] = maps[:, NSTATE:].astype(BF16)
            b_t = maps.T[:NSTATE].astype(BF16)
            continue
        x_out[:, lanes] = part
        to_end = jnp.dot(scales, matrix[:, lanes], preferred_element_type=F32)
        scaled = (part.astype(F32) * to_end).astype(BF16)
        state[0:NSTATE, lanes] = jnp.dot(b_t, scaled, preferred_element_type=F32)
    half = E // 2
    mine = pl.ds(pl.multiple_of(row * half, 128), half)
    theirs = pl.ds(pl.multiple_of((1 - row) * half, 128), half)
    keep_out[...] = state[:, mine]
    send_out[...] = wire(state[0:NSTATE, theirs], state[NSTATE : NSTATE + 8, theirs])


def wire(values, decay):
    high = decay.astype(BF16).astype(F32)
    rest = decay - high
    place = lax.broadcasted_iota(jnp.int32, decay.shape, 0)
    return jnp.concatenate([values, jnp.where(place == 0, high, rest)], axis=0).astype(BF16)


def unwire(message):
    values = message[0:NSTATE, :].astype(F32)
    rows = message[NSTATE : NSTATE + 8, :].astype(F32)
    return values, jnp.broadcast_to(rows[0:1] + rows[1:2], rows.shape)


def product(factors):
    total = factors[0]
    for factor in factors[1:]:
        total = total * factor
    return total


def folded(place, pieces):
    places = [place ^ step for step in range(len(pieces))]
    steps = range(len(pieces))
    one = jnp.ones_like(pieces[0][1])
    all_values, ahead_values = None, None
    for step in steps:
        after = [jnp.where(places[k] > places[step], pieces[k][1], one) for k in steps if k != step]
        between = [
            jnp.where((places[k] > places[step]) & (places[k] < place), pieces[k][1], one)
            for k in steps
            if k not in (0, step)
        ]
        term = product(after)[0:1] * pieces[step][0]
        all_values = term if step == 0 else all_values + term
        if step:
            weight = jnp.where(places[step] < place, product([one, *between]), 0.0)
            term = weight[0:1] * pieces[step][0]
            ahead_values = term if ahead_values is None else ahead_values + term
    all_decay = product([decay for _, decay in pieces])
    ahead_decay = product([jnp.where(places[k] < place, pieces[k][1], one) for k in steps if k])
    return (all_values, all_decay), (ahead_values, ahead_decay)


def read(summary):
    return summary[0:NSTATE, :], summary[NSTATE : NSTATE + 8, :]


def write(summary, piece):
    summary[0:NSTATE, :] = piece[0]
    summary[NSTATE : NSTATE + 8, :] = piece[1]


def chained(earlier, latter):
    return latter[1][0:1] * earlier[0] + latter[0], earlier[1] * latter[1]


def pair_kernel(keep, received, total_out, message_out):
    total, _ = folded(lax.axis_index("rows"), [read(keep), unwire(received)])
    write(total_out, total)
    message_out[...] = wire(*total)


def join_kernel(low, count, first, *refs):
    refs = list(refs)
    total = read(refs.pop(0))
    before = None if first else read(refs.pop(0))
    pieces = [total] + [unwire(refs.pop(0)) for _ in range(count - 1)]
    place = (lax.axis_index("cols") // low) & (count - 1)
    total, ahead = folded(place, pieces)
    before_out, message_out = refs[:2]
    write(before_out, ahead if first else chained(ahead, before))
    message_out[...] = wire(*total)
    write(refs[2], total)


def enter_kernel(low, count, first, *refs):
    refs = list(refs)
    total = read(refs.pop(0))
    before = None if first else read(refs.pop(0))
    pieces = [total] + [unwire(refs.pop(0)) for _ in range(count - 1)]
    keep, received, mine_out, theirs_out = refs
    _, ahead = folded((lax.axis_index("cols") // low) & (count - 1), pieces)
    if not first:
        ahead = chained(ahead, before)
    own, other = read(keep), unwire(received)
    upper = lax.axis_index("rows") == 1
    low_piece = tuple(jnp.where(upper, b, a) for a, b in zip(own, other))
    second = chained(ahead, low_piece)[0]
    mine_out[...] = jnp.where(upper, second, ahead[0]).astype(BF16)
    theirs_out[...] = jnp.where(upper, ahead[0], second).astype(BF16)


def gate_kernel(normed, gate_weight, local_a, local_b, cum, own_out, factor_out):
    gate = jnp.dot(normed[...], gate_weight[...], preferred_element_type=F32).astype(BF16).astype(F32)
    gate = silu(gate)
    half = local_a.shape[1]
    own_out[:, :half] = local_a[...] * gate[:, :half]
    own_out[:, half:] = local_b[...] * gate[:, half:]
    factor_out[...] = spread(jnp.exp(cum[...]), spread_matrix()) * gate


def intra_kernel(first, skip, x, b_mat, c_mat, step, cum, out):
    length = x.shape[0]
    half = length // 2
    scores = lax.dot_general(c_mat[...], b_mat[...], (((1,), (1,)), ((), ())), preferred_element_type=F32)
    causal = lax.broadcasted_iota(jnp.int32, (length, length), 0) >= lax.broadcasted_iota(
        jnp.int32, (length, length), 1
    )
    scores = jnp.where(causal, scores, 0.0)
    wide = jnp.zeros((length, 128 - HEADS), F32)
    cum_v = cum[...]
    cum_t = jnp.concatenate([cum_v, wide], axis=1).T
    step_t = jnp.concatenate([step[...], wide], axis=1).T
    for place in range(out.shape[1] // 128):
        pair = first + place
        x_pair = x[:, pair * 128 : (pair + 1) * 128]
        tops, bottoms = [], []
        for member in range(2):
            head = 2 * pair + member
            column = cum_v[:, head : head + 1]
            cum_row = cum_t[head : head + 1, :]
            step_row = step_t[head : head + 1, :]

            def weights(rows, span):
                gap = jnp.minimum(column[rows] - cum_row[:, span], 0.0)
                return (scores[rows, span] * jnp.exp(gap) * step_row[:, span]).astype(BF16)

            inputs = x_pair[:, member * HDIM : (member + 1) * HDIM]
            top = jnp.dot(weights(slice(0, half), slice(0, half)), inputs[:half], preferred_element_type=F32)
            bottom = jnp.dot(weights(slice(half, length), slice(0, length)), inputs, preferred_element_type=F32)
            tops.append(top)
            bottoms.append(bottom)
        lane = lax.broadcasted_iota(jnp.int32, x_pair.shape, 1)
        direct = jnp.where(lane < HDIM, skip[2 * pair], skip[2 * pair + 1]) * x_pair.astype(F32)
        lanes = slice(place * 128, (place + 1) * 128)
        out[0:half, lanes] = jnp.concatenate(tops, axis=1) + direct[:half]
        out[half:length, lanes] = jnp.concatenate(bottoms, axis=1) + direct[half:]


def half_product(which, state, own, factor, c_mat, out_gain, out_weight):
    half = own.shape[1] // 2
    lanes = pl.ds(pl.multiple_of(which * half, 128), half)
    carried = jnp.dot(c_mat[...], state[...], preferred_element_type=F32)
    gated = own[:, lanes] + carried * factor[:, lanes]
    squares = jnp.sum(gated * gated, axis=-1, keepdims=True)
    hidden = (gated * out_gain[:, lanes]).astype(BF16)
    return jnp.dot(hidden, out_weight[lanes, :], preferred_element_type=F32), squares


def first_kernel(mine, own, factor, c_mat, out_gain, out_weight, product_out, squares_out):
    product, squares = half_product(
        lax.axis_index("rows"), mine, own, factor, c_mat, out_gain, out_weight
    )
    product_out[...] = product
    squares_out[...] = jnp.broadcast_to(squares, squares_out.shape)


def finish_kernel(theirs, own, factor, c_mat, out_gain, out_weight, product, squares, embedded, out):
    rest, more = half_product(
        1 - lax.axis_index("rows"), theirs, own, factor, c_mat, out_gain, out_weight
    )
    mean_sq = (squares[:, 0:1] + more) / own.shape[1]
    result = (product[...] + rest) * lax.rsqrt(mean_sq + 1e-05)
    out[...] = (result + embedded[...].astype(F32)[LEAD:]).astype(BF16)


def swap(block, axis, bit):
    return lax.ppermute(block, axis, [(i, i ^ bit) for i in range(lax.axis_size(axis))])


def sending_order(side):
    return tuple(reversed(range(side)))


def across(block, step):
    side = lax.axis_size("cols") // 2
    pairs = []
    for col in range(2 * side):
        for row in range(2):
            other = side * row + ((col % side) ^ step)
            pairs.append((2 * col + row, 2 * other + col // side))
    return lax.ppermute(block, ("cols", "rows"), pairs)


def embed_by_rows(pixels, patch_weight, patch_bias):
    col_count = lax.axis_size("cols")
    side = col_count // 2
    width = pixels.shape[2]
    partner = swap(pixels, "rows", 1)
    pixels = call(stage_kernel, (pixels,), shape(pixels.shape))
    block = shape((5 * KERNEL + 8, width))
    scratch = [pltpu.VMEM((CHAN, 2 * pixels.shape[1] + 64, width), BF16)]
    blocks = call(pack_kernel, (pixels, partner), [block] * side, scratch, limit=8)
    near, far = [None] * side, [None] * side
    for step in sending_order(side):
        near[step] = across(blocks[step], step)
        far[step] = swap(near[step], "rows", 1)
    came = near + far
    weight = patch_weight.reshape(3, 8, KERNEL, CHAN, D).transpose(2, 0, 3, 1, 4).reshape(KERNEL, WIN, D)
    weight = jnp.pad(weight, ((0, 0), (0, 128 - WIN), (0, 0))).reshape(KERNEL * 128, D)
    tokens = col_count * width // PATCH
    scratch = [
        pltpu.VMEM((PATCH, 2 * LEAD + tokens, 128), F32),
        pltpu.VMEM((PATCH, 24, 128), F32),
        pltpu.VMEM((LEAD + tokens, KERNEL * 128), BF16),
    ]
    flops = 2 * tokens * KERNEL * 128 * D
    return call(
        embed_kernel, (*came, weight, patch_bias.reshape(1, -1)), shape((LEAD + tokens, D)), scratch,
        flops=flops, moved=6 << 20, limit=16,
    )


def extended(block, sides, width):
    for axis, dim in sides:
        count = lax.axis_size(axis)
        forward = [(i, i + 1) for i in range(count - 1)]
        backward = [(target, source) for source, target in forward]
        low = lax.ppermute(
            lax.slice_in_dim(block, block.shape[dim] - width, None, axis=dim), axis, forward
        )
        high = lax.ppermute(lax.slice_in_dim(block, 0, width, axis=dim), axis, backward)
        block = jnp.concatenate([low, block, high], axis=dim)
    return block


def shifted(block, axis, distance):
    devices = range(lax.axis_size(axis))
    route = [(i - distance, i) for i in devices if i - distance in devices]
    return lax.ppermute(block, axis, route)


def embed_by_blocks(pixels, patch_weight, patch_bias):
    padded = extended(pixels, (("cols", 2), ("rows", 1)), MARGIN)
    embed_grid = lax.conv_general_dilated(
        padded[None],
        patch_weight,
        (PATCH, PATCH),
        "VALID",
        dimension_numbers=("NCHW", "HWIO", "NHWC"),
        preferred_element_type=jnp.float32,
    )[0]
    embed_grid = (embed_grid + patch_bias).astype(jnp.bfloat16)
    row_local, col_local, feature_width = embed_grid.shape
    devices = lax.axis_size(("cols", "rows"))
    row_count = lax.axis_size("rows")
    col_count = lax.axis_size("cols")
    groups = col_count // row_local
    piece_len = col_local * feature_width // devices
    outgoing = embed_grid.reshape(row_local, devices, piece_len)
    spread = lax.all_to_all(outgoing, ("cols", "rows"), split_axis=1, concat_axis=1, tiled=True)
    spread = spread.reshape(row_local, groups, row_local, row_count, piece_len).transpose(
        3, 0, 1, 2, 4
    )
    landed = lax.all_to_all(
        spread.reshape(devices, row_local, piece_len),
        ("cols", "rows"),
        split_axis=0,
        concat_axis=0,
        tiled=True,
    )
    tokens = landed.transpose(1, 0, 2).reshape(row_local * col_local, feature_width)
    tail = shifted(tokens[tokens.shape[0] - LEAD :], ("cols", "rows"), 1)
    return jnp.concatenate([tail, tokens], axis=0)


def body(
    pixels,
    patch_weight,
    patch_bias,
    norm_gain,
    gate_weight,
    mix_weight,
    step_weight,
    step_bias,
    log_rate,
    conv_weight,
    conv_bias,
    skip_gain,
    out_gain,
    out_weight,
):
    col_count = lax.axis_size("cols")
    row_local = pixels.shape[1] // PATCH
    if col_count == row_local and lax.axis_size("rows") == 2:
        embedded = embed_by_rows(pixels, patch_weight, patch_bias)
    else:
        embedded = embed_by_blocks(pixels, patch_weight, patch_bias)
    length = embedded.shape[0] - LEAD
    line = lambda a: a.reshape(1, -1)
    mixed_width = mix_weight.shape[1]
    half = E // 2
    packed = NSTATE + 8
    normed, x, b_mat, c_mat, step, cum, keep, send = call(
        mix_kernel,
        (
            embedded, line(norm_gain), mix_weight, step_weight.T, line(step_bias), line(log_rate),
            conv_weight, line(conv_bias),
        ),
        [
            shape((length, D)), shape((length, E)), shape((length, NSTATE)), shape((length, NSTATE)),
            shape((length, HEADS), F32), shape((length, HEADS), F32), shape((packed, half), F32),
            shape((packed, half)),
        ],
        [pltpu.VMEM((packed, E), F32)],
        flops=2 * length * D * mixed_width, moved=4 << 20, limit=16,
    )
    came = swap(send, "rows", 1)
    summary, message = shape((packed, half), F32), shape((packed, half))
    total, out = call(pair_kernel, (keep, came), [summary, message])
    locals_ = []
    for part in range(2):
        locals_.append(
            call(
                partial(intra_kernel, part * HEADS // 4), (skip_gain, x, b_mat, c_mat, step, cum),
                shape((length, half), F32), scalars=1,
                flops=HEADS * length * length * 128, moved=2 << 20, limit=8,
            )
        )
    own, factor = call(
        gate_kernel, (normed, gate_weight, *locals_, cum), [shape((length, E), F32)] * 2,
        flops=2 * length * D * E, moved=4 << 20, limit=8,
    )
    groups, low = [], 1
    while low < col_count:
        count = min(4, col_count // low)
        groups.append((low, count))
        low *= count
    before = None
    for number, (low, count) in enumerate(groups):
        ending = number + 1 == len(groups)
        arrived = []
        for hop in range(1, count):
            arrived.append(swap(out, "cols", hop * low))
        first = before is None
        inputs = ([total] if first else [total, before]) + arrived
        if ending:
            entering = shape((NSTATE, half))
            mine, theirs = call(partial(enter_kernel, low, count, first), (*inputs, keep, came), [entering, entering])
        else:
            before, out, total = call(partial(join_kernel, low, count, first), inputs, [summary, message, summary])
    theirs = swap(theirs, "rows", 1)
    common = (own, factor, c_mat, line(out_gain), out_weight)
    partial_sum, squares = call(
        first_kernel, (mine, *common), [shape((length, D), F32), shape((length, 128), F32)],
        flops=length * D * E, moved=4 << 20, limit=8,
    )
    return call(
        finish_kernel, (theirs, *common, partial_sum, squares, embedded), shape((length, D)),
        flops=length * D * E, moved=4 << 20, limit=8,
    )


def solution(mesh):
    placed = (
        P(None, "rows", ("slides", "cols")),
        P(),
        P(),
        P(),
        P(),
        P(),
        P(),
        P(),
        P(),
        P(),
        P(),
        P(),
        P(),
        P(),
    )
    return jax.shard_map(
        body,
        mesh=mesh,
        in_specs=placed,
        out_specs=P(("slides", "cols", "rows"), None),
        check_vma=False,
    )
```

```python
from functools import partial

import jax
import jax.numpy as jnp
from jax import lax
from jax.experimental import pallas as pl
from jax.experimental.pallas import tpu as pltpu
from jax.sharding import PartitionSpec as P


E = 1536
D = 768
HDIM = 64
NSTATE = 64
PATCH = 16
KERNEL = 24
HEADS = 24
CHAN = 3
MARGIN = (KERNEL - PATCH) // 2
WIN = CHAN * KERNEL
LEAD = 8
F32 = jnp.float32
BF16 = jnp.bfloat16


def vmem():
    return pl.BlockSpec(memory_space=pltpu.VMEM)


def call(kernel, inputs, outs, scratch=(), limit=4, flops=0, moved=0, scalars=0):
    return pl.pallas_call(
        kernel,
        out_shape=outs,
        in_specs=[pl.BlockSpec(memory_space=pltpu.SMEM)] * scalars + [vmem()] * (len(inputs) - scalars),
        out_specs=jax.tree.map(lambda _: vmem(), outs),
        scratch_shapes=scratch,
        compiler_params=pltpu.CompilerParams(vmem_limit_bytes=limit << 20),
        cost_estimate=pl.CostEstimate(flops=flops, bytes_accessed=moved, transcendentals=0),
    )(*inputs)


def shape(dims, kind=BF16):
    return jax.ShapeDtypeStruct(dims, kind)


def pack_kernel(own, partner, *refs):
    outs, rows = refs[:-1], refs[-1]
    col, row = lax.axis_index("cols"), lax.axis_index("rows")
    local = own.shape[1]
    width = own.shape[2]
    edge = jnp.zeros((CHAN, 32, width), BF16)
    rows[:, 0:32, :] = edge
    rows[:, 32 + 2 * local : 64 + 2 * local, :] = edge
    rows[:, pl.ds(pl.multiple_of(32 + local * row, 32), local), :] = own[...]
    rows[:, pl.ds(pl.multiple_of(32 + local * (1 - row), 32), local), :] = partner[...]
    side = len(outs)
    for step, out in enumerate(outs):
        chip = side * row + ((col % side) ^ step)
        first = pl.multiple_of(2 * PATCH * chip, 32)
        blocks = [rows[channel, pl.ds(first, 80), :].astype(F32) for channel in range(CHAN)]
        pieces = [block[28 + 8 * group : 36 + 8 * group] for group in range(5) for block in blocks]
        tails = [block[12 + 8 * group : 20 + 8 * group, width - 64 :] for group in range(2) for block in blocks]
        tails.append(jnp.zeros((8, width - 64 * len(tails)), F32))
        out[...] = jnp.concatenate([*pieces, jnp.concatenate(tails, axis=1)], axis=0).astype(BF16)


def stage_kernel(pixels, out):
    out[...] = pixels[...]


def pick_matrix():
    row = lax.broadcasted_iota(jnp.int32, (256, 256), 0)
    pixel = lax.broadcasted_iota(jnp.int32, (256, 256), 1)
    return (pixel == (row & 15) * PATCH + (row >> 4)).astype(BF16)


def turned(pick, values):
    return lax.dot_general(pick, values, (((1,), (1,)), ((), ())), preferred_element_type=F32)


def embed_kernel(*refs):
    blocks, (weight, bias, out, picked, tail, wide) = refs[:-6], refs[-6:]
    col, row = lax.axis_index("cols"), lax.axis_index("rows")
    width = blocks[0].shape[1]
    count = len(blocks)
    side = count // 2
    tokens = count * width // PATCH
    local = width // PATCH
    zeros = jnp.zeros((PATCH, LEAD, 128), F32)
    picked[:, 0:LEAD, :] = zeros
    picked[:, LEAD + tokens :, :] = zeros
    blank = jnp.zeros((128 - WIN, width), BF16)
    pick = pick_matrix()
    window = pl.ds(pl.multiple_of(2 * KERNEL * row, 16), WIN)
    edge = jnp.zeros((WIN, 128), F32)
    extra = jnp.zeros((8, 128 * CHAN), F32)
    for place, block in enumerate(blocks):
        source = side * (row if place < side else 1 - row) + ((col % side) ^ (place % side))
        values = jnp.concatenate([block[window, :], blank], axis=0)
        for group in range(width // 256):
            found = turned(pick, values[:, 256 * group : 256 * (group + 1)])
            first = pl.multiple_of(LEAD + source * local + 16 * group, 8)
            picked[:, pl.ds(first, 16), :] = found.reshape(PATCH, 16, 128)
        last = source == count - 1
        edge = jnp.where(last, block[0:WIN, width - 128 :].astype(F32), edge)
        extra = jnp.where(last, block[5 * KERNEL - 8 : 5 * KERNEL + 8, : 128 * CHAN].astype(F32)[8:], extra)
    before = [extra[:, 64 * piece : 64 * (piece + 1)] for piece in range(2 * CHAN)] + [edge[:KERNEL, 64:]]
    last = jnp.where(row == 0, jnp.concatenate(before, axis=0), edge[:, 64:])
    last = jnp.concatenate([last, jnp.zeros((128 - WIN, 64), F32)], axis=0)
    last = jnp.concatenate([jnp.zeros((128, 64), F32), last, jnp.zeros((128, 128), F32)], axis=1)
    tail[:, 0:8, :] = zeros
    tail[:, 8:24, :] = turned(pick, last.astype(BF16)).reshape(PATCH, 16, 128)

    for offset in range(KERNEL):
        place = offset - MARGIN + PATCH
        shift, pixel = place // PATCH - 1, place % PATCH
        ahead = tail[pixel, 8 + shift : 16 + shift, :]
        part = jnp.concatenate([ahead, picked[pixel, LEAD + shift : LEAD + shift + tokens, :]], axis=0)
        wide[:, offset * 128 : (offset + 1) * 128] = part.astype(BF16)
    grid = jnp.dot(wide[...], weight[...], preferred_element_type=F32)
    out[...] = (grid + bias[...]).astype(BF16)


def spread_matrix():
    head = lax.broadcasted_iota(jnp.int32, (HEADS, E), 0)
    lane = lax.broadcasted_iota(jnp.int32, (HEADS, E), 1)
    return ((lane >= head * HDIM) & (lane < (head + 1) * HDIM)).astype(BF16)


def halves(values):
    high = values.astype(BF16)
    return high, (values - high.astype(F32)).astype(BF16)


def spread(values, matrix):
    high, low = halves(values)
    return jnp.dot(high, matrix, preferred_element_type=F32) + jnp.dot(low, matrix, preferred_element_type=F32)


def silu(values):
    half = 0.5 * values
    return half + half * jnp.tanh(half)


def softplus(values):
    small = jnp.exp(-jnp.abs(values))
    return jnp.maximum(values, 0.0) + jnp.log1p(small)


def half_mix(which, normed, scales, b_t, mix_weight, conv_weight, conv_bias, x_out):
    half = E // 2
    matrix = spread_matrix()
    states = []
    chunk = 256
    spans = [
        pl.ds(pl.multiple_of(which * half + first, 128), chunk) for first in range(0, half, chunk)
    ]
    wanted = jnp.where(which == 0, matrix[:, :half].astype(F32), matrix[:, half:].astype(F32)).astype(BF16)
    ahead = project(normed, mix_weight, spans[0])
    for place, lanes in enumerate(spans):
        raw = ahead
        if place + 1 < len(spans):
            ahead = project(normed, mix_weight, spans[place + 1])
        part = mixed(raw, conv_weight[:, lanes], conv_bias[:, lanes])
        local = slice(place * chunk, (place + 1) * chunk)
        x_out[:, local] = part
        to_end = jnp.dot(scales, wanted[:, local], preferred_element_type=F32)
        scaled = (part.astype(F32) * to_end).astype(BF16)
        states.append(jnp.dot(b_t, scaled, preferred_element_type=F32))
    return jnp.concatenate(states, axis=1)


def project(normed, mix_weight, lanes):
    return jnp.dot(normed, mix_weight[:, lanes], preferred_element_type=F32).astype(BF16)


def mixed(raw, weight, bias):
    raw = raw.astype(F32)
    total = weight[0:1] * raw
    for tap in range(1, weight.shape[0]):
        total = pltpu.roll(total, 1, 0) + weight[tap : tap + 1] * raw
    return silu(total[LEAD:] + bias).astype(BF16)


def mix_kernel(
    embedded, norm_gain, mix_weight, step_weight, step_bias, log_rate, conv_weight, conv_bias,
    normed_out, x_out, b_out, c_out, b_t_out, step_out, cum_out, scales_out, decay_out, send_out,
):
    col, row = lax.axis_index("cols"), lax.axis_index("rows")
    resid = embedded[...].astype(F32)
    mean_sq = jnp.mean(resid * resid, axis=-1, keepdims=True)
    normed_f = resid * lax.rsqrt(mean_sq + 1e-05) * norm_gain[...]
    rows = lax.broadcasted_iota(jnp.int32, normed_f.shape, 0)
    blank = (rows < LEAD) & (col == 0) & (row == 0)
    normed = jnp.where(blank, 0.0, normed_f).astype(BF16)
    normed_out[...] = normed
    length = embedded.shape[0] - LEAD
    maps_raw = project(normed, mix_weight, slice(E, E + 2 * NSTATE))
    step_raw = lax.dot_general(
        normed, step_weight[...], (((1,), (1,)), ((), ())), preferred_element_type=F32
    )[LEAD:]
    step = softplus(step_raw + step_bias[...])
    log_decay = -step * jnp.exp(log_rate[...])
    lower = (
        lax.broadcasted_iota(jnp.int32, (length, length), 0) >= lax.broadcasted_iota(jnp.int32, (length, length), 1)
    ).astype(BF16)
    high = log_decay.astype(BF16)
    middle = (log_decay - high.astype(F32)).astype(BF16)
    low = (log_decay - high.astype(F32) - middle.astype(F32)).astype(BF16)
    cum = jnp.dot(lower, high, preferred_element_type=F32)
    cum = cum + jnp.dot(lower, middle, preferred_element_type=F32)
    cum = cum + jnp.dot(lower, low, preferred_element_type=F32)
    step_out[...] = step
    cum_out[...] = cum
    last = cum[length - 1 :]
    scales = (jnp.exp(last - cum) * step).astype(BF16)
    scales_out[...] = scales
    decay = spread(jnp.broadcast_to(jnp.exp(last), (8, HEADS)), spread_matrix())
    maps = mixed(maps_raw, conv_weight[:, E:], conv_bias[:, E:]).astype(F32)
    b_out[...] = maps[:, :NSTATE].astype(BF16)
    c_out[...] = maps[:, NSTATE:].astype(BF16)
    b_t = maps.T[:NSTATE].astype(BF16)
    b_t_out[...] = b_t
    state = half_mix(1 - row, normed, scales, b_t, mix_weight, conv_weight, conv_bias, x_out)
    half = E // 2
    first = row == 0
    decay_out[...] = jnp.where(first, decay[:, :half], decay[:, half:])
    send_out[...] = wire(state, jnp.where(first, decay[:, half:], decay[:, :half]))


def rest_kernel(normed, scales, b_t, mix_weight, conv_weight, conv_bias, decay, x_out, keep_out):
    keep_out[0:NSTATE, :] = half_mix(
        lax.axis_index("rows"), normed[...], scales[...], b_t[...], mix_weight, conv_weight, conv_bias, x_out
    )
    keep_out[NSTATE : NSTATE + 8, :] = decay[...]


def wire(values, decay):
    high = decay.astype(BF16).astype(F32)
    rest = decay - high
    place = lax.broadcasted_iota(jnp.int32, decay.shape, 0)
    return jnp.concatenate([values, jnp.where(place == 0, high, rest)], axis=0).astype(BF16)


def unwire(message):
    values = message[0:NSTATE, :].astype(F32)
    rows = message[NSTATE : NSTATE + 8, :].astype(F32)
    return values, jnp.broadcast_to(rows[0:1] + rows[1:2], rows.shape)


def product(factors):
    total = factors[0]
    for factor in factors[1:]:
        total = total * factor
    return total


def folded(place, pieces):
    places = [place ^ step for step in range(len(pieces))]
    steps = range(len(pieces))
    one = jnp.ones_like(pieces[0][1])
    all_values, ahead_values = None, None
    for step in steps:
        after = [jnp.where(places[k] > places[step], pieces[k][1], one) for k in steps if k != step]
        between = [
            jnp.where((places[k] > places[step]) & (places[k] < place), pieces[k][1], one)
            for k in steps
            if k not in (0, step)
        ]
        term = product(after)[0:1] * pieces[step][0]
        all_values = term if step == 0 else all_values + term
        if step:
            weight = jnp.where(places[step] < place, product([one, *between]), 0.0)
            term = weight[0:1] * pieces[step][0]
            ahead_values = term if ahead_values is None else ahead_values + term
    all_decay = product([decay for _, decay in pieces])
    ahead_decay = product([jnp.where(places[k] < place, pieces[k][1], one) for k in steps if k])
    return (all_values, all_decay), (ahead_values, ahead_decay)


def read(summary):
    return summary[0:NSTATE, :], summary[NSTATE : NSTATE + 8, :]


def write(summary, piece):
    summary[0:NSTATE, :] = piece[0]
    summary[NSTATE : NSTATE + 8, :] = piece[1]


def chained(earlier, latter):
    return latter[1][0:1] * earlier[0] + latter[0], earlier[1] * latter[1]


def pair_kernel(keep, received, total_out, message_out):
    total, _ = folded(lax.axis_index("rows"), [read(keep), unwire(received)])
    write(total_out, total)
    message_out[...] = wire(*total)


def join_kernel(low, count, first, *refs):
    refs = list(refs)
    total = read(refs.pop(0))
    before = None if first else read(refs.pop(0))
    pieces = [total] + [unwire(refs.pop(0)) for _ in range(count - 1)]
    place = (lax.axis_index("cols") // low) & (count - 1)
    total, ahead = folded(place, pieces)
    before_out, message_out = refs[:2]
    write(before_out, ahead if first else chained(ahead, before))
    message_out[...] = wire(*total)
    write(refs[2], total)


def enter_kernel(low, count, first, *refs):
    refs = list(refs)
    total = read(refs.pop(0))
    before = None if first else read(refs.pop(0))
    pieces = [total] + [unwire(refs.pop(0)) for _ in range(count - 1)]
    keep, received, mine_out, theirs_out = refs
    _, ahead = folded((lax.axis_index("cols") // low) & (count - 1), pieces)
    if not first:
        ahead = chained(ahead, before)
    own, other = read(keep), unwire(received)
    upper = lax.axis_index("rows") == 1
    low_piece = tuple(jnp.where(upper, b, a) for a, b in zip(own, other))
    second = chained(ahead, low_piece)[0]
    mine_out[...] = jnp.where(upper, second, ahead[0]).astype(BF16)
    theirs_out[...] = jnp.where(upper, ahead[0], second).astype(BF16)


def gate_kernel(normed, gate_weight, local_mine, local_theirs, cum, own_out, factor_out):
    gate = jnp.dot(normed[...], gate_weight[...], preferred_element_type=F32)[LEAD:].astype(BF16).astype(F32)
    gate = silu(gate)
    half = local_mine.shape[1]
    upper = lax.axis_index("rows") == 1
    own_out[:, :half] = jnp.where(upper, local_theirs[...], local_mine[...]) * gate[:, :half]
    own_out[:, half:] = jnp.where(upper, local_mine[...], local_theirs[...]) * gate[:, half:]
    factor_out[...] = spread(jnp.exp(cum[...]), spread_matrix()) * gate


def intra_kernel(flip, skip, x, b_mat, c_mat, step, cum, out):
    row = lax.axis_index("rows")
    which = 1 - row if flip else row
    heads = HEADS // 2
    upper = which == 1
    length = x.shape[0]
    half = length // 2
    scores = lax.dot_general(c_mat[...], b_mat[...], (((1,), (1,)), ((), ())), preferred_element_type=F32)
    causal = lax.broadcasted_iota(jnp.int32, (length, length), 0) >= lax.broadcasted_iota(
        jnp.int32, (length, length), 1
    )
    scores = jnp.where(causal, scores, 0.0)
    wide = jnp.zeros((length, 128 - heads), F32)
    cum_v = jnp.where(upper, cum[:, heads:], cum[:, :heads])
    cum_t = jnp.concatenate([cum_v, wide], axis=1).T
    step_t = jnp.concatenate([jnp.where(upper, step[:, heads:], step[:, :heads]), wide], axis=1).T
    for place in range(out.shape[1] // 128):
        pair = place
        x_pair = x[:, pair * 128 : (pair + 1) * 128]
        tops, bottoms = [], []
        for member in range(2):
            head = 2 * pair + member
            column = cum_v[:, head : head + 1]
            cum_row = cum_t[head : head + 1, :]
            step_row = step_t[head : head + 1, :]

            def weights(rows, span):
                gap = jnp.minimum(column[rows] - cum_row[:, span], 0.0)
                return (scores[rows, span] * jnp.exp(gap) * step_row[:, span]).astype(BF16)

            inputs = x_pair[:, member * HDIM : (member + 1) * HDIM]
            top = jnp.dot(weights(slice(0, half), slice(0, half)), inputs[:half], preferred_element_type=F32)
            bottom = jnp.dot(weights(slice(half, length), slice(0, length)), inputs, preferred_element_type=F32)
            tops.append(top)
            bottoms.append(bottom)
        lane = lax.broadcasted_iota(jnp.int32, x_pair.shape, 1)
        base = which * heads + 2 * pair
        direct = jnp.where(lane < HDIM, skip[base], skip[base + 1]) * x_pair.astype(F32)
        lanes = slice(place * 128, (place + 1) * 128)
        out[0:half, lanes] = jnp.concatenate(tops, axis=1) + direct[:half]
        out[half:length, lanes] = jnp.concatenate(bottoms, axis=1) + direct[half:]


def half_product(which, state, own, factor, c_mat, out_gain, out_weight):
    half = own.shape[1] // 2
    lanes = pl.ds(pl.multiple_of(which * half, 128), half)
    carried = jnp.dot(c_mat[...], state[...], preferred_element_type=F32)
    gated = own[:, lanes] + carried * factor[:, lanes]
    squares = jnp.sum(gated * gated, axis=-1, keepdims=True)
    hidden = (gated * out_gain[:, lanes]).astype(BF16)
    return jnp.dot(hidden, out_weight[lanes, :], preferred_element_type=F32), squares


def first_kernel(mine, own, factor, c_mat, out_gain, out_weight, product_out, squares_out):
    product, squares = half_product(
        lax.axis_index("rows"), mine, own, factor, c_mat, out_gain, out_weight
    )
    product_out[...] = product
    squares_out[...] = jnp.broadcast_to(squares, squares_out.shape)


def finish_kernel(theirs, own, factor, c_mat, out_gain, out_weight, product, squares, embedded, out):
    rest, more = half_product(
        1 - lax.axis_index("rows"), theirs, own, factor, c_mat, out_gain, out_weight
    )
    mean_sq = (squares[:, 0:1] + more) / own.shape[1]
    result = (product[...] + rest) * lax.rsqrt(mean_sq + 1e-05)
    out[...] = (result + embedded[...].astype(F32)[LEAD:]).astype(BF16)


def swap(block, axis, bit):
    return lax.ppermute(block, axis, [(i, i ^ bit) for i in range(lax.axis_size(axis))])


def sending_order(side):
    return (*range(side // 2, side), *reversed(range(side // 2)))


def across(block, step):
    side = lax.axis_size("cols") // 2
    pairs = []
    for col in range(2 * side):
        for row in range(2):
            other = side * row + ((col % side) ^ step)
            pairs.append((2 * col + row, 2 * other + col // side))
    return lax.ppermute(block, ("cols", "rows"), pairs)


def embed_by_rows(pixels, patch_weight, patch_bias):
    col_count = lax.axis_size("cols")
    side = col_count // 2
    width = pixels.shape[2]
    partner = swap(pixels, "rows", 1)
    pixels = call(stage_kernel, (pixels,), shape(pixels.shape))
    block = shape((5 * KERNEL + 8, width))
    scratch = [pltpu.VMEM((CHAN, 2 * pixels.shape[1] + 64, width), BF16)]
    blocks = call(pack_kernel, (pixels, partner), [block] * side, scratch, limit=8)
    near, far = [None] * side, [None] * side
    for step in sending_order(side):
        near[step] = across(blocks[step], step)
        far[step] = swap(near[step], "rows", 1)
    came = near + far
    weight = patch_weight.reshape(3, 8, KERNEL, CHAN, D).transpose(2, 0, 3, 1, 4).reshape(KERNEL, WIN, D)
    weight = jnp.pad(weight, ((0, 0), (0, 128 - WIN), (0, 0))).reshape(KERNEL * 128, D)
    tokens = col_count * width // PATCH
    scratch = [
        pltpu.VMEM((PATCH, 2 * LEAD + tokens, 128), F32),
        pltpu.VMEM((PATCH, 24, 128), F32),
        pltpu.VMEM((LEAD + tokens, KERNEL * 128), BF16),
    ]
    flops = 2 * tokens * KERNEL * 128 * D
    return call(
        embed_kernel, (*came, weight, patch_bias.reshape(1, -1)), shape((LEAD + tokens, D)), scratch,
        flops=flops, moved=6 << 20, limit=16,
    )


def extended(block, sides, width):
    for axis, dim in sides:
        count = lax.axis_size(axis)
        forward = [(i, i + 1) for i in range(count - 1)]
        backward = [(target, source) for source, target in forward]
        low = lax.ppermute(
            lax.slice_in_dim(block, block.shape[dim] - width, None, axis=dim), axis, forward
        )
        high = lax.ppermute(lax.slice_in_dim(block, 0, width, axis=dim), axis, backward)
        block = jnp.concatenate([low, block, high], axis=dim)
    return block


def shifted(block, axis, distance):
    devices = range(lax.axis_size(axis))
    route = [(i - distance, i) for i in devices if i - distance in devices]
    return lax.ppermute(block, axis, route)


def embed_by_blocks(pixels, patch_weight, patch_bias):
    padded = extended(pixels, (("cols", 2), ("rows", 1)), MARGIN)
    embed_grid = lax.conv_general_dilated(
        padded[None],
        patch_weight,
        (PATCH, PATCH),
        "VALID",
        dimension_numbers=("NCHW", "HWIO", "NHWC"),
        preferred_element_type=jnp.float32,
    )[0]
    embed_grid = (embed_grid + patch_bias).astype(jnp.bfloat16)
    row_local, col_local, feature_width = embed_grid.shape
    devices = lax.axis_size(("cols", "rows"))
    row_count = lax.axis_size("rows")
    col_count = lax.axis_size("cols")
    groups = col_count // row_local
    piece_len = col_local * feature_width // devices
    outgoing = embed_grid.reshape(row_local, devices, piece_len)
    spread = lax.all_to_all(outgoing, ("cols", "rows"), split_axis=1, concat_axis=1, tiled=True)
    spread = spread.reshape(row_local, groups, row_local, row_count, piece_len).transpose(
        3, 0, 1, 2, 4
    )
    landed = lax.all_to_all(
        spread.reshape(devices, row_local, piece_len),
        ("cols", "rows"),
        split_axis=0,
        concat_axis=0,
        tiled=True,
    )
    tokens = landed.transpose(1, 0, 2).reshape(row_local * col_local, feature_width)
    tail = shifted(tokens[tokens.shape[0] - LEAD :], ("cols", "rows"), 1)
    return jnp.concatenate([tail, tokens], axis=0)


def body(
    pixels,
    patch_weight,
    patch_bias,
    norm_gain,
    gate_weight,
    mix_weight,
    step_weight,
    step_bias,
    log_rate,
    conv_weight,
    conv_bias,
    skip_gain,
    out_gain,
    out_weight,
):
    col_count = lax.axis_size("cols")
    row_local = pixels.shape[1] // PATCH
    if col_count == row_local and lax.axis_size("rows") == 2:
        embedded = embed_by_rows(pixels, patch_weight, patch_bias)
    else:
        embedded = embed_by_blocks(pixels, patch_weight, patch_bias)
    length = embedded.shape[0] - LEAD
    line = lambda a: a.reshape(1, -1)
    mixed_width = mix_weight.shape[1]
    half = E // 2
    packed = NSTATE + 8
    conv = (conv_weight, line(conv_bias))
    normed, x_theirs, b_mat, c_mat, b_t, step, cum, scales, decay, send = call(
        mix_kernel,
        (embedded, line(norm_gain), mix_weight, step_weight.T, line(step_bias), line(log_rate), *conv),
        [
            shape((LEAD + length, D)), shape((length, half)), shape((length, NSTATE)), shape((length, NSTATE)),
            shape((NSTATE, length)), shape((length, HEADS), F32), shape((length, HEADS), F32),
            shape((length, HEADS)), shape((8, half), F32), shape((packed, half)),
        ],
        flops=length * D * mixed_width, moved=4 << 20, limit=16,
    )
    came = swap(send, "rows", 1)
    summary, message = shape((packed, half), F32), shape((packed, half))
    x_mine, keep = call(
        rest_kernel, (normed, scales, b_t, mix_weight, *conv, decay), [shape((length, half)), summary],
        flops=length * D * mixed_width, moved=4 << 20, limit=16,
    )
    total, out = call(pair_kernel, (keep, came), [summary, message])
    locals_ = []
    for part in range(2):
        locals_.append(
            call(
                partial(intra_kernel, bool(part)), (skip_gain, (x_mine, x_theirs)[part], b_mat, c_mat, step, cum),
                shape((length, half), F32), scalars=1,
                flops=HEADS * length * length * 128, moved=2 << 20, limit=8,
            )
        )
    own, factor = call(
        gate_kernel, (normed, gate_weight, *locals_, cum), [shape((length, E), F32)] * 2,
        flops=2 * length * D * E, moved=4 << 20, limit=8,
    )
    groups, low = [], 1
    while low < col_count:
        count = min(4, col_count // low)
        groups.append((low, count))
        low *= count
    before = None
    for number, (low, count) in enumerate(groups):
        ending = number + 1 == len(groups)
        arrived = []
        for hop in range(1, count):
            arrived.append(swap(out, "cols", hop * low))
        first = before is None
        inputs = ([total] if first else [total, before]) + arrived
        if ending:
            entering = shape((NSTATE, half))
            mine, theirs = call(partial(enter_kernel, low, count, first), (*inputs, keep, came), [entering, entering])
        else:
            before, out, total = call(partial(join_kernel, low, count, first), inputs, [summary, message, summary])
    theirs = swap(theirs, "rows", 1)
    common = (own, factor, c_mat, line(out_gain), out_weight)
    partial_sum, squares = call(
        first_kernel, (mine, *common), [shape((length, D), F32), shape((length, 128), F32)],
        flops=length * D * E, moved=4 << 20, limit=8,
    )
    return call(
        finish_kernel, (theirs, *common, partial_sum, squares, embedded), shape((length, D)),
        flops=length * D * E, moved=4 << 20, limit=8,
    )


def solution(mesh):
    placed = (
        P(None, "rows", ("slides", "cols")),
        P(),
        P(),
        P(),
        P(),
        P(),
        P(),
        P(),
        P(),
        P(),
        P(),
        P(),
        P(),
        P(),
    )
    return jax.shard_map(
        body,
        mesh=mesh,
        in_specs=placed,
        out_specs=P(("slides", "cols", "rows"), None),
        check_vma=False,
    )
```

```python
from functools import partial

import jax
import jax.numpy as jnp
from jax import lax
from jax.experimental import pallas as pl
from jax.experimental.pallas import tpu as pltpu
from jax.sharding import PartitionSpec as P


E = 1536
D = 768
HDIM = 64
NSTATE = 64
PATCH = 16
KERNEL = 24
HEADS = 24
CHAN = 3
MARGIN = (KERNEL - PATCH) // 2
WIN = CHAN * KERNEL
LEAD = 8
F32 = jnp.float32
BF16 = jnp.bfloat16


def vmem():
    return pl.BlockSpec(memory_space=pltpu.VMEM)


def call(kernel, inputs, outs, scratch=(), limit=4, flops=0, moved=0, scalars=0):
    return pl.pallas_call(
        kernel,
        out_shape=outs,
        in_specs=[pl.BlockSpec(memory_space=pltpu.SMEM)] * scalars + [vmem()] * (len(inputs) - scalars),
        out_specs=jax.tree.map(lambda _: vmem(), outs),
        scratch_shapes=scratch,
        compiler_params=pltpu.CompilerParams(vmem_limit_bytes=limit << 20),
        cost_estimate=pl.CostEstimate(flops=flops, bytes_accessed=moved, transcendentals=0),
    )(*inputs)


def shape(dims, kind=BF16):
    return jax.ShapeDtypeStruct(dims, kind)


def pack_kernel(own, partner, *refs):
    outs, rows = refs[:-1], refs[-1]
    col, row = lax.axis_index("cols"), lax.axis_index("rows")
    local = own.shape[1]
    width = own.shape[2]
    edge = jnp.zeros((CHAN, 32, width), BF16)
    rows[:, 0:32, :] = edge
    rows[:, 32 + 2 * local : 64 + 2 * local, :] = edge
    rows[:, pl.ds(pl.multiple_of(32 + local * row, 32), local), :] = own[...]
    rows[:, pl.ds(pl.multiple_of(32 + local * (1 - row), 32), local), :] = partner[...]
    side = len(outs)
    for step, out in enumerate(outs):
        chip = side * row + ((col % side) ^ step)
        first = pl.multiple_of(2 * PATCH * chip, 32)
        blocks = [rows[channel, pl.ds(first, 80), :].astype(F32) for channel in range(CHAN)]
        pieces = [block[28 + 8 * group : 36 + 8 * group] for group in range(5) for block in blocks]
        tails = [block[12 + 8 * group : 20 + 8 * group, width - 64 :] for group in range(2) for block in blocks]
        tails.append(jnp.zeros((8, width - 64 * len(tails)), F32))
        out[...] = jnp.concatenate([*pieces, jnp.concatenate(tails, axis=1)], axis=0).astype(BF16)


def stage_kernel(pixels, out):
    out[...] = pixels[...]


def pick_matrix():
    row = lax.broadcasted_iota(jnp.int32, (256, 256), 0)
    pixel = lax.broadcasted_iota(jnp.int32, (256, 256), 1)
    return (pixel == (row & 15) * PATCH + (row >> 4)).astype(BF16)


def turned(pick, values):
    return lax.dot_general(pick, values, (((1,), (1,)), ((), ())), preferred_element_type=F32)


def window_pixel(offset):
    place = offset - MARGIN + PATCH
    return place % PATCH, place // PATCH - 1


def neighbours():
    return [offset for offset in range(KERNEL) if window_pixel(offset)[1]]


def place_tokens(pick, values, first, wide, beside):
    found = turned(pick, values).reshape(PATCH, 16, 128)
    rounded = found.astype(BF16)
    for offset in range(KERNEL):
        pixel, shift = window_pixel(offset)
        if shift == 0:
            wide[pl.ds(first, 16), offset * 128 : (offset + 1) * 128] = rounded[pixel]
    for slot, offset in enumerate(neighbours()):
        beside[slot, pl.ds(pl.multiple_of(LEAD + first, 8), 16), :] = found[window_pixel(offset)[0]]


def place_beside(count, first, wide, beside):
    for slot, offset in enumerate(neighbours()):
        start = LEAD + window_pixel(offset)[1]
        part = beside[slot, start : start + count, :]
        wide[first : first + count, offset * 128 : (offset + 1) * 128] = part.astype(BF16)


def clear_ends(count, beside):
    zeros = jnp.zeros((beside.shape[0], LEAD, 128), F32)
    beside[:, 0:LEAD, :] = zeros
    beside[:, LEAD + count : LEAD + count + LEAD, :] = zeros


def windows_of(block, row, lanes):
    window = pl.ds(pl.multiple_of(2 * KERNEL * row, 16), WIN)
    values = block[window, lanes]
    return jnp.concatenate([values, jnp.zeros((128 - WIN, values.shape[1]), BF16)], axis=0)


def own_kernel(*refs):
    blocks, (weight, bias, out, wide, beside) = refs[:-5], refs[-5:]
    col, row = lax.axis_index("cols"), lax.axis_index("rows")
    side = len(blocks)
    width = blocks[0].shape[1]
    tokens = side * width // PATCH
    pick = pick_matrix()
    clear_ends(tokens, beside)
    for step, block in enumerate(blocks):
        for group in range(width // 256):
            first = pl.multiple_of(((col % side) ^ step) * (width // PATCH) + 16 * group, 16)
            values = windows_of(block, row, slice(256 * group, 256 * (group + 1)))
            place_tokens(pick, values, first, wide, beside)
    place_beside(tokens, 0, wide, beside)
    grid = jnp.dot(wide[...], weight[...], preferred_element_type=F32)
    out[...] = (grid + bias[...]).astype(BF16)


def rest_of_row_kernel(*refs):
    blocks, (weight, bias, own, out, wide, beside, tail) = refs[:-7], refs[-7:]
    col, row = lax.axis_index("cols"), lax.axis_index("rows")
    count = len(blocks)
    side = count // 2
    width = blocks[0].shape[1]
    tokens = side * width // PATCH
    reach = tokens + 16
    pick = pick_matrix()
    clear_ends(reach, beside)
    lower = row == 0
    for step, block in enumerate(blocks[side:]):
        for group in range(width // 256):
            place = ((col % side) ^ step) * (width // PATCH) + 16 * group + 16 * (1 - row)
            values = windows_of(block, row, slice(256 * group, 256 * (group + 1)))
            place_tokens(pick, values, pl.multiple_of(place, 16), wide, beside)
    middle = jnp.zeros((128, 256), F32)
    for step, block in enumerate(blocks[:side]):
        here = ((col % side) ^ step) == jnp.where(lower, side - 1, 0)
        values = jnp.where(
            lower, windows_of(block, row, slice(width - 256, width)).astype(F32),
            windows_of(block, row, slice(0, 256)).astype(F32),
        )
        middle = jnp.where(here, values, middle)
    place_tokens(pick, middle.astype(BF16), pl.multiple_of(tokens * row, 16), wide, beside)
    place_beside(reach, 0, wide, beside)
    edge = jnp.zeros((WIN, 128), F32)
    extra = jnp.zeros((8, 128 * CHAN), F32)
    for place, block in enumerate(blocks):
        source = side * (row if place < side else 1 - row) + ((col % side) ^ (place % side))
        last = source == count - 1
        edge = jnp.where(last, block[0:WIN, width - 128 :].astype(F32), edge)
        extra = jnp.where(last, block[5 * KERNEL - 8 : 5 * KERNEL + 8, : 128 * CHAN].astype(F32)[8:], extra)
    before = [extra[:, 64 * piece : 64 * (piece + 1)] for piece in range(2 * CHAN)] + [edge[:KERNEL, 64:]]
    last = jnp.where(lower, jnp.concatenate(before, axis=0), edge[:, 64:])
    last = jnp.concatenate([last, jnp.zeros((128 - WIN, 64), F32)], axis=0)
    last = jnp.concatenate([jnp.zeros((128, 64), F32), last, jnp.zeros((128, 128), F32)], axis=1)
    tail[:, 0:8, :] = jnp.zeros((PATCH, 8, 128), F32)
    tail[:, 8:24, :] = turned(pick, last.astype(BF16)).reshape(PATCH, 16, 128)
    for offset in range(KERNEL):
        pixel, shift = window_pixel(offset)
        part = tail[pixel, 8 + shift : 16 + shift, :]
        wide[reach:, offset * 128 : (offset + 1) * 128] = part.astype(BF16)
    grid = jnp.dot(wide[...], weight[...], preferred_element_type=F32) + bias[...]
    near, far = pl.ds(pl.multiple_of(tokens * row, 16), tokens), pl.ds(pl.multiple_of(tokens * (1 - row), 16), tokens)
    spot = lax.broadcasted_iota(jnp.int32, own.shape, 0)
    midway = jnp.where(lower, grid[15:16], grid[tokens : tokens + 1])
    here = spot == jnp.where(lower, tokens - 1, 0)
    out[near, :] = jnp.where(here, midway, own[...].astype(F32)).astype(BF16)
    out[far, :] = jnp.where(lower, grid[16:reach], grid[:tokens]).astype(BF16)
    out[2 * tokens :, :] = grid[reach:].astype(BF16)


def spread_matrix():
    head = lax.broadcasted_iota(jnp.int32, (HEADS, E), 0)
    lane = lax.broadcasted_iota(jnp.int32, (HEADS, E), 1)
    return ((lane >= head * HDIM) & (lane < (head + 1) * HDIM)).astype(BF16)


def halves(values):
    high = values.astype(BF16)
    return high, (values - high.astype(F32)).astype(BF16)


def spread(values, matrix):
    high, low = halves(values)
    return jnp.dot(high, matrix, preferred_element_type=F32) + jnp.dot(low, matrix, preferred_element_type=F32)


def silu(values):
    half = 0.5 * values
    return half + half * jnp.tanh(half)


def softplus(values):
    small = jnp.exp(-jnp.abs(values))
    return jnp.maximum(values, 0.0) + jnp.log1p(small)


def half_mix(which, normed, scales, b_t, mix_weight, conv_weight, conv_bias, x_out):
    half = E // 2
    matrix = spread_matrix()
    states = []
    chunk = 256
    spans = [
        pl.ds(pl.multiple_of(which * half + first, 128), chunk) for first in range(0, half, chunk)
    ]
    wanted = jnp.where(which == 0, matrix[:, :half].astype(F32), matrix[:, half:].astype(F32)).astype(BF16)
    ahead = project(normed, mix_weight, spans[0])
    for place, lanes in enumerate(spans):
        raw = ahead
        if place + 1 < len(spans):
            ahead = project(normed, mix_weight, spans[place + 1])
        part = mixed(raw, conv_weight[:, lanes], conv_bias[:, lanes])
        local = slice(place * chunk, (place + 1) * chunk)
        x_out[:, local] = part
        to_end = jnp.dot(scales, wanted[:, local], preferred_element_type=F32)
        scaled = (part.astype(F32) * to_end).astype(BF16)
        states.append(jnp.dot(b_t, scaled, preferred_element_type=F32))
    return jnp.concatenate(states, axis=1)


def project(normed, mix_weight, lanes):
    return jnp.dot(normed, mix_weight[:, lanes], preferred_element_type=F32).astype(BF16)


def mixed(raw, weight, bias):
    raw = raw.astype(F32)
    total = weight[0:1] * raw
    for tap in range(1, weight.shape[0]):
        total = pltpu.roll(total, 1, 0) + weight[tap : tap + 1] * raw
    return silu(total[:-LEAD] + bias).astype(BF16)


def mix_kernel(
    embedded, norm_gain, mix_weight, step_weight, step_bias, log_rate, conv_weight, conv_bias,
    normed_out, x_out, b_out, c_out, b_t_out, step_out, cum_out, scales_out, decay_out, send_out,
):
    col, row = lax.axis_index("cols"), lax.axis_index("rows")
    resid = embedded[...].astype(F32)
    mean_sq = jnp.mean(resid * resid, axis=-1, keepdims=True)
    normed_f = resid * lax.rsqrt(mean_sq + 1e-05) * norm_gain[...]
    rows = lax.broadcasted_iota(jnp.int32, normed_f.shape, 0)
    blank = (rows >= embedded.shape[0] - LEAD) & (col == 0) & (row == 0)
    normed = jnp.where(blank, 0.0, normed_f).astype(BF16)
    normed_out[...] = normed
    length = embedded.shape[0] - LEAD
    maps_raw = project(normed, mix_weight, slice(E, E + 2 * NSTATE))
    step_raw = lax.dot_general(
        normed, step_weight[...], (((1,), (1,)), ((), ())), preferred_element_type=F32
    )[:-LEAD]
    step = softplus(step_raw + step_bias[...])
    log_decay = -step * jnp.exp(log_rate[...])
    lower = (
        lax.broadcasted_iota(jnp.int32, (length, length), 0) >= lax.broadcasted_iota(jnp.int32, (length, length), 1)
    ).astype(BF16)
    high = log_decay.astype(BF16)
    middle = (log_decay - high.astype(F32)).astype(BF16)
    low = (log_decay - high.astype(F32) - middle.astype(F32)).astype(BF16)
    cum = jnp.dot(lower, high, preferred_element_type=F32)
    cum = cum + jnp.dot(lower, middle, preferred_element_type=F32)
    cum = cum + jnp.dot(lower, low, preferred_element_type=F32)
    step_out[...] = step
    cum_out[...] = cum
    last = cum[length - 1 :]
    scales = (jnp.exp(last - cum) * step).astype(BF16)
    scales_out[...] = scales
    decay = spread(jnp.broadcast_to(jnp.exp(last), (8, HEADS)), spread_matrix())
    maps = mixed(maps_raw, conv_weight[:, E:], conv_bias[:, E:]).astype(F32)
    b_out[...] = maps[:, :NSTATE].astype(BF16)
    c_out[...] = maps[:, NSTATE:].astype(BF16)
    b_t = maps.T[:NSTATE].astype(BF16)
    b_t_out[...] = b_t
    state = half_mix(1 - row, normed, scales, b_t, mix_weight, conv_weight, conv_bias, x_out)
    half = E // 2
    first = row == 0
    decay_out[...] = jnp.where(first, decay[:, :half], decay[:, half:])
    send_out[...] = wire(state, jnp.where(first, decay[:, half:], decay[:, :half]))


def rest_kernel(normed, scales, b_t, mix_weight, conv_weight, conv_bias, decay, x_out, keep_out):
    keep_out[0:NSTATE, :] = half_mix(
        lax.axis_index("rows"), normed[...], scales[...], b_t[...], mix_weight, conv_weight, conv_bias, x_out
    )
    keep_out[NSTATE : NSTATE + 8, :] = decay[...]


def wire(values, decay):
    high = decay.astype(BF16).astype(F32)
    rest = decay - high
    place = lax.broadcasted_iota(jnp.int32, decay.shape, 0)
    return jnp.concatenate([values, jnp.where(place == 0, high, rest)], axis=0).astype(BF16)


def unwire(message):
    values = message[0:NSTATE, :].astype(F32)
    rows = message[NSTATE : NSTATE + 8, :].astype(F32)
    return values, jnp.broadcast_to(rows[0:1] + rows[1:2], rows.shape)


def product(factors):
    total = factors[0]
    for factor in factors[1:]:
        total = total * factor
    return total


def folded(place, pieces):
    places = [place ^ step for step in range(len(pieces))]
    steps = range(len(pieces))
    one = jnp.ones_like(pieces[0][1])
    all_values, ahead_values = None, None
    for step in steps:
        after = [jnp.where(places[k] > places[step], pieces[k][1], one) for k in steps if k != step]
        between = [
            jnp.where((places[k] > places[step]) & (places[k] < place), pieces[k][1], one)
            for k in steps
            if k not in (0, step)
        ]
        term = product(after)[0:1] * pieces[step][0]
        all_values = term if step == 0 else all_values + term
        if step:
            weight = jnp.where(places[step] < place, product([one, *between]), 0.0)
            term = weight[0:1] * pieces[step][0]
            ahead_values = term if ahead_values is None else ahead_values + term
    all_decay = product([decay for _, decay in pieces])
    ahead_decay = product([jnp.where(places[k] < place, pieces[k][1], one) for k in steps if k])
    return (all_values, all_decay), (ahead_values, ahead_decay)


def read(summary):
    return summary[0:NSTATE, :], summary[NSTATE : NSTATE + 8, :]


def write(summary, piece):
    summary[0:NSTATE, :] = piece[0]
    summary[NSTATE : NSTATE + 8, :] = piece[1]


def chained(earlier, latter):
    return latter[1][0:1] * earlier[0] + latter[0], earlier[1] * latter[1]


def pair_kernel(keep, received, total_out, message_out):
    total, _ = folded(lax.axis_index("rows"), [read(keep), unwire(received)])
    write(total_out, total)
    message_out[...] = wire(*total)


def join_kernel(low, count, first, *refs):
    refs = list(refs)
    total = read(refs.pop(0))
    before = None if first else read(refs.pop(0))
    pieces = [total] + [unwire(refs.pop(0)) for _ in range(count - 1)]
    place = (lax.axis_index("cols") // low) & (count - 1)
    total, ahead = folded(place, pieces)
    before_out, message_out = refs[:2]
    write(before_out, ahead if first else chained(ahead, before))
    message_out[...] = wire(*total)
    write(refs[2], total)


def enter_kernel(low, count, first, *refs):
    refs = list(refs)
    total = read(refs.pop(0))
    before = None if first else read(refs.pop(0))
    pieces = [total] + [unwire(refs.pop(0)) for _ in range(count - 1)]
    keep, received, mine_out, theirs_out = refs
    _, ahead = folded((lax.axis_index("cols") // low) & (count - 1), pieces)
    if not first:
        ahead = chained(ahead, before)
    own, other = read(keep), unwire(received)
    upper = lax.axis_index("rows") == 1
    low_piece = tuple(jnp.where(upper, b, a) for a, b in zip(own, other))
    second = chained(ahead, low_piece)[0]
    mine_out[...] = jnp.where(upper, second, ahead[0]).astype(BF16)
    theirs_out[...] = jnp.where(upper, ahead[0], second).astype(BF16)


def gate_kernel(normed, gate_weight, local_mine, local_theirs, cum, own_out, factor_out):
    gate = jnp.dot(normed[...], gate_weight[...], preferred_element_type=F32)[:-LEAD].astype(BF16).astype(F32)
    gate = silu(gate)
    half = local_mine.shape[1]
    upper = lax.axis_index("rows") == 1
    own_out[:, :half] = jnp.where(upper, local_theirs[...], local_mine[...]) * gate[:, :half]
    own_out[:, half:] = jnp.where(upper, local_mine[...], local_theirs[...]) * gate[:, half:]
    factor_out[...] = spread(jnp.exp(cum[...]), spread_matrix()) * gate


def intra_kernel(flip, skip, x, b_mat, c_mat, step, cum, out):
    row = lax.axis_index("rows")
    which = 1 - row if flip else row
    heads = HEADS // 2
    upper = which == 1
    length = x.shape[0]
    half = length // 2
    scores = lax.dot_general(c_mat[...], b_mat[...], (((1,), (1,)), ((), ())), preferred_element_type=F32)
    causal = lax.broadcasted_iota(jnp.int32, (length, length), 0) >= lax.broadcasted_iota(
        jnp.int32, (length, length), 1
    )
    scores = jnp.where(causal, scores, 0.0)
    wide = jnp.zeros((length, 128 - heads), F32)
    cum_v = jnp.where(upper, cum[:, heads:], cum[:, :heads])
    cum_t = jnp.concatenate([cum_v, wide], axis=1).T
    step_t = jnp.concatenate([jnp.where(upper, step[:, heads:], step[:, :heads]), wide], axis=1).T
    for place in range(out.shape[1] // 128):
        pair = place
        x_pair = x[:, pair * 128 : (pair + 1) * 128]
        tops, bottoms = [], []
        for member in range(2):
            head = 2 * pair + member
            column = cum_v[:, head : head + 1]
            cum_row = cum_t[head : head + 1, :]
            step_row = step_t[head : head + 1, :]

            def weights(rows, span):
                gap = jnp.minimum(column[rows] - cum_row[:, span], 0.0)
                return (scores[rows, span] * jnp.exp(gap) * step_row[:, span]).astype(BF16)

            inputs = x_pair[:, member * HDIM : (member + 1) * HDIM]
            top = jnp.dot(weights(slice(0, half), slice(0, half)), inputs[:half], preferred_element_type=F32)
            bottom = jnp.dot(weights(slice(half, length), slice(0, length)), inputs, preferred_element_type=F32)
            tops.append(top)
            bottoms.append(bottom)
        lane = lax.broadcasted_iota(jnp.int32, x_pair.shape, 1)
        base = which * heads + 2 * pair
        direct = jnp.where(lane < HDIM, skip[base], skip[base + 1]) * x_pair.astype(F32)
        lanes = slice(place * 128, (place + 1) * 128)
        out[0:half, lanes] = jnp.concatenate(tops, axis=1) + direct[:half]
        out[half:length, lanes] = jnp.concatenate(bottoms, axis=1) + direct[half:]


def half_product(which, state, own, factor, c_mat, out_gain, out_weight):
    half = own.shape[1] // 2
    lanes = pl.ds(pl.multiple_of(which * half, 128), half)
    carried = jnp.dot(c_mat[...], state[...], preferred_element_type=F32)
    gated = own[:, lanes] + carried * factor[:, lanes]
    squares = jnp.sum(gated * gated, axis=-1, keepdims=True)
    hidden = (gated * out_gain[:, lanes]).astype(BF16)
    return jnp.dot(hidden, out_weight[lanes, :], preferred_element_type=F32), squares


def first_kernel(mine, own, factor, c_mat, out_gain, out_weight, product_out, squares_out):
    product, squares = half_product(
        lax.axis_index("rows"), mine, own, factor, c_mat, out_gain, out_weight
    )
    product_out[...] = product
    squares_out[...] = jnp.broadcast_to(squares, squares_out.shape)


def finish_kernel(theirs, own, factor, c_mat, out_gain, out_weight, product, squares, embedded, out):
    rest, more = half_product(
        1 - lax.axis_index("rows"), theirs, own, factor, c_mat, out_gain, out_weight
    )
    mean_sq = (squares[:, 0:1] + more) / own.shape[1]
    result = (product[...] + rest) * lax.rsqrt(mean_sq + 1e-05)
    out[...] = (result + embedded[...].astype(F32)[:-LEAD]).astype(BF16)


def swap(block, axis, bit):
    return lax.ppermute(block, axis, [(i, i ^ bit) for i in range(lax.axis_size(axis))])


def sending_order(side):
    return (*range(side // 2, side), *reversed(range(side // 2)))


def across(block, step):
    side = lax.axis_size("cols") // 2
    pairs = []
    for col in range(2 * side):
        for row in range(2):
            other = side * row + ((col % side) ^ step)
            pairs.append((2 * col + row, 2 * other + col // side))
    return lax.ppermute(block, ("cols", "rows"), pairs)


def embed_by_rows(pixels, patch_weight, patch_bias):
    col_count = lax.axis_size("cols")
    side = col_count // 2
    width = pixels.shape[2]
    partner = swap(pixels, "rows", 1)
    pixels = call(stage_kernel, (pixels,), shape(pixels.shape))
    block = shape((5 * KERNEL + 8, width))
    scratch = [pltpu.VMEM((CHAN, 2 * pixels.shape[1] + 64, width), BF16)]
    blocks = call(pack_kernel, (pixels, partner), [block] * side, scratch, limit=8)
    near, far = [None] * side, [None] * side
    for step in sending_order(side):
        near[step] = across(blocks[step], step)
        far[step] = swap(near[step], "rows", 1)
    weight = patch_weight.reshape(3, 8, KERNEL, CHAN, D).transpose(2, 0, 3, 1, 4).reshape(KERNEL, WIN, D)
    weight = jnp.pad(weight, ((0, 0), (0, 128 - WIN), (0, 0))).reshape(KERNEL * 128, D)
    tokens = col_count * width // PATCH
    half = tokens // 2
    line = patch_bias.reshape(1, -1)
    slots = len(neighbours())

    def scratch(rows, reach):
        return [pltpu.VMEM((rows, KERNEL * 128), BF16), pltpu.VMEM((slots, reach + 2 * LEAD, 128), F32)]

    own = call(
        own_kernel, (*near, weight, line), shape((half, D)), scratch(half, half),
        flops=tokens * KERNEL * 128 * D, moved=6 << 20, limit=16,
    )
    return call(
        rest_of_row_kernel, (*near, *far, weight, line, own), shape((tokens + LEAD, D)),
        [*scratch(half + 16 + LEAD, half + 16), pltpu.VMEM((PATCH, 24, 128), F32)],
        flops=tokens * KERNEL * 128 * D, moved=6 << 20, limit=16,
    )


def extended(block, sides, width):
    for axis, dim in sides:
        count = lax.axis_size(axis)
        forward = [(i, i + 1) for i in range(count - 1)]
        backward = [(target, source) for source, target in forward]
        low = lax.ppermute(
            lax.slice_in_dim(block, block.shape[dim] - width, None, axis=dim), axis, forward
        )
        high = lax.ppermute(lax.slice_in_dim(block, 0, width, axis=dim), axis, backward)
        block = jnp.concatenate([low, block, high], axis=dim)
    return block


def shifted(block, axis, distance):
    devices = range(lax.axis_size(axis))
    route = [(i - distance, i) for i in devices if i - distance in devices]
    return lax.ppermute(block, axis, route)


def embed_by_blocks(pixels, patch_weight, patch_bias):
    padded = extended(pixels, (("cols", 2), ("rows", 1)), MARGIN)
    embed_grid = lax.conv_general_dilated(
        padded[None],
        patch_weight,
        (PATCH, PATCH),
        "VALID",
        dimension_numbers=("NCHW", "HWIO", "NHWC"),
        preferred_element_type=jnp.float32,
    )[0]
    embed_grid = (embed_grid + patch_bias).astype(jnp.bfloat16)
    row_local, col_local, feature_width = embed_grid.shape
    devices = lax.axis_size(("cols", "rows"))
    row_count = lax.axis_size("rows")
    col_count = lax.axis_size("cols")
    groups = col_count // row_local
    piece_len = col_local * feature_width // devices
    outgoing = embed_grid.reshape(row_local, devices, piece_len)
    spread = lax.all_to_all(outgoing, ("cols", "rows"), split_axis=1, concat_axis=1, tiled=True)
    spread = spread.reshape(row_local, groups, row_local, row_count, piece_len).transpose(
        3, 0, 1, 2, 4
    )
    landed = lax.all_to_all(
        spread.reshape(devices, row_local, piece_len),
        ("cols", "rows"),
        split_axis=0,
        concat_axis=0,
        tiled=True,
    )
    tokens = landed.transpose(1, 0, 2).reshape(row_local * col_local, feature_width)
    tail = shifted(tokens[tokens.shape[0] - LEAD :], ("cols", "rows"), 1)
    return jnp.concatenate([tokens, tail], axis=0)


def body(
    pixels,
    patch_weight,
    patch_bias,
    norm_gain,
    gate_weight,
    mix_weight,
    step_weight,
    step_bias,
    log_rate,
    conv_weight,
    conv_bias,
    skip_gain,
    out_gain,
    out_weight,
):
    col_count = lax.axis_size("cols")
    row_local = pixels.shape[1] // PATCH
    if col_count == row_local and lax.axis_size("rows") == 2:
        embedded = embed_by_rows(pixels, patch_weight, patch_bias)
    else:
        embedded = embed_by_blocks(pixels, patch_weight, patch_bias)
    length = embedded.shape[0] - LEAD
    line = lambda a: a.reshape(1, -1)
    mixed_width = mix_weight.shape[1]
    half = E // 2
    packed = NSTATE + 8
    conv = (conv_weight, line(conv_bias))
    normed, x_theirs, b_mat, c_mat, b_t, step, cum, scales, decay, send = call(
        mix_kernel,
        (embedded, line(norm_gain), mix_weight, step_weight.T, line(step_bias), line(log_rate), *conv),
        [
            shape((LEAD + length, D)), shape((length, half)), shape((length, NSTATE)), shape((length, NSTATE)),
            shape((NSTATE, length)), shape((length, HEADS), F32), shape((length, HEADS), F32),
            shape((length, HEADS)), shape((8, half), F32), shape((packed, half)),
        ],
        flops=length * D * mixed_width, moved=4 << 20, limit=16,
    )
    came = swap(send, "rows", 1)
    summary, message = shape((packed, half), F32), shape((packed, half))
    x_mine, keep = call(
        rest_kernel, (normed, scales, b_t, mix_weight, *conv, decay), [shape((length, half)), summary],
        flops=length * D * mixed_width, moved=4 << 20, limit=16,
    )
    total, out = call(pair_kernel, (keep, came), [summary, message])
    locals_ = []
    for part in range(2):
        locals_.append(
            call(
                partial(intra_kernel, bool(part)), (skip_gain, (x_mine, x_theirs)[part], b_mat, c_mat, step, cum),
                shape((length, half), F32), scalars=1,
                flops=HEADS * length * length * 128, moved=2 << 20, limit=8,
            )
        )
    own, factor = call(
        gate_kernel, (normed, gate_weight, *locals_, cum), [shape((length, E), F32)] * 2,
        flops=2 * length * D * E, moved=4 << 20, limit=8,
    )
    groups, low = [], 1
    while low < col_count:
        count = min(4, col_count // low)
        groups.append((low, count))
        low *= count
    before = None
    for number, (low, count) in enumerate(groups):
        ending = number + 1 == len(groups)
        arrived = []
        for hop in range(1, count):
            arrived.append(swap(out, "cols", hop * low))
        first = before is None
        inputs = ([total] if first else [total, before]) + arrived
        if ending:
            entering = shape((NSTATE, half))
            mine, theirs = call(partial(enter_kernel, low, count, first), (*inputs, keep, came), [entering, entering])
        else:
            before, out, total = call(partial(join_kernel, low, count, first), inputs, [summary, message, summary])
    theirs = swap(theirs, "rows", 1)
    common = (own, factor, c_mat, line(out_gain), out_weight)
    partial_sum, squares = call(
        first_kernel, (mine, *common), [shape((length, D), F32), shape((length, 128), F32)],
        flops=length * D * E, moved=4 << 20, limit=8,
    )
    return call(
        finish_kernel, (theirs, *common, partial_sum, squares, embedded), shape((length, D)),
        flops=length * D * E, moved=4 << 20, limit=8,
    )


def solution(mesh):
    placed = (
        P(None, "rows", ("slides", "cols")),
        P(),
        P(),
        P(),
        P(),
        P(),
        P(),
        P(),
        P(),
        P(),
        P(),
        P(),
        P(),
        P(),
    )
    return jax.shard_map(
        body,
        mesh=mesh,
        in_specs=placed,
        out_specs=P(("slides", "cols", "rows"), None),
        check_vma=False,
    )
```

```python
from functools import partial

import jax
import jax.numpy as jnp
from jax import lax
from jax.experimental import pallas as pl
from jax.experimental.pallas import tpu as pltpu
from jax.sharding import PartitionSpec as P


E = 1536
D = 768
HDIM = 64
NSTATE = 64
PATCH = 16
KERNEL = 24
HEADS = 24
CHAN = 3
MARGIN = (KERNEL - PATCH) // 2
WIN = CHAN * KERNEL
LEAD = 8
F32 = jnp.float32
BF16 = jnp.bfloat16


def vmem():
    return pl.BlockSpec(memory_space=pltpu.VMEM)


def call(kernel, inputs, outs, scratch=(), limit=4, flops=0, moved=0, scalars=0, outside=False):
    return pl.pallas_call(
        kernel,
        out_shape=outs,
        in_specs=[pl.BlockSpec(memory_space=pltpu.SMEM)] * scalars + [vmem()] * (len(inputs) - scalars),
        out_specs=jax.tree.map(lambda _: pl.BlockSpec(memory_space=pl.ANY) if outside else vmem(), outs),
        scratch_shapes=scratch,
        compiler_params=pltpu.CompilerParams(vmem_limit_bytes=limit << 20),
        cost_estimate=pl.CostEstimate(flops=flops, bytes_accessed=moved, transcendentals=0),
    )(*inputs)


def shape(dims, kind=BF16):
    return jax.ShapeDtypeStruct(dims, kind)


def pack_kernel(own, partner, *refs):
    outs, rows = refs[:-1], refs[-1]
    col, row = lax.axis_index("cols"), lax.axis_index("rows")
    local = own.shape[1]
    width = own.shape[2]
    edge = jnp.zeros((CHAN, 32, width), BF16)
    rows[:, 0:32, :] = edge
    rows[:, 32 + 2 * local : 64 + 2 * local, :] = edge
    rows[:, pl.ds(pl.multiple_of(32 + local * row, 32), local), :] = own[...]
    rows[:, pl.ds(pl.multiple_of(32 + local * (1 - row), 32), local), :] = partner[...]
    side = len(outs)
    for step, out in enumerate(outs):
        chip = side * row + ((col % side) ^ step)
        first = pl.multiple_of(2 * PATCH * chip, 32)
        blocks = [rows[channel, pl.ds(first, 80), :].astype(F32) for channel in range(CHAN)]
        pieces = [block[28 + 8 * group : 36 + 8 * group] for group in range(5) for block in blocks]
        tails = [block[12 + 8 * group : 20 + 8 * group, width - 64 :] for group in range(2) for block in blocks]
        tails.append(jnp.zeros((8, width - 64 * len(tails)), F32))
        out[...] = jnp.concatenate([*pieces, jnp.concatenate(tails, axis=1)], axis=0).astype(BF16)


def stage_kernel(pixels, out):
    out[...] = pixels[...]


def pick_matrix():
    row = lax.broadcasted_iota(jnp.int32, (256, 256), 0)
    pixel = lax.broadcasted_iota(jnp.int32, (256, 256), 1)
    return (pixel == (row & 15) * PATCH + (row >> 4)).astype(BF16)


def turned(pick, values):
    return lax.dot_general(pick, values, (((1,), (1,)), ((), ())), preferred_element_type=F32)


def window_pixel(offset):
    place = offset - MARGIN + PATCH
    return place % PATCH, place // PATCH - 1


def neighbours():
    return [offset for offset in range(KERNEL) if window_pixel(offset)[1]]


def place_tokens(pick, values, first, wide, beside):
    found = turned(pick, values).reshape(PATCH, 16, 128)
    rounded = found.astype(BF16)
    for offset in range(KERNEL):
        pixel, shift = window_pixel(offset)
        if shift == 0:
            wide[pl.ds(first, 16), offset * 128 : (offset + 1) * 128] = rounded[pixel]
    for slot, offset in enumerate(neighbours()):
        beside[slot, pl.ds(pl.multiple_of(LEAD + first, 8), 16), :] = found[window_pixel(offset)[0]]


def place_beside(count, first, wide, beside):
    for slot, offset in enumerate(neighbours()):
        start = LEAD + window_pixel(offset)[1]
        part = beside[slot, start : start + count, :]
        wide[first : first + count, offset * 128 : (offset + 1) * 128] = part.astype(BF16)


def clear_ends(count, beside):
    zeros = jnp.zeros((beside.shape[0], LEAD, 128), F32)
    beside[:, 0:LEAD, :] = zeros
    beside[:, LEAD + count : LEAD + count + LEAD, :] = zeros


def windows_of(block, row, lanes):
    window = pl.ds(pl.multiple_of(2 * KERNEL * row, 16), WIN)
    values = block[window, lanes]
    return jnp.concatenate([values, jnp.zeros((128 - WIN, values.shape[1]), BF16)], axis=0)


def embed_kernel(*refs):
    blocks, (weight, bias, out, wide, beside, tail) = refs[:-6], refs[-6:]
    col, row = lax.axis_index("cols"), lax.axis_index("rows")
    count = len(blocks)
    side = count // 2
    width = blocks[0].shape[1]
    tokens = count * width // PATCH
    pick = pick_matrix()
    clear_ends(tokens, beside)
    edge = jnp.zeros((WIN, 128), F32)
    extra = jnp.zeros((8, 128 * CHAN), F32)
    for place, block in enumerate(blocks):
        source = side * (row if place < side else 1 - row) + ((col % side) ^ (place % side))
        for group in range(width // 256):
            first = pl.multiple_of(source * (width // PATCH) + 16 * group, 16)
            place_tokens(pick, windows_of(block, row, slice(256 * group, 256 * (group + 1))), first, wide, beside)
        last = source == count - 1
        edge = jnp.where(last, block[0:WIN, width - 128 :].astype(F32), edge)
        extra = jnp.where(last, block[5 * KERNEL - 8 : 5 * KERNEL + 8, : 128 * CHAN].astype(F32)[8:], extra)
    before = [extra[:, 64 * piece : 64 * (piece + 1)] for piece in range(2 * CHAN)] + [edge[:KERNEL, 64:]]
    last = jnp.where(row == 0, jnp.concatenate(before, axis=0), edge[:, 64:])
    last = jnp.concatenate([last, jnp.zeros((128 - WIN, 64), F32)], axis=0)
    last = jnp.concatenate([jnp.zeros((128, 64), F32), last, jnp.zeros((128, 128), F32)], axis=1)
    tail[:, 0:8, :] = jnp.zeros((PATCH, 8, 128), F32)
    tail[:, 8:24, :] = turned(pick, last.astype(BF16)).reshape(PATCH, 16, 128)
    for offset in range(KERNEL):
        pixel, shift = window_pixel(offset)
        part = tail[pixel, 8 + shift : 16 + shift, :]
        wide[tokens:, offset * 128 : (offset + 1) * 128] = part.astype(BF16)
    place_beside(tokens, 0, wide, beside)
    grid = jnp.dot(wide[...], weight[...], preferred_element_type=F32)
    out[...] = (grid + bias[...]).astype(BF16)


def spread_matrix():
    head = lax.broadcasted_iota(jnp.int32, (HEADS, E), 0)
    lane = lax.broadcasted_iota(jnp.int32, (HEADS, E), 1)
    return ((lane >= head * HDIM) & (lane < (head + 1) * HDIM)).astype(BF16)


def halves(values):
    high = values.astype(BF16)
    return high, (values - high.astype(F32)).astype(BF16)


def spread(values, matrix):
    high, low = halves(values)
    return jnp.dot(high, matrix, preferred_element_type=F32) + jnp.dot(low, matrix, preferred_element_type=F32)


def silu(values):
    half = 0.5 * values
    return half + half * jnp.tanh(half)


def softplus(values):
    small = jnp.exp(-jnp.abs(values))
    return jnp.maximum(values, 0.0) + jnp.log1p(small)


def half_mix(which, normed, scales, b_t, mix_weight, conv_weight, conv_bias, x_out):
    half = E // 2
    matrix = spread_matrix()
    states = []
    chunk = 256
    spans = [
        pl.ds(pl.multiple_of(which * half + first, 128), chunk) for first in range(0, half, chunk)
    ]
    wanted = jnp.where(which == 0, matrix[:, :half].astype(F32), matrix[:, half:].astype(F32)).astype(BF16)
    ahead = project(normed, mix_weight, spans[0])
    for place, lanes in enumerate(spans):
        raw = ahead
        if place + 1 < len(spans):
            ahead = project(normed, mix_weight, spans[place + 1])
        part = mixed(raw, conv_weight[:, lanes], conv_bias[:, lanes])
        local = slice(place * chunk, (place + 1) * chunk)
        x_out[:, local] = part
        to_end = jnp.dot(scales, wanted[:, local], preferred_element_type=F32)
        scaled = (part.astype(F32) * to_end).astype(BF16)
        states.append(jnp.dot(b_t, scaled, preferred_element_type=F32))
    return jnp.concatenate(states, axis=1)


def project(normed, mix_weight, lanes):
    return jnp.dot(normed, mix_weight[:, lanes], preferred_element_type=F32).astype(BF16)


def mixed(raw, weight, bias):
    raw = raw.astype(F32)
    total = weight[0:1] * raw
    for tap in range(1, weight.shape[0]):
        total = pltpu.roll(total, 1, 0) + weight[tap : tap + 1] * raw
    return silu(total[:-LEAD] + bias).astype(BF16)


def mix_kernel(
    embedded, norm_gain, mix_weight, step_weight, step_bias, log_rate, conv_weight, conv_bias,
    normed_out, x_out, b_out, c_out, b_t_out, step_out, cum_out, scales_out, decay_out, send_out,
):
    col, row = lax.axis_index("cols"), lax.axis_index("rows")
    resid = embedded[...].astype(F32)
    mean_sq = jnp.mean(resid * resid, axis=-1, keepdims=True)
    normed_f = resid * lax.rsqrt(mean_sq + 1e-05) * norm_gain[...]
    rows = lax.broadcasted_iota(jnp.int32, normed_f.shape, 0)
    blank = (rows >= embedded.shape[0] - LEAD) & (col == 0) & (row == 0)
    normed = jnp.where(blank, 0.0, normed_f).astype(BF16)
    normed_out[...] = normed
    length = embedded.shape[0] - LEAD
    maps_raw = project(normed, mix_weight, slice(E, E + 2 * NSTATE))
    step_raw = lax.dot_general(
        normed, step_weight[...], (((1,), (1,)), ((), ())), preferred_element_type=F32
    )[:-LEAD]
    step = softplus(step_raw + step_bias[...])
    log_decay = -step * jnp.exp(log_rate[...])
    lower = (
        lax.broadcasted_iota(jnp.int32, (length, length), 0) >= lax.broadcasted_iota(jnp.int32, (length, length), 1)
    ).astype(BF16)
    high = log_decay.astype(BF16)
    middle = (log_decay - high.astype(F32)).astype(BF16)
    low = (log_decay - high.astype(F32) - middle.astype(F32)).astype(BF16)
    cum = jnp.dot(lower, high, preferred_element_type=F32)
    cum = cum + jnp.dot(lower, middle, preferred_element_type=F32)
    cum = cum + jnp.dot(lower, low, preferred_element_type=F32)
    step_out[...] = step
    cum_out[...] = cum
    last = cum[length - 1 :]
    scales = (jnp.exp(last - cum) * step).astype(BF16)
    scales_out[...] = scales
    decay = spread(jnp.broadcast_to(jnp.exp(last), (8, HEADS)), spread_matrix())
    maps = mixed(maps_raw, conv_weight[:, E:], conv_bias[:, E:]).astype(F32)
    b_out[...] = maps[:, :NSTATE].astype(BF16)
    c_out[...] = maps[:, NSTATE:].astype(BF16)
    b_t = maps.T[:NSTATE].astype(BF16)
    b_t_out[...] = b_t
    state = half_mix(1 - row, normed, scales, b_t, mix_weight, conv_weight, conv_bias, x_out)
    half = E // 2
    first = row == 0
    decay_out[...] = jnp.where(first, decay[:, :half], decay[:, half:])
    send_out[...] = wire(state, jnp.where(first, decay[:, half:], decay[:, :half]))


def rest_kernel(normed, scales, b_t, mix_weight, conv_weight, conv_bias, decay, x_out, keep_out):
    keep_out[0:NSTATE, :] = half_mix(
        lax.axis_index("rows"), normed[...], scales[...], b_t[...], mix_weight, conv_weight, conv_bias, x_out
    )
    keep_out[NSTATE : NSTATE + 8, :] = decay[...]


TILES = E // 2 // 128
MESSAGE = (TILES * NSTATE + 16, 128)


def wire(values, decay):
    high = decay.astype(BF16).astype(F32)
    place = lax.broadcasted_iota(jnp.int32, (8, 128), 0)
    rows = [jnp.zeros((8, 128), F32)] * 2
    for tile in range(TILES):
        lanes = slice(128 * tile, 128 * (tile + 1))
        for part, piece in enumerate((high, decay - high)):
            rows[part] = jnp.where(place == tile, piece[:, lanes], rows[part])
    columns = [values[:, 128 * tile : 128 * (tile + 1)] for tile in range(TILES)]
    return jnp.concatenate([*columns, *rows], axis=0).astype(BF16)


def unwire(message):
    columns = [message[NSTATE * tile : NSTATE * (tile + 1), :].astype(F32) for tile in range(TILES)]
    rows = message[TILES * NSTATE :, :].astype(F32)
    decay = rows[:8] + rows[8:]
    decays = [jnp.broadcast_to(decay[tile : tile + 1], (8, 128)) for tile in range(TILES)]
    return jnp.concatenate(columns, axis=1), jnp.concatenate(decays, axis=1)


def product(factors):
    total = factors[0]
    for factor in factors[1:]:
        total = total * factor
    return total


def folded(place, pieces):
    places = [place ^ step for step in range(len(pieces))]
    steps = range(len(pieces))
    one = jnp.ones_like(pieces[0][1])
    all_values, ahead_values = None, None
    for step in steps:
        after = [jnp.where(places[k] > places[step], pieces[k][1], one) for k in steps if k != step]
        between = [
            jnp.where((places[k] > places[step]) & (places[k] < place), pieces[k][1], one)
            for k in steps
            if k not in (0, step)
        ]
        term = product(after)[0:1] * pieces[step][0]
        all_values = term if step == 0 else all_values + term
        if step:
            weight = jnp.where(places[step] < place, product([one, *between]), 0.0)
            term = weight[0:1] * pieces[step][0]
            ahead_values = term if ahead_values is None else ahead_values + term
    all_decay = product([decay for _, decay in pieces])
    ahead_decay = product([jnp.where(places[k] < place, pieces[k][1], one) for k in steps if k])
    return (all_values, all_decay), (ahead_values, ahead_decay)


def read(summary):
    return summary[0:NSTATE, :], summary[NSTATE : NSTATE + 8, :]


def write(summary, piece):
    summary[0:NSTATE, :] = piece[0]
    summary[NSTATE : NSTATE + 8, :] = piece[1]


def chained(earlier, latter):
    return latter[1][0:1] * earlier[0] + latter[0], earlier[1] * latter[1]


def pair_kernel(keep, received, total_out, message_out):
    total, _ = folded(lax.axis_index("rows"), [read(keep), unwire(received)])
    write(total_out, total)
    message_out[...] = wire(*total)


def join_kernel(low, count, first, *refs):
    refs = list(refs)
    total = read(refs.pop(0))
    before = None if first else read(refs.pop(0))
    pieces = [total] + [unwire(refs.pop(0)) for _ in range(count - 1)]
    place = (lax.axis_index("cols") // low) & (count - 1)
    total, ahead = folded(place, pieces)
    before_out, message_out = refs[:2]
    write(before_out, ahead if first else chained(ahead, before))
    message_out[...] = wire(*total)
    write(refs[2], total)


def enter_kernel(low, count, first, *refs):
    refs = list(refs)
    total = read(refs.pop(0))
    before = None if first else read(refs.pop(0))
    pieces = [total] + [unwire(refs.pop(0)) for _ in range(count - 1)]
    keep, received, mine_out, theirs_out = refs
    _, ahead = folded((lax.axis_index("cols") // low) & (count - 1), pieces)
    if not first:
        ahead = chained(ahead, before)
    own, other = read(keep), unwire(received)
    upper = lax.axis_index("rows") == 1
    low_piece = tuple(jnp.where(upper, b, a) for a, b in zip(own, other))
    second = chained(ahead, low_piece)[0]
    mine_out[...] = jnp.where(upper, second, ahead[0]).astype(BF16)
    theirs_out[...] = jnp.where(upper, ahead[0], second).astype(BF16)


def gate_kernel(normed, gate_weight, local_mine, local_theirs, cum, own_out, factor_out):
    gate = jnp.dot(normed[...], gate_weight[...], preferred_element_type=F32)[:-LEAD].astype(BF16).astype(F32)
    gate = silu(gate)
    half = local_mine.shape[1]
    upper = lax.axis_index("rows") == 1
    own_out[:, :half] = jnp.where(upper, local_theirs[...], local_mine[...]) * gate[:, :half]
    own_out[:, half:] = jnp.where(upper, local_mine[...], local_theirs[...]) * gate[:, half:]
    factor_out[...] = spread(jnp.exp(cum[...]), spread_matrix()) * gate


def intra_kernel(flip, skip, x, b_mat, c_mat, step, cum, out):
    row = lax.axis_index("rows")
    which = 1 - row if flip else row
    heads = HEADS // 2
    upper = which == 1
    length = x.shape[0]
    half = length // 2
    scores = lax.dot_general(c_mat[...], b_mat[...], (((1,), (1,)), ((), ())), preferred_element_type=F32)
    causal = lax.broadcasted_iota(jnp.int32, (length, length), 0) >= lax.broadcasted_iota(
        jnp.int32, (length, length), 1
    )
    scores = jnp.where(causal, scores, 0.0)
    wide = jnp.zeros((length, 128 - heads), F32)
    cum_v = jnp.where(upper, cum[:, heads:], cum[:, :heads])
    cum_t = jnp.concatenate([cum_v, wide], axis=1).T
    step_t = jnp.concatenate([jnp.where(upper, step[:, heads:], step[:, :heads]), wide], axis=1).T
    for place in range(out.shape[1] // 128):
        pair = place
        lanes = slice(place * 128, (place + 1) * 128)
        x_pair = x[:, lanes].astype(F32)
        lane = lax.broadcasted_iota(jnp.int32, x_pair.shape, 1)
        top = bottom = None
        for member in range(2):
            head = 2 * pair + member
            column = cum_v[:, head : head + 1]
            cum_row = cum_t[head : head + 1, :]
            step_row = step_t[head : head + 1, :]

            def weights(rows, span):
                gap = jnp.minimum(column[rows] - cum_row[:, span], 0.0)
                return (scores[rows, span] * jnp.exp(gap) * step_row[:, span]).astype(BF16)

            inputs = jnp.where((lane < HDIM) == (member == 0), x_pair, 0.0).astype(BF16)
            upper_part = jnp.dot(
                weights(slice(0, half), slice(0, half)), inputs[:half], preferred_element_type=F32
            )
            lower_part = jnp.dot(
                weights(slice(half, length), slice(0, length)), inputs, preferred_element_type=F32
            )
            top = upper_part if top is None else top + upper_part
            bottom = lower_part if bottom is None else bottom + lower_part
        base = which * heads + 2 * pair
        direct = jnp.where(lane < HDIM, skip[base], skip[base + 1]) * x_pair
        out[0:half, lanes] = top + direct[:half]
        out[half:length, lanes] = bottom + direct[half:]


def half_hidden(lanes, state, own, factor, c_mat, out_gain):
    carried = jnp.dot(c_mat[...], state[...], preferred_element_type=F32)
    gated = own[:, lanes] + carried * factor[:, lanes]
    squares = jnp.sum(gated * gated, axis=-1, keepdims=True)
    return (gated * out_gain[:, lanes]).astype(BF16), squares


def first_kernel(mine, own, factor, c_mat, out_gain, out_weight, product_out, squares_out):
    half = own.shape[1] // 2
    lanes = pl.ds(pl.multiple_of(lax.axis_index("rows") * half, 128), half)
    hidden, squares = half_hidden(lanes, mine, own, factor, c_mat, out_gain)
    product = jnp.dot(hidden, out_weight[lanes, :], preferred_element_type=F32)
    product_out[...] = product
    squares_out[...] = jnp.broadcast_to(squares, squares_out.shape)


def finish_kernel(
    theirs, own, factor, c_mat, out_gain, out_weight, product, squares, embedded, out, result, sems
):
    which = 1 - lax.axis_index("rows")
    half = own.shape[1] // 2
    lanes = pl.ds(pl.multiple_of(which * half, 128), half)
    hidden, more = half_hidden(lanes, theirs, own, factor, c_mat, out_gain)
    scale = lax.rsqrt((squares[:, 0:1] + more) / own.shape[1] + 1e-05)
    chunk = result.shape[2]
    copies = []
    for place in range(result.shape[0]):
        span = slice(place * chunk, (place + 1) * chunk)
        rest = jnp.dot(hidden, out_weight[lanes, span], preferred_element_type=F32)
        resid = embedded[:, span].astype(F32)[:-LEAD]
        result[place] = ((product[:, span] + rest) * scale + resid).astype(BF16)
        copies.append(pltpu.make_async_copy(result.at[place], out.at[:, span], sems.at[place]))
        copies[-1].start()
    for copy in copies:
        copy.wait()


def swap(block, axis, bit):
    return lax.ppermute(block, axis, [(i, i ^ bit) for i in range(lax.axis_size(axis))])


def sending_order(side):
    return (*range(side // 2, side), *reversed(range(side // 2)))


def across(block, step):
    side = lax.axis_size("cols") // 2
    pairs = []
    for col in range(2 * side):
        for row in range(2):
            other = side * row + ((col % side) ^ step)
            pairs.append((2 * col + row, 2 * other + col // side))
    return lax.ppermute(block, ("cols", "rows"), pairs)


def embed_by_rows(pixels, patch_weight, patch_bias):
    col_count = lax.axis_size("cols")
    side = col_count // 2
    width = pixels.shape[2]
    partner = swap(pixels, "rows", 1)
    pixels = call(stage_kernel, (pixels,), shape(pixels.shape))
    block = shape((5 * KERNEL + 8, width))
    scratch = [pltpu.VMEM((CHAN, 2 * pixels.shape[1] + 64, width), BF16)]
    blocks = call(pack_kernel, (pixels, partner), [block] * side, scratch, limit=8)
    near, far = [None] * side, [None] * side
    for step in sending_order(side):
        near[step] = across(blocks[step], step)
        far[step] = swap(near[step], "rows", 1)
    came = near + far
    weight = patch_weight.reshape(3, 8, KERNEL, CHAN, D).transpose(2, 0, 3, 1, 4).reshape(KERNEL, WIN, D)
    weight = jnp.pad(weight, ((0, 0), (0, 128 - WIN), (0, 0))).reshape(KERNEL * 128, D)
    tokens = col_count * width // PATCH
    scratch = [
        pltpu.VMEM((tokens + LEAD, KERNEL * 128), BF16),
        pltpu.VMEM((len(neighbours()), tokens + 2 * LEAD, 128), F32),
        pltpu.VMEM((PATCH, 24, 128), F32),
    ]
    return call(
        embed_kernel, (*came, weight, patch_bias.reshape(1, -1)), shape((tokens + LEAD, D)), scratch,
        flops=2 * tokens * KERNEL * 128 * D, moved=6 << 20, limit=16,
    )


def extended(block, sides, width):
    for axis, dim in sides:
        count = lax.axis_size(axis)
        forward = [(i, i + 1) for i in range(count - 1)]
        backward = [(target, source) for source, target in forward]
        low = lax.ppermute(
            lax.slice_in_dim(block, block.shape[dim] - width, None, axis=dim), axis, forward
        )
        high = lax.ppermute(lax.slice_in_dim(block, 0, width, axis=dim), axis, backward)
        block = jnp.concatenate([low, block, high], axis=dim)
    return block


def shifted(block, axis, distance):
    devices = range(lax.axis_size(axis))
    route = [(i - distance, i) for i in devices if i - distance in devices]
    return lax.ppermute(block, axis, route)


def embed_by_blocks(pixels, patch_weight, patch_bias):
    padded = extended(pixels, (("cols", 2), ("rows", 1)), MARGIN)
    embed_grid = lax.conv_general_dilated(
        padded[None],
        patch_weight,
        (PATCH, PATCH),
        "VALID",
        dimension_numbers=("NCHW", "HWIO", "NHWC"),
        preferred_element_type=jnp.float32,
    )[0]
    embed_grid = (embed_grid + patch_bias).astype(jnp.bfloat16)
    row_local, col_local, feature_width = embed_grid.shape
    devices = lax.axis_size(("cols", "rows"))
    row_count = lax.axis_size("rows")
    col_count = lax.axis_size("cols")
    groups = col_count // row_local
    piece_len = col_local * feature_width // devices
    outgoing = embed_grid.reshape(row_local, devices, piece_len)
    spread = lax.all_to_all(outgoing, ("cols", "rows"), split_axis=1, concat_axis=1, tiled=True)
    spread = spread.reshape(row_local, groups, row_local, row_count, piece_len).transpose(
        3, 0, 1, 2, 4
    )
    landed = lax.all_to_all(
        spread.reshape(devices, row_local, piece_len),
        ("cols", "rows"),
        split_axis=0,
        concat_axis=0,
        tiled=True,
    )
    tokens = landed.transpose(1, 0, 2).reshape(row_local * col_local, feature_width)
    tail = shifted(tokens[tokens.shape[0] - LEAD :], ("cols", "rows"), 1)
    return jnp.concatenate([tokens, tail], axis=0)


def body(
    pixels,
    patch_weight,
    patch_bias,
    norm_gain,
    gate_weight,
    mix_weight,
    step_weight,
    step_bias,
    log_rate,
    conv_weight,
    conv_bias,
    skip_gain,
    out_gain,
    out_weight,
):
    col_count = lax.axis_size("cols")
    row_local = pixels.shape[1] // PATCH
    if col_count == row_local and lax.axis_size("rows") == 2:
        embedded = embed_by_rows(pixels, patch_weight, patch_bias)
    else:
        embedded = embed_by_blocks(pixels, patch_weight, patch_bias)
    length = embedded.shape[0] - LEAD
    line = lambda a: a.reshape(1, -1)
    mixed_width = mix_weight.shape[1]
    half = E // 2
    packed = NSTATE + 8
    conv = (conv_weight, line(conv_bias))
    normed, x_theirs, b_mat, c_mat, b_t, step, cum, scales, decay, send = call(
        mix_kernel,
        (embedded, line(norm_gain), mix_weight, step_weight.T, line(step_bias), line(log_rate), *conv),
        [
            shape((LEAD + length, D)), shape((length, half)), shape((length, NSTATE)), shape((length, NSTATE)),
            shape((NSTATE, length)), shape((length, HEADS), F32), shape((length, HEADS), F32),
            shape((length, HEADS)), shape((8, half), F32), shape(MESSAGE),
        ],
        flops=length * D * mixed_width, moved=4 << 20, limit=16,
    )
    came = swap(send, "rows", 1)
    summary, message = shape((packed, half), F32), shape(MESSAGE)
    x_mine, keep = call(
        rest_kernel, (normed, scales, b_t, mix_weight, *conv, decay), [shape((length, half)), summary],
        flops=length * D * mixed_width, moved=4 << 20, limit=16,
    )
    total, out = call(pair_kernel, (keep, came), [summary, message])
    locals_ = []
    for part in range(2):
        locals_.append(
            call(
                partial(intra_kernel, bool(part)), (skip_gain, (x_mine, x_theirs)[part], b_mat, c_mat, step, cum),
                shape((length, half), F32), scalars=1,
                flops=HEADS * length * length * 128, moved=2 << 20, limit=8,
            )
        )
    own, factor = call(
        gate_kernel, (normed, gate_weight, *locals_, cum), [shape((length, E), F32)] * 2,
        flops=2 * length * D * E, moved=4 << 20, limit=8,
    )
    groups, low = [], 1
    while low < col_count:
        count = min(4, col_count // low)
        groups.append((low, count))
        low *= count
    before = None
    for number, (low, count) in enumerate(groups):
        ending = number + 1 == len(groups)
        arrived = []
        for hop in range(1, count):
            arrived.append(swap(out, "cols", hop * low))
        first = before is None
        inputs = ([total] if first else [total, before]) + arrived
        if ending:
            entering = shape((NSTATE, half))
            mine, theirs = call(partial(enter_kernel, low, count, first), (*inputs, keep, came), [entering, entering])
        else:
            before, out, total = call(partial(join_kernel, low, count, first), inputs, [summary, message, summary])
    theirs = swap(theirs, "rows", 1)
    common = (own, factor, c_mat, line(out_gain), out_weight)
    partial_sum, squares = call(
        first_kernel, (mine, *common), [shape((length, D), F32), shape((length, 128), F32)],
        flops=length * D * E, moved=4 << 20, limit=8,
    )
    return call(
        finish_kernel, (theirs, *common, partial_sum, squares, embedded), shape((length, D)),
        [pltpu.VMEM((3, length, D // 3), BF16), pltpu.SemaphoreType.DMA((3,))],
        flops=length * D * E, moved=4 << 20, limit=8, outside=True,
    )


def solution(mesh):
    placed = (
        P(None, "rows", ("slides", "cols")),
        P(),
        P(),
        P(),
        P(),
        P(),
        P(),
        P(),
        P(),
        P(),
        P(),
        P(),
        P(),
        P(),
    )
    return jax.shard_map(
        body,
        mesh=mesh,
        in_specs=placed,
        out_specs=P(("slides", "cols", "rows"), None),
        check_vma=False,
    )
```

```python
from functools import partial

import jax
import jax.numpy as jnp
from jax import lax
from jax.experimental import pallas as pl
from jax.experimental.pallas import tpu as pltpu
from jax.sharding import PartitionSpec as P


E = 1536
D = 768
HDIM = 64
NSTATE = 64
PATCH = 16
KERNEL = 24
HEADS = 24
CHAN = 3
MARGIN = (KERNEL - PATCH) // 2
WIN = CHAN * KERNEL
LEAD = 8
F32 = jnp.float32
BF16 = jnp.bfloat16


def vmem():
    return pl.BlockSpec(memory_space=pltpu.VMEM)


def call(kernel, inputs, outs, scratch=(), limit=4, flops=0, moved=0, scalars=0, outside=False):
    return pl.pallas_call(
        kernel,
        out_shape=outs,
        in_specs=[pl.BlockSpec(memory_space=pltpu.SMEM)] * scalars + [vmem()] * (len(inputs) - scalars),
        out_specs=jax.tree.map(lambda _: pl.BlockSpec(memory_space=pl.ANY) if outside else vmem(), outs),
        scratch_shapes=scratch,
        compiler_params=pltpu.CompilerParams(vmem_limit_bytes=limit << 20),
        cost_estimate=pl.CostEstimate(flops=flops, bytes_accessed=moved, transcendentals=0),
    )(*inputs)


def shape(dims, kind=BF16):
    return jax.ShapeDtypeStruct(dims, kind)


def pack_kernel(own, partner, *refs):
    outs, rows = refs[:-1], refs[-1]
    col, row = lax.axis_index("cols"), lax.axis_index("rows")
    local = own.shape[1]
    width = own.shape[2]
    edge = jnp.zeros((CHAN, 32, width), BF16)
    rows[:, 0:32, :] = edge
    rows[:, 32 + 2 * local : 64 + 2 * local, :] = edge
    rows[:, pl.ds(pl.multiple_of(32 + local * row, 32), local), :] = own[...]
    rows[:, pl.ds(pl.multiple_of(32 + local * (1 - row), 32), local), :] = partner[...]
    side = len(outs)
    for step, out in enumerate(outs):
        chip = side * row + ((col % side) ^ step)
        first = pl.multiple_of(2 * PATCH * chip, 32)
        blocks = [rows[channel, pl.ds(first, 80), :].astype(F32) for channel in range(CHAN)]
        pieces = [block[28 + 8 * group : 36 + 8 * group] for group in range(5) for block in blocks]
        tails = [block[12 + 8 * group : 20 + 8 * group, width - 64 :] for group in range(2) for block in blocks]
        tails.append(jnp.zeros((8, width - 64 * len(tails)), F32))
        out[...] = jnp.concatenate([*pieces, jnp.concatenate(tails, axis=1)], axis=0).astype(BF16)


def stage_kernel(pixels, out):
    out[...] = pixels[...]


def pick_matrix():
    row = lax.broadcasted_iota(jnp.int32, (256, 256), 0)
    pixel = lax.broadcasted_iota(jnp.int32, (256, 256), 1)
    return (pixel == (row & 15) * PATCH + (row >> 4)).astype(BF16)


def turned(pick, values):
    return lax.dot_general(pick, values, (((1,), (1,)), ((), ())), preferred_element_type=F32)


def window_pixel(offset):
    place = offset - MARGIN + PATCH
    return place % PATCH, place // PATCH - 1


def neighbours():
    return [offset for offset in range(KERNEL) if window_pixel(offset)[1]]


def place_tokens(pick, values, first, wide, beside):
    both = jnp.concatenate([values[:, :256], values[:, 256:]], axis=0)
    found = turned(pick, both).reshape(PATCH, 16, 256)
    for group in range(2):
        piece = found[:, :, 128 * group : 128 * (group + 1)]
        rounded = piece.astype(BF16)
        rows = pl.ds(pl.multiple_of(first + 16 * group, 16), 16)
        for offset in range(KERNEL):
            pixel, shift = window_pixel(offset)
            if shift == 0:
                wide[rows, offset * 128 : (offset + 1) * 128] = rounded[pixel]
        rows = pl.ds(pl.multiple_of(LEAD + first + 16 * group, 8), 16)
        for slot, offset in enumerate(neighbours()):
            beside[slot, rows, :] = piece[window_pixel(offset)[0]]


def place_beside(count, first, wide, beside):
    for slot, offset in enumerate(neighbours()):
        start = LEAD + window_pixel(offset)[1]
        part = beside[slot, start : start + count, :]
        wide[first : first + count, offset * 128 : (offset + 1) * 128] = part.astype(BF16)


def clear_ends(count, beside):
    zeros = jnp.zeros((beside.shape[0], LEAD, 128), F32)
    beside[:, 0:LEAD, :] = zeros
    beside[:, LEAD + count : LEAD + count + LEAD, :] = zeros


def windows_of(block, row, lanes):
    window = pl.ds(pl.multiple_of(2 * KERNEL * row, 16), WIN)
    values = block[window, lanes]
    return jnp.concatenate([values, jnp.zeros((128 - WIN, values.shape[1]), BF16)], axis=0)


def embed_kernel(*refs):
    blocks, (weight, bias, out, wide, beside, tail) = refs[:-6], refs[-6:]
    col, row = lax.axis_index("cols"), lax.axis_index("rows")
    count = len(blocks)
    side = count // 2
    width = blocks[0].shape[1]
    tokens = count * width // PATCH
    pick = pick_matrix()
    clear_ends(tokens, beside)
    edge = jnp.zeros((WIN, 128), F32)
    extra = jnp.zeros((8, 128 * CHAN), F32)
    for place, block in enumerate(blocks):
        source = side * (row if place < side else 1 - row) + ((col % side) ^ (place % side))
        for group in range(width // 512):
            first = source * (width // PATCH) + 32 * group
            place_tokens(pick, windows_of(block, row, slice(512 * group, 512 * (group + 1))), first, wide, beside)
        last = source == count - 1
        edge = jnp.where(last, block[0:WIN, width - 128 :].astype(F32), edge)
        extra = jnp.where(last, block[5 * KERNEL - 8 : 5 * KERNEL + 8, : 128 * CHAN].astype(F32)[8:], extra)
    before = [extra[:, 64 * piece : 64 * (piece + 1)] for piece in range(2 * CHAN)] + [edge[:KERNEL, 64:]]
    last = jnp.where(row == 0, jnp.concatenate(before, axis=0), edge[:, 64:])
    last = jnp.concatenate([last, jnp.zeros((128 - WIN, 64), F32)], axis=0)
    last = jnp.concatenate([jnp.zeros((128, 64), F32), last, jnp.zeros((128, 128), F32)], axis=1)
    tail[:, 0:8, :] = jnp.zeros((PATCH, 8, 128), F32)
    tail[:, 8:24, :] = turned(pick, last.astype(BF16)).reshape(PATCH, 16, 128)
    for offset in range(KERNEL):
        pixel, shift = window_pixel(offset)
        part = tail[pixel, 8 + shift : 16 + shift, :]
        wide[tokens:, offset * 128 : (offset + 1) * 128] = part.astype(BF16)
    place_beside(tokens, 0, wide, beside)
    grid = jnp.dot(wide[...], weight[...], preferred_element_type=F32)
    out[...] = (grid + bias[...]).astype(BF16)


def spread_matrix():
    head = lax.broadcasted_iota(jnp.int32, (HEADS, E), 0)
    lane = lax.broadcasted_iota(jnp.int32, (HEADS, E), 1)
    return ((lane >= head * HDIM) & (lane < (head + 1) * HDIM)).astype(BF16)


def halves(values):
    high = values.astype(BF16)
    return high, (values - high.astype(F32)).astype(BF16)


def spread(values, matrix):
    high, low = halves(values)
    return jnp.dot(high, matrix, preferred_element_type=F32) + jnp.dot(low, matrix, preferred_element_type=F32)


def silu(values):
    half = 0.5 * values
    return half + half * jnp.tanh(half)


def softplus(values):
    small = jnp.exp(-jnp.abs(values))
    return jnp.maximum(values, 0.0) + jnp.log1p(small)


def half_inputs(which, normed, mix_weight, conv_weight, conv_bias, x_out):
    half = E // 2
    chunk = 256
    parts = []
    spans = [
        pl.ds(pl.multiple_of(which * half + first, 128), chunk) for first in range(0, half, chunk)
    ]
    ahead = project(normed, mix_weight, spans[0])
    for place, lanes in enumerate(spans):
        raw = ahead
        if place + 1 < len(spans):
            ahead = project(normed, mix_weight, spans[place + 1])
        part = mixed(raw, conv_weight[:, lanes], conv_bias[:, lanes])
        x_out[:, place * chunk : (place + 1) * chunk] = part
        parts.append(part)
    return parts


def half_state(which, parts, scales, b_t):
    half = E // 2
    matrix = spread_matrix().astype(F32)
    wanted = jnp.where(which == 0, matrix[:, :half], matrix[:, half:]).astype(BF16)
    states = []
    for place, part in enumerate(parts):
        chunk = part.shape[1]
        to_end = jnp.dot(scales, wanted[:, place * chunk : (place + 1) * chunk], preferred_element_type=F32)
        scaled = (part.astype(F32) * to_end).astype(BF16)
        states.append(jnp.dot(b_t, scaled, preferred_element_type=F32))
    return jnp.concatenate(states, axis=1)


def project(normed, mix_weight, lanes):
    return jnp.dot(normed, mix_weight[:, lanes], preferred_element_type=F32).astype(BF16)


def mixed(raw, weight, bias):
    raw = raw.astype(F32)
    total = weight[0:1] * raw
    for tap in range(1, weight.shape[0]):
        total = pltpu.roll(total, 1, 0) + weight[tap : tap + 1] * raw
    return silu(total[:-LEAD] + bias).astype(BF16)


def mix_kernel(
    embedded, norm_gain, mix_weight, step_weight, step_bias, log_rate, conv_weight, conv_bias,
    normed_out, x_out, b_out, c_out, b_t_out, step_out, cum_out, scales_out, decay_out, send_out,
):
    col, row = lax.axis_index("cols"), lax.axis_index("rows")
    resid = embedded[...].astype(F32)
    mean_sq = jnp.mean(resid * resid, axis=-1, keepdims=True)
    normed_f = resid * lax.rsqrt(mean_sq + 1e-05) * norm_gain[...]
    rows = lax.broadcasted_iota(jnp.int32, normed_f.shape, 0)
    blank = (rows >= embedded.shape[0] - LEAD) & (col == 0) & (row == 0)
    normed = jnp.where(blank, 0.0, normed_f).astype(BF16)
    normed_out[...] = normed
    length = embedded.shape[0] - LEAD
    maps_raw = project(normed, mix_weight, slice(E, E + 2 * NSTATE))
    step_raw = lax.dot_general(
        normed, step_weight[...], (((1,), (1,)), ((), ())), preferred_element_type=F32
    )[:-LEAD]
    step = softplus(step_raw + step_bias[...])
    log_decay = -step * jnp.exp(log_rate[...])
    lower = (
        lax.broadcasted_iota(jnp.int32, (length, length), 0) >= lax.broadcasted_iota(jnp.int32, (length, length), 1)
    ).astype(BF16)
    high = log_decay.astype(BF16)
    middle = (log_decay - high.astype(F32)).astype(BF16)
    low = (log_decay - high.astype(F32) - middle.astype(F32)).astype(BF16)
    cum = jnp.dot(lower, high, preferred_element_type=F32)
    cum = cum + jnp.dot(lower, middle, preferred_element_type=F32)
    cum = cum + jnp.dot(lower, low, preferred_element_type=F32)
    step_out[...] = step
    cum_out[...] = cum
    parts = half_inputs(1 - row, normed, mix_weight, conv_weight, conv_bias, x_out)
    last = cum[length - 1 :]
    scales = (jnp.exp(last - cum) * step).astype(BF16)
    scales_out[...] = scales
    decay = spread(jnp.broadcast_to(jnp.exp(last), (8, HEADS)), spread_matrix())
    maps = mixed(maps_raw, conv_weight[:, E:], conv_bias[:, E:]).astype(F32)
    b_out[...] = maps[:, :NSTATE].astype(BF16)
    c_out[...] = maps[:, NSTATE:].astype(BF16)
    b_t = maps.T[:NSTATE].astype(BF16)
    b_t_out[...] = b_t
    state = half_state(1 - row, parts, scales, b_t)
    half = E // 2
    first = row == 0
    decay_out[...] = jnp.where(first, decay[:, :half], decay[:, half:])
    send_out[...] = wire(state, jnp.where(first, decay[:, half:], decay[:, :half]))


def rest_kernel(normed, scales, b_t, mix_weight, conv_weight, conv_bias, decay, x_out, keep_out):
    row = lax.axis_index("rows")
    parts = half_inputs(row, normed[...], mix_weight, conv_weight, conv_bias, x_out)
    keep_out[0:NSTATE, :] = half_state(row, parts, scales[...], b_t[...])
    keep_out[NSTATE : NSTATE + 8, :] = decay[...]


TILES = E // 2 // 128
MESSAGE = (TILES * NSTATE + 16, 128)


def wire(values, decay):
    high = decay.astype(BF16).astype(F32)
    place = lax.broadcasted_iota(jnp.int32, (8, 128), 0)
    rows = [jnp.zeros((8, 128), F32)] * 2
    for tile in range(TILES):
        lanes = slice(128 * tile, 128 * (tile + 1))
        for part, piece in enumerate((high, decay - high)):
            rows[part] = jnp.where(place == tile, piece[:, lanes], rows[part])
    columns = [values[:, 128 * tile : 128 * (tile + 1)] for tile in range(TILES)]
    return jnp.concatenate([*columns, *rows], axis=0).astype(BF16)


def unwire(message):
    columns = [message[NSTATE * tile : NSTATE * (tile + 1), :].astype(F32) for tile in range(TILES)]
    rows = message[TILES * NSTATE :, :].astype(F32)
    decay = rows[:8] + rows[8:]
    decays = [jnp.broadcast_to(decay[tile : tile + 1], (8, 128)) for tile in range(TILES)]
    return jnp.concatenate(columns, axis=1), jnp.concatenate(decays, axis=1)


def product(factors):
    total = factors[0]
    for factor in factors[1:]:
        total = total * factor
    return total


def folded(place, pieces):
    places = [place ^ step for step in range(len(pieces))]
    steps = range(len(pieces))
    one = jnp.ones_like(pieces[0][1])
    all_values, ahead_values = None, None
    for step in steps:
        after = [jnp.where(places[k] > places[step], pieces[k][1], one) for k in steps if k != step]
        between = [
            jnp.where((places[k] > places[step]) & (places[k] < place), pieces[k][1], one)
            for k in steps
            if k not in (0, step)
        ]
        term = product(after)[0:1] * pieces[step][0]
        all_values = term if step == 0 else all_values + term
        if step:
            weight = jnp.where(places[step] < place, product([one, *between]), 0.0)
            term = weight[0:1] * pieces[step][0]
            ahead_values = term if ahead_values is None else ahead_values + term
    all_decay = product([decay for _, decay in pieces])
    ahead_decay = product([jnp.where(places[k] < place, pieces[k][1], one) for k in steps if k])
    return (all_values, all_decay), (ahead_values, ahead_decay)


def read(summary):
    return summary[0:NSTATE, :], summary[NSTATE : NSTATE + 8, :]


def write(summary, piece):
    summary[0:NSTATE, :] = piece[0]
    summary[NSTATE : NSTATE + 8, :] = piece[1]


def chained(earlier, latter):
    return latter[1][0:1] * earlier[0] + latter[0], earlier[1] * latter[1]


def pair_kernel(keep, received, total_out, message_out):
    total, _ = folded(lax.axis_index("rows"), [read(keep), unwire(received)])
    write(total_out, total)
    message_out[...] = wire(*total)


def join_kernel(low, count, first, *refs):
    refs = list(refs)
    total = read(refs.pop(0))
    before = None if first else read(refs.pop(0))
    pieces = [total] + [unwire(refs.pop(0)) for _ in range(count - 1)]
    place = (lax.axis_index("cols") // low) & (count - 1)
    total, ahead = folded(place, pieces)
    before_out, message_out = refs[:2]
    write(before_out, ahead if first else chained(ahead, before))
    message_out[...] = wire(*total)
    write(refs[2], total)


def enter_kernel(low, count, first, *refs):
    refs = list(refs)
    total = read(refs.pop(0))
    before = None if first else read(refs.pop(0))
    pieces = [total] + [unwire(refs.pop(0)) for _ in range(count - 1)]
    keep, received, mine_out, theirs_out = refs
    _, ahead = folded((lax.axis_index("cols") // low) & (count - 1), pieces)
    if not first:
        ahead = chained(ahead, before)
    own, other = read(keep), unwire(received)
    upper = lax.axis_index("rows") == 1
    low_piece = tuple(jnp.where(upper, b, a) for a, b in zip(own, other))
    second = chained(ahead, low_piece)[0]
    mine_out[...] = jnp.where(upper, second, ahead[0]).astype(BF16)
    theirs_out[...] = jnp.where(upper, ahead[0], second).astype(BF16)


def gate_kernel(normed, gate_weight, local_mine, local_theirs, cum, own_out, factor_out):
    gate = jnp.dot(normed[...], gate_weight[...], preferred_element_type=F32)[:-LEAD].astype(BF16).astype(F32)
    gate = silu(gate)
    half = local_mine.shape[1]
    upper = lax.axis_index("rows") == 1
    own_out[:, :half] = jnp.where(upper, local_theirs[...], local_mine[...]) * gate[:, :half]
    own_out[:, half:] = jnp.where(upper, local_mine[...], local_theirs[...]) * gate[:, half:]
    factor_out[...] = spread(jnp.exp(cum[...]), spread_matrix()) * gate


def intra_kernel(flip, skip, x, b_mat, c_mat, step, cum, out):
    row = lax.axis_index("rows")
    which = 1 - row if flip else row
    heads = HEADS // 2
    upper = which == 1
    length = x.shape[0]
    half = length // 2
    scores = lax.dot_general(c_mat[...], b_mat[...], (((1,), (1,)), ((), ())), preferred_element_type=F32)
    causal = lax.broadcasted_iota(jnp.int32, (length, length), 0) >= lax.broadcasted_iota(
        jnp.int32, (length, length), 1
    )
    scores = jnp.where(causal, scores, 0.0)
    wide = jnp.zeros((length, 128 - heads), F32)
    cum_v = jnp.where(upper, cum[:, heads:], cum[:, :heads])
    cum_t = jnp.concatenate([cum_v, wide], axis=1).T
    step_t = jnp.concatenate([jnp.where(upper, step[:, heads:], step[:, :heads]), wide], axis=1).T
    for place in range(out.shape[1] // 128):
        pair = place
        lanes = slice(place * 128, (place + 1) * 128)
        x_pair = x[:, lanes].astype(F32)
        lane = lax.broadcasted_iota(jnp.int32, x_pair.shape, 1)
        top = bottom = None
        for member in range(2):
            head = 2 * pair + member
            column = cum_v[:, head : head + 1]
            cum_row = cum_t[head : head + 1, :]
            step_row = step_t[head : head + 1, :]

            def weights(rows, span):
                gap = jnp.minimum(column[rows] - cum_row[:, span], 0.0)
                return (scores[rows, span] * jnp.exp(gap) * step_row[:, span]).astype(BF16)

            inputs = jnp.where((lane < HDIM) == (member == 0), x_pair, 0.0).astype(BF16)
            upper_part = jnp.dot(
                weights(slice(0, half), slice(0, half)), inputs[:half], preferred_element_type=F32
            )
            lower_part = jnp.dot(
                weights(slice(half, length), slice(0, length)), inputs, preferred_element_type=F32
            )
            top = upper_part if top is None else top + upper_part
            bottom = lower_part if bottom is None else bottom + lower_part
        base = which * heads + 2 * pair
        direct = jnp.where(lane < HDIM, skip[base], skip[base + 1]) * x_pair
        out[0:half, lanes] = top + direct[:half]
        out[half:length, lanes] = bottom + direct[half:]


def half_hidden(lanes, state, own, factor, c_mat, out_gain):
    carried = jnp.dot(c_mat[...], state[...], preferred_element_type=F32)
    gated = own[:, lanes] + carried * factor[:, lanes]
    squares = jnp.sum(gated * gated, axis=-1, keepdims=True)
    return (gated * out_gain[:, lanes]).astype(BF16), squares


def first_kernel(mine, own, factor, c_mat, out_gain, out_weight, product_out, squares_out):
    half = own.shape[1] // 2
    lanes = pl.ds(pl.multiple_of(lax.axis_index("rows") * half, 128), half)
    hidden, squares = half_hidden(lanes, mine, own, factor, c_mat, out_gain)
    product = jnp.dot(hidden, out_weight[lanes, :], preferred_element_type=F32)
    product_out[...] = product
    squares_out[...] = jnp.broadcast_to(squares, squares_out.shape)


def finish_kernel(
    theirs, own, factor, c_mat, out_gain, out_weight, product, squares, embedded, out, result, sems
):
    which = 1 - lax.axis_index("rows")
    half = own.shape[1] // 2
    lanes = pl.ds(pl.multiple_of(which * half, 128), half)
    hidden, more = half_hidden(lanes, theirs, own, factor, c_mat, out_gain)
    scale = lax.rsqrt((squares[:, 0:1] + more) / own.shape[1] + 1e-05)
    chunk = result.shape[2]
    copies = []
    for place in range(result.shape[0]):
        span = slice(place * chunk, (place + 1) * chunk)
        rest = jnp.dot(hidden, out_weight[lanes, span], preferred_element_type=F32)
        resid = embedded[:, span].astype(F32)[:-LEAD]
        result[place] = ((product[:, span] + rest) * scale + resid).astype(BF16)
        copies.append(pltpu.make_async_copy(result.at[place], out.at[:, span], sems.at[place]))
        copies[-1].start()
    for copy in copies:
        copy.wait()


def swap(block, axis, bit):
    return lax.ppermute(block, axis, [(i, i ^ bit) for i in range(lax.axis_size(axis))])


def sending_order(side):
    return (*range(side // 2, side), *reversed(range(side // 2)))


def across(block, step):
    side = lax.axis_size("cols") // 2
    pairs = []
    for col in range(2 * side):
        for row in range(2):
            other = side * row + ((col % side) ^ step)
            pairs.append((2 * col + row, 2 * other + col // side))
    return lax.ppermute(block, ("cols", "rows"), pairs)


def embed_by_rows(pixels, patch_weight, patch_bias):
    col_count = lax.axis_size("cols")
    side = col_count // 2
    width = pixels.shape[2]
    partner = swap(pixels, "rows", 1)
    pixels = call(stage_kernel, (pixels,), shape(pixels.shape))
    block = shape((5 * KERNEL + 8, width))
    scratch = [pltpu.VMEM((CHAN, 2 * pixels.shape[1] + 64, width), BF16)]
    blocks = call(pack_kernel, (pixels, partner), [block] * side, scratch, limit=8)
    near, far = [None] * side, [None] * side
    for step in sending_order(side):
        near[step] = across(blocks[step], step)
        far[step] = swap(near[step], "rows", 1)
    came = near + far
    weight = patch_weight.reshape(3, 8, KERNEL, CHAN, D).transpose(2, 0, 3, 1, 4).reshape(KERNEL, WIN, D)
    weight = jnp.pad(weight, ((0, 0), (0, 128 - WIN), (0, 0))).reshape(KERNEL * 128, D)
    tokens = col_count * width // PATCH
    scratch = [
        pltpu.VMEM((tokens + LEAD, KERNEL * 128), BF16),
        pltpu.VMEM((len(neighbours()), tokens + 2 * LEAD, 128), F32),
        pltpu.VMEM((PATCH, 24, 128), F32),
    ]
    return call(
        embed_kernel, (*came, weight, patch_bias.reshape(1, -1)), shape((tokens + LEAD, D)), scratch,
        flops=2 * tokens * KERNEL * 128 * D, moved=6 << 20, limit=16,
    )


def extended(block, sides, width):
    for axis, dim in sides:
        count = lax.axis_size(axis)
        forward = [(i, i + 1) for i in range(count - 1)]
        backward = [(target, source) for source, target in forward]
        low = lax.ppermute(
            lax.slice_in_dim(block, block.shape[dim] - width, None, axis=dim), axis, forward
        )
        high = lax.ppermute(lax.slice_in_dim(block, 0, width, axis=dim), axis, backward)
        block = jnp.concatenate([low, block, high], axis=dim)
    return block


def shifted(block, axis, distance):
    devices = range(lax.axis_size(axis))
    route = [(i - distance, i) for i in devices if i - distance in devices]
    return lax.ppermute(block, axis, route)


def embed_by_blocks(pixels, patch_weight, patch_bias):
    padded = extended(pixels, (("cols", 2), ("rows", 1)), MARGIN)
    embed_grid = lax.conv_general_dilated(
        padded[None],
        patch_weight,
        (PATCH, PATCH),
        "VALID",
        dimension_numbers=("NCHW", "HWIO", "NHWC"),
        preferred_element_type=jnp.float32,
    )[0]
    embed_grid = (embed_grid + patch_bias).astype(jnp.bfloat16)
    row_local, col_local, feature_width = embed_grid.shape
    devices = lax.axis_size(("cols", "rows"))
    row_count = lax.axis_size("rows")
    col_count = lax.axis_size("cols")
    groups = col_count // row_local
    piece_len = col_local * feature_width // devices
    outgoing = embed_grid.reshape(row_local, devices, piece_len)
    spread = lax.all_to_all(outgoing, ("cols", "rows"), split_axis=1, concat_axis=1, tiled=True)
    spread = spread.reshape(row_local, groups, row_local, row_count, piece_len).transpose(
        3, 0, 1, 2, 4
    )
    landed = lax.all_to_all(
        spread.reshape(devices, row_local, piece_len),
        ("cols", "rows"),
        split_axis=0,
        concat_axis=0,
        tiled=True,
    )
    tokens = landed.transpose(1, 0, 2).reshape(row_local * col_local, feature_width)
    tail = shifted(tokens[tokens.shape[0] - LEAD :], ("cols", "rows"), 1)
    return jnp.concatenate([tokens, tail], axis=0)


def body(
    pixels,
    patch_weight,
    patch_bias,
    norm_gain,
    gate_weight,
    mix_weight,
    step_weight,
    step_bias,
    log_rate,
    conv_weight,
    conv_bias,
    skip_gain,
    out_gain,
    out_weight,
):
    col_count = lax.axis_size("cols")
    row_local = pixels.shape[1] // PATCH
    if col_count == row_local and lax.axis_size("rows") == 2:
        embedded = embed_by_rows(pixels, patch_weight, patch_bias)
    else:
        embedded = embed_by_blocks(pixels, patch_weight, patch_bias)
    length = embedded.shape[0] - LEAD
    line = lambda a: a.reshape(1, -1)
    mixed_width = mix_weight.shape[1]
    half = E // 2
    packed = NSTATE + 8
    conv = (conv_weight, line(conv_bias))
    normed, x_theirs, b_mat, c_mat, b_t, step, cum, scales, decay, send = call(
        mix_kernel,
        (embedded, line(norm_gain), mix_weight, step_weight.T, line(step_bias), line(log_rate), *conv),
        [
            shape((LEAD + length, D)), shape((length, half)), shape((length, NSTATE)), shape((length, NSTATE)),
            shape((NSTATE, length)), shape((length, HEADS), F32), shape((length, HEADS), F32),
            shape((length, HEADS)), shape((8, half), F32), shape(MESSAGE),
        ],
        flops=length * D * mixed_width, moved=4 << 20, limit=16,
    )
    came = swap(send, "rows", 1)
    summary, message = shape((packed, half), F32), shape(MESSAGE)
    x_mine, keep = call(
        rest_kernel, (normed, scales, b_t, mix_weight, *conv, decay), [shape((length, half)), summary],
        flops=length * D * mixed_width, moved=4 << 20, limit=16,
    )
    total, out = call(pair_kernel, (keep, came), [summary, message])
    locals_ = []
    for part in range(2):
        locals_.append(
            call(
                partial(intra_kernel, bool(part)), (skip_gain, (x_mine, x_theirs)[part], b_mat, c_mat, step, cum),
                shape((length, half), F32), scalars=1,
                flops=HEADS * length * length * 128, moved=2 << 20, limit=8,
            )
        )
    own, factor = call(
        gate_kernel, (normed, gate_weight, *locals_, cum), [shape((length, E), F32)] * 2,
        flops=2 * length * D * E, moved=4 << 20, limit=8,
    )
    groups, low = [], 1
    while low < col_count:
        count = min(4, col_count // low)
        groups.append((low, count))
        low *= count
    before = None
    for number, (low, count) in enumerate(groups):
        ending = number + 1 == len(groups)
        arrived = []
        for hop in range(1, count):
            arrived.append(swap(out, "cols", hop * low))
        first = before is None
        inputs = ([total] if first else [total, before]) + arrived
        if ending:
            entering = shape((NSTATE, half))
            mine, theirs = call(partial(enter_kernel, low, count, first), (*inputs, keep, came), [entering, entering])
        else:
            before, out, total = call(partial(join_kernel, low, count, first), inputs, [summary, message, summary])
    theirs = swap(theirs, "rows", 1)
    common = (own, factor, c_mat, line(out_gain), out_weight)
    partial_sum, squares = call(
        first_kernel, (mine, *common), [shape((length, D), F32), shape((length, 128), F32)],
        flops=length * D * E, moved=4 << 20, limit=8,
    )
    return call(
        finish_kernel, (theirs, *common, partial_sum, squares, embedded), shape((length, D)),
        [pltpu.VMEM((3, length, D // 3), BF16), pltpu.SemaphoreType.DMA((3,))],
        flops=length * D * E, moved=4 << 20, limit=8, outside=True,
    )


def solution(mesh):
    placed = (
        P(None, "rows", ("slides", "cols")),
        P(),
        P(),
        P(),
        P(),
        P(),
        P(),
        P(),
        P(),
        P(),
        P(),
        P(),
        P(),
        P(),
    )
    return jax.shard_map(
        body,
        mesh=mesh,
        in_specs=placed,
        out_specs=P(("slides", "cols", "rows"), None),
        check_vma=False,
    )
```

```python
from functools import partial

import jax
import jax.numpy as jnp
from jax import lax
from jax.experimental import pallas as pl
from jax.experimental.pallas import tpu as pltpu
from jax.sharding import PartitionSpec as P


E = 1536
D = 768
HDIM = 64
NSTATE = 64
PATCH = 16
KERNEL = 24
HEADS = 24
CHAN = 3
MARGIN = (KERNEL - PATCH) // 2
WIN = CHAN * KERNEL
LEAD = 8
F32 = jnp.float32
BF16 = jnp.bfloat16


def vmem():
    return pl.BlockSpec(memory_space=pltpu.VMEM)


def call(kernel, inputs, outs, scratch=(), limit=4, flops=0, moved=0, scalars=0, outside=False):
    return pl.pallas_call(
        kernel,
        out_shape=outs,
        in_specs=[pl.BlockSpec(memory_space=pltpu.SMEM)] * scalars + [vmem()] * (len(inputs) - scalars),
        out_specs=jax.tree.map(lambda _: pl.BlockSpec(memory_space=pl.ANY) if outside else vmem(), outs),
        scratch_shapes=scratch,
        compiler_params=pltpu.CompilerParams(vmem_limit_bytes=limit << 20),
        cost_estimate=pl.CostEstimate(flops=flops, bytes_accessed=moved, transcendentals=0),
    )(*inputs)


def shape(dims, kind=BF16):
    return jax.ShapeDtypeStruct(dims, kind)


def pack_kernel(own, partner, *refs):
    outs, rows = refs[:-1], refs[-1]
    col, row = lax.axis_index("cols"), lax.axis_index("rows")
    local = own.shape[1]
    width = own.shape[2]
    edge = jnp.zeros((CHAN, 32, width), BF16)
    rows[:, 0:32, :] = edge
    rows[:, 32 + 2 * local : 64 + 2 * local, :] = edge
    rows[:, pl.ds(pl.multiple_of(32 + local * row, 32), local), :] = own[...]
    rows[:, pl.ds(pl.multiple_of(32 + local * (1 - row), 32), local), :] = partner[...]
    side = len(outs)
    for step, out in enumerate(outs):
        chip = side * row + ((col % side) ^ step)
        first = pl.multiple_of(2 * PATCH * chip, 32)
        blocks = [rows[channel, pl.ds(first, 80), :].astype(F32) for channel in range(CHAN)]
        pieces = [block[28 + 8 * group : 36 + 8 * group] for group in range(5) for block in blocks]
        tails = [block[12 + 8 * group : 20 + 8 * group, width - 64 :] for group in range(2) for block in blocks]
        tails.append(jnp.zeros((8, width - 64 * len(tails)), F32))
        out[...] = jnp.concatenate([*pieces, jnp.concatenate(tails, axis=1)], axis=0).astype(BF16)


def stage_kernel(pixels, out):
    out[...] = pixels[...]


def pick_matrix():
    row = lax.broadcasted_iota(jnp.int32, (256, 256), 0)
    pixel = lax.broadcasted_iota(jnp.int32, (256, 256), 1)
    return (pixel == (row & 15) * PATCH + (row >> 4)).astype(BF16)


def turned(pick, values):
    return lax.dot_general(pick, values, (((1,), (1,)), ((), ())), preferred_element_type=F32)


def window_pixel(offset):
    place = offset - MARGIN + PATCH
    return place % PATCH, place // PATCH - 1


def neighbours():
    return [offset for offset in range(KERNEL) if window_pixel(offset)[1]]


def place_tokens(pick, values, first, wide, beside):
    both = jnp.concatenate([values[:, :256], values[:, 256:]], axis=0)
    found = turned(pick, both).reshape(PATCH, 16, 256)
    for group in range(2):
        piece = found[:, :, 128 * group : 128 * (group + 1)]
        rounded = piece.astype(BF16)
        rows = pl.ds(pl.multiple_of(first + 16 * group, 16), 16)
        for offset in range(KERNEL):
            pixel, shift = window_pixel(offset)
            if shift == 0:
                wide[rows, offset * 128 : (offset + 1) * 128] = rounded[pixel]
        rows = pl.ds(pl.multiple_of(LEAD + first + 16 * group, 8), 16)
        for slot, offset in enumerate(neighbours()):
            beside[slot, rows, :] = piece[window_pixel(offset)[0]]


def place_beside(count, first, wide, beside):
    for slot, offset in enumerate(neighbours()):
        start = LEAD + window_pixel(offset)[1]
        part = beside[slot, start : start + count, :]
        wide[first : first + count, offset * 128 : (offset + 1) * 128] = part.astype(BF16)


def clear_ends(count, beside):
    zeros = jnp.zeros((beside.shape[0], LEAD, 128), F32)
    beside[:, 0:LEAD, :] = zeros
    beside[:, LEAD + count : LEAD + count + LEAD, :] = zeros


def windows_of(block, row, lanes):
    window = pl.ds(pl.multiple_of(2 * KERNEL * row, 16), WIN)
    values = block[window, lanes]
    return jnp.concatenate([values, jnp.zeros((128 - WIN, values.shape[1]), BF16)], axis=0)


def embed_kernel(*refs):
    blocks, (weight, bias, out, wide, beside, tail) = refs[:-6], refs[-6:]
    col, row = lax.axis_index("cols"), lax.axis_index("rows")
    count = len(blocks)
    side = count // 2
    width = blocks[0].shape[1]
    tokens = count * width // PATCH
    pick = pick_matrix()
    clear_ends(tokens, beside)
    edge = jnp.zeros((WIN, 128), F32)
    extra = jnp.zeros((8, 128 * CHAN), F32)
    for place, block in enumerate(blocks):
        source = side * (row if place < side else 1 - row) + ((col % side) ^ (place % side))
        for group in range(width // 512):
            first = source * (width // PATCH) + 32 * group
            place_tokens(pick, windows_of(block, row, slice(512 * group, 512 * (group + 1))), first, wide, beside)
        last = source == count - 1
        edge = jnp.where(last, block[0:WIN, width - 128 :].astype(F32), edge)
        extra = jnp.where(last, block[5 * KERNEL - 8 : 5 * KERNEL + 8, : 128 * CHAN].astype(F32)[8:], extra)
    before = [extra[:, 64 * piece : 64 * (piece + 1)] for piece in range(2 * CHAN)] + [edge[:KERNEL, 64:]]
    last = jnp.where(row == 0, jnp.concatenate(before, axis=0), edge[:, 64:])
    last = jnp.concatenate([last, jnp.zeros((128 - WIN, 64), F32)], axis=0)
    last = jnp.concatenate([jnp.zeros((128, 64), F32), last, jnp.zeros((128, 128), F32)], axis=1)
    tail[:, 0:8, :] = jnp.zeros((PATCH, 8, 128), F32)
    tail[:, 8:24, :] = turned(pick, last.astype(BF16)).reshape(PATCH, 16, 128)
    for offset in range(KERNEL):
        pixel, shift = window_pixel(offset)
        part = tail[pixel, 8 + shift : 16 + shift, :]
        wide[tokens:, offset * 128 : (offset + 1) * 128] = part.astype(BF16)
    place_beside(tokens, 0, wide, beside)
    for first in range(0, D, 256):
        lanes = slice(first, first + 256)
        grid = jnp.dot(wide[...], weight[:, lanes], preferred_element_type=F32)
        out[:, lanes] = (grid + bias[:, lanes]).astype(BF16)


def spread_matrix():
    head = lax.broadcasted_iota(jnp.int32, (HEADS, E), 0)
    lane = lax.broadcasted_iota(jnp.int32, (HEADS, E), 1)
    return ((lane >= head * HDIM) & (lane < (head + 1) * HDIM)).astype(BF16)


def halves(values):
    high = values.astype(BF16)
    return high, (values - high.astype(F32)).astype(BF16)


def spread(values, matrix):
    high, low = halves(values)
    return jnp.dot(high, matrix, preferred_element_type=F32) + jnp.dot(low, matrix, preferred_element_type=F32)


def silu(values):
    half = 0.5 * values
    return half + half * jnp.tanh(half)


def softplus(values):
    small = jnp.exp(-jnp.abs(values))
    return jnp.maximum(values, 0.0) + jnp.log1p(small)


def half_inputs(which, normed, mix_weight, conv_weight, conv_bias, x_out):
    half = E // 2
    chunk = 384
    parts = []
    spans = [
        pl.ds(pl.multiple_of(which * half + first, 128), chunk) for first in range(0, half, chunk)
    ]
    ahead = project(normed, mix_weight, spans[0])
    for place, lanes in enumerate(spans):
        raw = ahead
        if place + 1 < len(spans):
            ahead = project(normed, mix_weight, spans[place + 1])
        part = mixed(raw, conv_weight[:, lanes], conv_bias[:, lanes])
        x_out[:, place * chunk : (place + 1) * chunk] = part
        parts.append(part)
    return parts


def half_state(which, parts, scales, b_t):
    half = E // 2
    matrix = spread_matrix().astype(F32)
    wanted = jnp.where(which == 0, matrix[:, :half], matrix[:, half:]).astype(BF16)
    states = []
    for place, part in enumerate(parts):
        chunk = part.shape[1]
        to_end = jnp.dot(scales, wanted[:, place * chunk : (place + 1) * chunk], preferred_element_type=F32)
        scaled = (part.astype(F32) * to_end).astype(BF16)
        states.append(jnp.dot(b_t, scaled, preferred_element_type=F32))
    return jnp.concatenate(states, axis=1)


def project(normed, mix_weight, lanes):
    return jnp.dot(normed, mix_weight[:, lanes], preferred_element_type=F32).astype(BF16)


def mixed(raw, weight, bias):
    raw = raw.astype(F32)
    total = weight[0:1] * raw
    for tap in range(1, weight.shape[0]):
        total = pltpu.roll(total, 1, 0) + weight[tap : tap + 1] * raw
    return silu(total[:-LEAD] + bias).astype(BF16)


def mix_kernel(
    embedded, norm_gain, mix_weight, step_weight, step_bias, log_rate, conv_weight, conv_bias,
    normed_out, x_out, b_out, c_out, b_t_out, step_out, cum_out, scales_out, decay_out, send_out,
):
    col, row = lax.axis_index("cols"), lax.axis_index("rows")
    resid = embedded[...].astype(F32)
    mean_sq = jnp.mean(resid * resid, axis=-1, keepdims=True)
    normed_f = resid * lax.rsqrt(mean_sq + 1e-05) * norm_gain[...]
    rows = lax.broadcasted_iota(jnp.int32, normed_f.shape, 0)
    blank = (rows >= embedded.shape[0] - LEAD) & (col == 0) & (row == 0)
    normed = jnp.where(blank, 0.0, normed_f).astype(BF16)
    normed_out[...] = normed
    length = embedded.shape[0] - LEAD
    maps_raw = project(normed, mix_weight, slice(E, E + 2 * NSTATE))
    step_raw = lax.dot_general(
        normed, step_weight[...], (((1,), (1,)), ((), ())), preferred_element_type=F32
    )[:-LEAD]
    step = softplus(step_raw + step_bias[...])
    log_decay = -step * jnp.exp(log_rate[...])
    lower = (
        lax.broadcasted_iota(jnp.int32, (length, length), 0) >= lax.broadcasted_iota(jnp.int32, (length, length), 1)
    ).astype(BF16)
    high = log_decay.astype(BF16)
    middle = (log_decay - high.astype(F32)).astype(BF16)
    low = (log_decay - high.astype(F32) - middle.astype(F32)).astype(BF16)
    cum = jnp.dot(lower, high, preferred_element_type=F32)
    cum = cum + jnp.dot(lower, middle, preferred_element_type=F32)
    cum = cum + jnp.dot(lower, low, preferred_element_type=F32)
    step_out[...] = step
    cum_out[...] = cum
    parts = half_inputs(1 - row, normed, mix_weight, conv_weight, conv_bias, x_out)
    last = cum[length - 1 :]
    scales = (jnp.exp(last - cum) * step).astype(BF16)
    scales_out[...] = scales
    decay = spread(jnp.broadcast_to(jnp.exp(last), (8, HEADS)), spread_matrix())
    maps = mixed(maps_raw, conv_weight[:, E:], conv_bias[:, E:]).astype(F32)
    b_out[...] = maps[:, :NSTATE].astype(BF16)
    c_out[...] = maps[:, NSTATE:].astype(BF16)
    b_t = maps.T[:NSTATE].astype(BF16)
    b_t_out[...] = b_t
    state = half_state(1 - row, parts, scales, b_t)
    half = E // 2
    first = row == 0
    decay_out[...] = jnp.where(first, decay[:, :half], decay[:, half:])
    send_out[...] = wire(state, jnp.where(first, decay[:, half:], decay[:, :half]))


def rest_kernel(normed, scales, b_t, mix_weight, conv_weight, conv_bias, decay, x_out, keep_out):
    row = lax.axis_index("rows")
    parts = half_inputs(row, normed[...], mix_weight, conv_weight, conv_bias, x_out)
    keep_out[0:NSTATE, :] = half_state(row, parts, scales[...], b_t[...])
    keep_out[NSTATE : NSTATE + 8, :] = decay[...]


TILES = E // 2 // 128
MESSAGE = (TILES * NSTATE + 16, 128)


def wire(values, decay):
    high = decay.astype(BF16).astype(F32)
    place = lax.broadcasted_iota(jnp.int32, (8, 128), 0)
    rows = [jnp.zeros((8, 128), F32)] * 2
    for tile in range(TILES):
        lanes = slice(128 * tile, 128 * (tile + 1))
        for part, piece in enumerate((high, decay - high)):
            rows[part] = jnp.where(place == tile, piece[:, lanes], rows[part])
    columns = [values[:, 128 * tile : 128 * (tile + 1)] for tile in range(TILES)]
    return jnp.concatenate([*columns, *rows], axis=0).astype(BF16)


def unwire(message):
    columns = [message[NSTATE * tile : NSTATE * (tile + 1), :].astype(F32) for tile in range(TILES)]
    rows = message[TILES * NSTATE :, :].astype(F32)
    decay = rows[:8] + rows[8:]
    decays = [jnp.broadcast_to(decay[tile : tile + 1], (8, 128)) for tile in range(TILES)]
    return jnp.concatenate(columns, axis=1), jnp.concatenate(decays, axis=1)


def product(factors):
    total = factors[0]
    for factor in factors[1:]:
        total = total * factor
    return total


def folded(place, pieces):
    places = [place ^ step for step in range(len(pieces))]
    steps = range(len(pieces))
    one = jnp.ones_like(pieces[0][1])
    all_values, ahead_values = None, None
    for step in steps:
        after = [jnp.where(places[k] > places[step], pieces[k][1], one) for k in steps if k != step]
        between = [
            jnp.where((places[k] > places[step]) & (places[k] < place), pieces[k][1], one)
            for k in steps
            if k not in (0, step)
        ]
        term = product(after)[0:1] * pieces[step][0]
        all_values = term if step == 0 else all_values + term
        if step:
            weight = jnp.where(places[step] < place, product([one, *between]), 0.0)
            term = weight[0:1] * pieces[step][0]
            ahead_values = term if ahead_values is None else ahead_values + term
    all_decay = product([decay for _, decay in pieces])
    ahead_decay = product([jnp.where(places[k] < place, pieces[k][1], one) for k in steps if k])
    return (all_values, all_decay), (ahead_values, ahead_decay)


def read(summary):
    return summary[0:NSTATE, :], summary[NSTATE : NSTATE + 8, :]


def write(summary, piece):
    summary[0:NSTATE, :] = piece[0]
    summary[NSTATE : NSTATE + 8, :] = piece[1]


def chained(earlier, latter):
    return latter[1][0:1] * earlier[0] + latter[0], earlier[1] * latter[1]


def pair_kernel(keep, received, total_out, message_out):
    total, _ = folded(lax.axis_index("rows"), [read(keep), unwire(received)])
    write(total_out, total)
    message_out[...] = wire(*total)


def join_kernel(low, count, first, *refs):
    refs = list(refs)
    total = read(refs.pop(0))
    before = None if first else read(refs.pop(0))
    pieces = [total] + [unwire(refs.pop(0)) for _ in range(count - 1)]
    place = (lax.axis_index("cols") // low) & (count - 1)
    total, ahead = folded(place, pieces)
    before_out, message_out = refs[:2]
    write(before_out, ahead if first else chained(ahead, before))
    message_out[...] = wire(*total)
    write(refs[2], total)


def enter_kernel(low, count, first, *refs):
    refs = list(refs)
    total = read(refs.pop(0))
    before = None if first else read(refs.pop(0))
    pieces = [total] + [unwire(refs.pop(0)) for _ in range(count - 1)]
    keep, received, mine_out, theirs_out = refs
    _, ahead = folded((lax.axis_index("cols") // low) & (count - 1), pieces)
    if not first:
        ahead = chained(ahead, before)
    own, other = read(keep), unwire(received)
    upper = lax.axis_index("rows") == 1
    low_piece = tuple(jnp.where(upper, b, a) for a, b in zip(own, other))
    second = chained(ahead, low_piece)[0]
    mine_out[...] = jnp.where(upper, second, ahead[0]).astype(BF16)
    theirs_out[...] = jnp.where(upper, ahead[0], second).astype(BF16)


def gate_kernel(normed, gate_weight, local_mine, local_theirs, cum, own_out, factor_out):
    gate = jnp.dot(normed[...], gate_weight[...], preferred_element_type=F32)[:-LEAD].astype(BF16).astype(F32)
    gate = silu(gate)
    half = local_mine.shape[1]
    upper = lax.axis_index("rows") == 1
    own_out[:, :half] = jnp.where(upper, local_theirs[...], local_mine[...]) * gate[:, :half]
    own_out[:, half:] = jnp.where(upper, local_mine[...], local_theirs[...]) * gate[:, half:]
    factor_out[...] = spread(jnp.exp(cum[...]), spread_matrix()) * gate


def intra_kernel(flip, skip, x, b_mat, c_mat, step, cum, out):
    row = lax.axis_index("rows")
    which = 1 - row if flip else row
    heads = HEADS // 2
    upper = which == 1
    length = x.shape[0]
    half = length // 2
    scores = lax.dot_general(c_mat[...], b_mat[...], (((1,), (1,)), ((), ())), preferred_element_type=F32)
    causal = lax.broadcasted_iota(jnp.int32, (length, length), 0) >= lax.broadcasted_iota(
        jnp.int32, (length, length), 1
    )
    scores = jnp.where(causal, scores, 0.0)
    wide = jnp.zeros((length, 128 - heads), F32)
    cum_v = jnp.where(upper, cum[:, heads:], cum[:, :heads])
    cum_t = jnp.concatenate([cum_v, wide], axis=1).T
    step_t = jnp.concatenate([jnp.where(upper, step[:, heads:], step[:, :heads]), wide], axis=1).T
    for place in range(out.shape[1] // 128):
        pair = place
        lanes = slice(place * 128, (place + 1) * 128)
        x_pair = x[:, lanes].astype(F32)
        lane = lax.broadcasted_iota(jnp.int32, x_pair.shape, 1)
        top = bottom = None
        for member in range(2):
            head = 2 * pair + member
            column = cum_v[:, head : head + 1]
            cum_row = cum_t[head : head + 1, :]
            step_row = step_t[head : head + 1, :]

            def weights(rows, span):
                gap = jnp.minimum(column[rows] - cum_row[:, span], 0.0)
                return (scores[rows, span] * jnp.exp(gap) * step_row[:, span]).astype(BF16)

            inputs = jnp.where((lane < HDIM) == (member == 0), x_pair, 0.0).astype(BF16)
            upper_part = jnp.dot(
                weights(slice(0, half), slice(0, half)), inputs[:half], preferred_element_type=F32
            )
            lower_part = jnp.dot(
                weights(slice(half, length), slice(0, length)), inputs, preferred_element_type=F32
            )
            top = upper_part if top is None else top + upper_part
            bottom = lower_part if bottom is None else bottom + lower_part
        base = which * heads + 2 * pair
        direct = jnp.where(lane < HDIM, skip[base], skip[base + 1]) * x_pair
        out[0:half, lanes] = top + direct[:half]
        out[half:length, lanes] = bottom + direct[half:]


def half_hidden(lanes, state, own, factor, c_mat, out_gain):
    carried = jnp.dot(c_mat[...], state[...], preferred_element_type=F32)
    gated = own[:, lanes] + carried * factor[:, lanes]
    squares = jnp.sum(gated * gated, axis=-1, keepdims=True)
    return (gated * out_gain[:, lanes]).astype(BF16), squares


def first_kernel(mine, own, factor, c_mat, out_gain, out_weight, product_out, squares_out):
    half = own.shape[1] // 2
    lanes = pl.ds(pl.multiple_of(lax.axis_index("rows") * half, 128), half)
    hidden, squares = half_hidden(lanes, mine, own, factor, c_mat, out_gain)
    product = jnp.dot(hidden, out_weight[lanes, :], preferred_element_type=F32)
    product_out[...] = product
    squares_out[...] = jnp.broadcast_to(squares, squares_out.shape)


def finish_kernel(
    theirs, own, factor, c_mat, out_gain, out_weight, product, squares, embedded, out, result, sems
):
    which = 1 - lax.axis_index("rows")
    half = own.shape[1] // 2
    lanes = pl.ds(pl.multiple_of(which * half, 128), half)
    hidden, more = half_hidden(lanes, theirs, own, factor, c_mat, out_gain)
    scale = lax.rsqrt((squares[:, 0:1] + more) / own.shape[1] + 1e-05)
    chunk = result.shape[2]
    copies = []
    for place in range(result.shape[0]):
        span = slice(place * chunk, (place + 1) * chunk)
        rest = jnp.dot(hidden, out_weight[lanes, span], preferred_element_type=F32)
        resid = embedded[:, span].astype(F32)[:-LEAD]
        result[place] = ((product[:, span] + rest) * scale + resid).astype(BF16)
        copies.append(pltpu.make_async_copy(result.at[place], out.at[:, span], sems.at[place]))
        copies[-1].start()
    for copy in copies:
        copy.wait()


def swap(block, axis, bit):
    return lax.ppermute(block, axis, [(i, i ^ bit) for i in range(lax.axis_size(axis))])


def sending_order(side):
    return (*range(side // 2, side), *reversed(range(side // 2)))


def across(block, step):
    side = lax.axis_size("cols") // 2
    pairs = []
    for col in range(2 * side):
        for row in range(2):
            other = side * row + ((col % side) ^ step)
            pairs.append((2 * col + row, 2 * other + col // side))
    return lax.ppermute(block, ("cols", "rows"), pairs)


def embed_by_rows(pixels, patch_weight, patch_bias):
    col_count = lax.axis_size("cols")
    side = col_count // 2
    width = pixels.shape[2]
    partner = swap(pixels, "rows", 1)
    pixels = call(stage_kernel, (pixels,), shape(pixels.shape))
    block = shape((5 * KERNEL + 8, width))
    scratch = [pltpu.VMEM((CHAN, 2 * pixels.shape[1] + 64, width), BF16)]
    blocks = call(pack_kernel, (pixels, partner), [block] * side, scratch, limit=8)
    near, far = [None] * side, [None] * side
    for step in sending_order(side):
        near[step] = across(blocks[step], step)
        far[step] = swap(near[step], "rows", 1)
    came = near + far
    weight = patch_weight.reshape(3, 8, KERNEL, CHAN, D).transpose(2, 0, 3, 1, 4).reshape(KERNEL, WIN, D)
    weight = jnp.pad(weight, ((0, 0), (0, 128 - WIN), (0, 0))).reshape(KERNEL * 128, D)
    tokens = col_count * width // PATCH
    scratch = [
        pltpu.VMEM((tokens + LEAD, KERNEL * 128), BF16),
        pltpu.VMEM((len(neighbours()), tokens + 2 * LEAD, 128), F32),
        pltpu.VMEM((PATCH, 24, 128), F32),
    ]
    return call(
        embed_kernel, (*came, weight, patch_bias.reshape(1, -1)), shape((tokens + LEAD, D)), scratch,
        flops=2 * tokens * KERNEL * 128 * D, moved=6 << 20, limit=16,
    )


def extended(block, sides, width):
    for axis, dim in sides:
        count = lax.axis_size(axis)
        forward = [(i, i + 1) for i in range(count - 1)]
        backward = [(target, source) for source, target in forward]
        low = lax.ppermute(
            lax.slice_in_dim(block, block.shape[dim] - width, None, axis=dim), axis, forward
        )
        high = lax.ppermute(lax.slice_in_dim(block, 0, width, axis=dim), axis, backward)
        block = jnp.concatenate([low, block, high], axis=dim)
    return block


def shifted(block, axis, distance):
    devices = range(lax.axis_size(axis))
    route = [(i - distance, i) for i in devices if i - distance in devices]
    return lax.ppermute(block, axis, route)


def embed_by_blocks(pixels, patch_weight, patch_bias):
    padded = extended(pixels, (("cols", 2), ("rows", 1)), MARGIN)
    embed_grid = lax.conv_general_dilated(
        padded[None],
        patch_weight,
        (PATCH, PATCH),
        "VALID",
        dimension_numbers=("NCHW", "HWIO", "NHWC"),
        preferred_element_type=jnp.float32,
    )[0]
    embed_grid = (embed_grid + patch_bias).astype(jnp.bfloat16)
    row_local, col_local, feature_width = embed_grid.shape
    devices = lax.axis_size(("cols", "rows"))
    row_count = lax.axis_size("rows")
    col_count = lax.axis_size("cols")
    groups = col_count // row_local
    piece_len = col_local * feature_width // devices
    outgoing = embed_grid.reshape(row_local, devices, piece_len)
    spread = lax.all_to_all(outgoing, ("cols", "rows"), split_axis=1, concat_axis=1, tiled=True)
    spread = spread.reshape(row_local, groups, row_local, row_count, piece_len).transpose(
        3, 0, 1, 2, 4
    )
    landed = lax.all_to_all(
        spread.reshape(devices, row_local, piece_len),
        ("cols", "rows"),
        split_axis=0,
        concat_axis=0,
        tiled=True,
    )
    tokens = landed.transpose(1, 0, 2).reshape(row_local * col_local, feature_width)
    tail = shifted(tokens[tokens.shape[0] - LEAD :], ("cols", "rows"), 1)
    return jnp.concatenate([tokens, tail], axis=0)


def body(
    pixels,
    patch_weight,
    patch_bias,
    norm_gain,
    gate_weight,
    mix_weight,
    step_weight,
    step_bias,
    log_rate,
    conv_weight,
    conv_bias,
    skip_gain,
    out_gain,
    out_weight,
):
    col_count = lax.axis_size("cols")
    row_local = pixels.shape[1] // PATCH
    if col_count == row_local and lax.axis_size("rows") == 2:
        embedded = embed_by_rows(pixels, patch_weight, patch_bias)
    else:
        embedded = embed_by_blocks(pixels, patch_weight, patch_bias)
    length = embedded.shape[0] - LEAD
    line = lambda a: a.reshape(1, -1)
    mixed_width = mix_weight.shape[1]
    half = E // 2
    packed = NSTATE + 8
    conv = (conv_weight, line(conv_bias))
    normed, x_theirs, b_mat, c_mat, b_t, step, cum, scales, decay, send = call(
        mix_kernel,
        (embedded, line(norm_gain), mix_weight, step_weight.T, line(step_bias), line(log_rate), *conv),
        [
            shape((LEAD + length, D)), shape((length, half)), shape((length, NSTATE)), shape((length, NSTATE)),
            shape((NSTATE, length)), shape((length, HEADS), F32), shape((length, HEADS), F32),
            shape((length, HEADS)), shape((8, half), F32), shape(MESSAGE),
        ],
        flops=length * D * mixed_width, moved=4 << 20, limit=16,
    )
    came = swap(send, "rows", 1)
    summary, message = shape((packed, half), F32), shape(MESSAGE)
    x_mine, keep = call(
        rest_kernel, (normed, scales, b_t, mix_weight, *conv, decay), [shape((length, half)), summary],
        flops=length * D * mixed_width, moved=4 << 20, limit=16,
    )
    total, out = call(pair_kernel, (keep, came), [summary, message])
    locals_ = []
    for part in range(2):
        locals_.append(
            call(
                partial(intra_kernel, bool(part)), (skip_gain, (x_mine, x_theirs)[part], b_mat, c_mat, step, cum),
                shape((length, half), F32), scalars=1,
                flops=HEADS * length * length * 128, moved=2 << 20, limit=8,
            )
        )
    own, factor = call(
        gate_kernel, (normed, gate_weight, *locals_, cum), [shape((length, E), F32)] * 2,
        flops=2 * length * D * E, moved=4 << 20, limit=8,
    )
    groups, low = [], 1
    while low < col_count:
        count = min(4, col_count // low)
        groups.append((low, count))
        low *= count
    before = None
    for number, (low, count) in enumerate(groups):
        ending = number + 1 == len(groups)
        arrived = []
        for hop in range(1, count):
            arrived.append(swap(out, "cols", hop * low))
        first = before is None
        inputs = ([total] if first else [total, before]) + arrived
        if ending:
            entering = shape((NSTATE, half))
            mine, theirs = call(partial(enter_kernel, low, count, first), (*inputs, keep, came), [entering, entering])
        else:
            before, out, total = call(partial(join_kernel, low, count, first), inputs, [summary, message, summary])
    theirs = swap(theirs, "rows", 1)
    common = (own, factor, c_mat, line(out_gain), out_weight)
    partial_sum, squares = call(
        first_kernel, (mine, *common), [shape((length, D), F32), shape((length, 128), F32)],
        flops=length * D * E, moved=4 << 20, limit=8,
    )
    return call(
        finish_kernel, (theirs, *common, partial_sum, squares, embedded), shape((length, D)),
        [pltpu.VMEM((3, length, D // 3), BF16), pltpu.SemaphoreType.DMA((3,))],
        flops=length * D * E, moved=4 << 20, limit=8, outside=True,
    )


def solution(mesh):
    placed = (
        P(None, "rows", ("slides", "cols")),
        P(),
        P(),
        P(),
        P(),
        P(),
        P(),
        P(),
        P(),
        P(),
        P(),
        P(),
        P(),
        P(),
    )
    return jax.shard_map(
        body,
        mesh=mesh,
        in_specs=placed,
        out_specs=P(("slides", "cols", "rows"), None),
        check_vma=False,
    )
```

```python
from functools import partial

import jax
import jax.numpy as jnp
from jax import lax
from jax.experimental import pallas as pl
from jax.experimental.pallas import tpu as pltpu
from jax.sharding import PartitionSpec as P


E = 1536
D = 768
HDIM = 64
NSTATE = 64
PATCH = 16
KERNEL = 24
HEADS = 24
CHAN = 3
MARGIN = (KERNEL - PATCH) // 2
WIN = CHAN * KERNEL
LEAD = 8
F32 = jnp.float32
BF16 = jnp.bfloat16


def vmem():
    return pl.BlockSpec(memory_space=pltpu.VMEM)


def call(kernel, inputs, outs, scratch=(), limit=4, flops=0, moved=0, scalars=0, outside=False):
    return pl.pallas_call(
        kernel,
        out_shape=outs,
        in_specs=[pl.BlockSpec(memory_space=pltpu.SMEM)] * scalars + [vmem()] * (len(inputs) - scalars),
        out_specs=jax.tree.map(lambda _: pl.BlockSpec(memory_space=pl.ANY) if outside else vmem(), outs),
        scratch_shapes=scratch,
        compiler_params=pltpu.CompilerParams(vmem_limit_bytes=limit << 20),
        cost_estimate=pl.CostEstimate(flops=flops, bytes_accessed=moved, transcendentals=0),
    )(*inputs)


def shape(dims, kind=BF16):
    return jax.ShapeDtypeStruct(dims, kind)


def pack_kernel(own, partner, *refs):
    outs, rows = refs[:-1], refs[-1]
    col, row = lax.axis_index("cols"), lax.axis_index("rows")
    local = own.shape[1]
    width = own.shape[2]
    edge = jnp.zeros((CHAN, 32, width), BF16)
    rows[:, 0:32, :] = edge
    rows[:, 32 + 2 * local : 64 + 2 * local, :] = edge
    rows[:, pl.ds(pl.multiple_of(32 + local * row, 32), local), :] = own[...]
    rows[:, pl.ds(pl.multiple_of(32 + local * (1 - row), 32), local), :] = partner[...]
    side = len(outs)
    for step, out in enumerate(outs):
        chip = side * row + ((col % side) ^ step)
        first = pl.multiple_of(2 * PATCH * chip, 32)
        blocks = [rows[channel, pl.ds(first, 80), :].astype(F32) for channel in range(CHAN)]
        pieces = [block[28 + 8 * group : 36 + 8 * group] for group in range(5) for block in blocks]
        tails = [block[12 + 8 * group : 20 + 8 * group, width - 64 :] for group in range(2) for block in blocks]
        tails.append(jnp.zeros((8, width - 64 * len(tails)), F32))
        out[...] = jnp.concatenate([*pieces, jnp.concatenate(tails, axis=1)], axis=0).astype(BF16)


def stage_kernel(pixels, out):
    out[...] = pixels[...]


def pick_matrix():
    row = lax.broadcasted_iota(jnp.int32, (256, 256), 0)
    pixel = lax.broadcasted_iota(jnp.int32, (256, 256), 1)
    return (pixel == (row & 15) * PATCH + (row >> 4)).astype(BF16)


def turned(pick, values):
    return lax.dot_general(pick, values, (((1,), (1,)), ((), ())), preferred_element_type=F32)


def window_pixel(offset):
    place = offset - MARGIN + PATCH
    return place % PATCH, place // PATCH - 1


def neighbours():
    return [offset for offset in range(KERNEL) if window_pixel(offset)[1]]


def place_tokens(pick, values, first, wide, beside):
    both = jnp.concatenate([values[:, :256], values[:, 256:]], axis=0)
    found = turned(pick, both).reshape(PATCH, 16, 256)
    for group in range(2):
        piece = found[:, :, 128 * group : 128 * (group + 1)]
        rounded = piece.astype(BF16)
        rows = pl.ds(pl.multiple_of(first + 16 * group, 16), 16)
        for offset in range(KERNEL):
            pixel, shift = window_pixel(offset)
            if shift == 0:
                wide[rows, offset * 128 : (offset + 1) * 128] = rounded[pixel]
        rows = pl.ds(pl.multiple_of(LEAD + first + 16 * group, 8), 16)
        for slot, offset in enumerate(neighbours()):
            beside[slot, rows, :] = piece[window_pixel(offset)[0]]


def place_beside(count, first, wide, beside):
    for slot, offset in enumerate(neighbours()):
        start = LEAD + window_pixel(offset)[1]
        part = beside[slot, start : start + count, :]
        wide[first : first + count, offset * 128 : (offset + 1) * 128] = part.astype(BF16)


def clear_ends(count, beside):
    zeros = jnp.zeros((beside.shape[0], LEAD, 128), F32)
    beside[:, 0:LEAD, :] = zeros
    beside[:, LEAD + count : LEAD + count + LEAD, :] = zeros


def windows_of(block, row, lanes):
    window = pl.ds(pl.multiple_of(2 * KERNEL * row, 16), WIN)
    values = block[window, lanes]
    return jnp.concatenate([values, jnp.zeros((128 - WIN, values.shape[1]), BF16)], axis=0)


def embed_kernel(*refs):
    blocks, (weight, bias, out, wide, beside, tail) = refs[:-6], refs[-6:]
    col, row = lax.axis_index("cols"), lax.axis_index("rows")
    count = len(blocks)
    side = count // 2
    width = blocks[0].shape[1]
    tokens = count * width // PATCH
    pick = pick_matrix()
    clear_ends(tokens, beside)
    edge = jnp.zeros((WIN, 128), F32)
    extra = jnp.zeros((8, 128 * CHAN), F32)
    for place, block in enumerate(blocks):
        source = side * (row if place < side else 1 - row) + ((col % side) ^ (place % side))
        for group in range(width // 512):
            first = source * (width // PATCH) + 32 * group
            place_tokens(pick, windows_of(block, row, slice(512 * group, 512 * (group + 1))), first, wide, beside)
        last = source == count - 1
        edge = jnp.where(last, block[0:WIN, width - 128 :].astype(F32), edge)
        extra = jnp.where(last, block[5 * KERNEL - 8 : 5 * KERNEL + 8, : 128 * CHAN].astype(F32)[8:], extra)
    before = [extra[:, 64 * piece : 64 * (piece + 1)] for piece in range(2 * CHAN)] + [edge[:KERNEL, 64:]]
    last = jnp.where(row == 0, jnp.concatenate(before, axis=0), edge[:, 64:])
    last = jnp.concatenate([last, jnp.zeros((128 - WIN, 64), F32)], axis=0)
    last = jnp.concatenate([jnp.zeros((128, 64), F32), last, jnp.zeros((128, 128), F32)], axis=1)
    tail[:, 0:8, :] = jnp.zeros((PATCH, 8, 128), F32)
    tail[:, 8:24, :] = turned(pick, last.astype(BF16)).reshape(PATCH, 16, 128)
    for offset in range(KERNEL):
        pixel, shift = window_pixel(offset)
        part = tail[pixel, 8 + shift : 16 + shift, :]
        wide[tokens:, offset * 128 : (offset + 1) * 128] = part.astype(BF16)
    place_beside(tokens, 0, wide, beside)
    for first in range(0, D, 256):
        lanes = slice(first, first + 256)
        grid = jnp.dot(wide[...], weight[:, lanes], preferred_element_type=F32)
        out[:, lanes] = (grid + bias[:, lanes]).astype(BF16)


def spread_matrix():
    head = lax.broadcasted_iota(jnp.int32, (HEADS, E), 0)
    lane = lax.broadcasted_iota(jnp.int32, (HEADS, E), 1)
    return ((lane >= head * HDIM) & (lane < (head + 1) * HDIM)).astype(BF16)


def halves(values):
    high = values.astype(BF16)
    return high, (values - high.astype(F32)).astype(BF16)


def spread(values, matrix):
    high, low = halves(values)
    return jnp.dot(high, matrix, preferred_element_type=F32) + jnp.dot(low, matrix, preferred_element_type=F32)


def silu(values):
    half = 0.5 * values
    return half + half * jnp.tanh(half)


def softplus(values):
    small = jnp.exp(-jnp.abs(values))
    return jnp.maximum(values, 0.0) + jnp.log1p(small)


def half_inputs(which, normed, mix_weight, conv_weight, conv_bias, x_out):
    half = E // 2
    chunk = 384
    parts = []
    spans = [
        pl.ds(pl.multiple_of(which * half + first, 128), chunk) for first in range(0, half, chunk)
    ]
    ahead = project(normed, mix_weight, spans[0])
    for place, lanes in enumerate(spans):
        raw = ahead
        if place + 1 < len(spans):
            ahead = project(normed, mix_weight, spans[place + 1])
        part = mixed(raw, conv_weight[:, lanes], conv_bias[:, lanes])
        x_out[:, place * chunk : (place + 1) * chunk] = part
        parts.append(part)
    return parts


def half_state(which, parts, scales, b_t):
    half = E // 2
    matrix = spread_matrix().astype(F32)
    wanted = jnp.where(which == 0, matrix[:, :half], matrix[:, half:]).astype(BF16)
    states = []
    for place, part in enumerate(parts):
        chunk = part.shape[1]
        to_end = jnp.dot(scales, wanted[:, place * chunk : (place + 1) * chunk], preferred_element_type=F32)
        scaled = (part.astype(F32) * to_end).astype(BF16)
        states.append(jnp.dot(b_t, scaled, preferred_element_type=F32))
    return jnp.concatenate(states, axis=1)


def project(normed, mix_weight, lanes):
    return jnp.dot(normed, mix_weight[:, lanes], preferred_element_type=F32).astype(BF16)


def mixed(raw, weight, bias):
    raw = raw.astype(F32)
    total = weight[0:1] * raw
    for tap in range(1, weight.shape[0]):
        total = pltpu.roll(total, 1, 0) + weight[tap : tap + 1] * raw
    return silu(total[:-LEAD] + bias).astype(BF16)


def mix_kernel(
    embedded, norm_gain, mix_weight, step_weight, step_bias, log_rate, conv_weight, conv_bias,
    normed_out, x_out, b_out, c_out, b_t_out, step_out, cum_out, scales_out, decay_out, send_out,
):
    col, row = lax.axis_index("cols"), lax.axis_index("rows")
    resid = embedded[...].astype(F32)
    mean_sq = jnp.mean(resid * resid, axis=-1, keepdims=True)
    normed_f = resid * lax.rsqrt(mean_sq + 1e-05) * norm_gain[...]
    rows = lax.broadcasted_iota(jnp.int32, normed_f.shape, 0)
    blank = (rows >= embedded.shape[0] - LEAD) & (col == 0) & (row == 0)
    normed = jnp.where(blank, 0.0, normed_f).astype(BF16)
    normed_out[...] = normed
    length = embedded.shape[0] - LEAD
    maps_raw = project(normed, mix_weight, slice(E, E + 2 * NSTATE))
    step_raw = lax.dot_general(
        normed, step_weight[...], (((1,), (1,)), ((), ())), preferred_element_type=F32
    )[:-LEAD]
    step = softplus(step_raw + step_bias[...])
    log_decay = -step * jnp.exp(log_rate[...])
    lower = (
        lax.broadcasted_iota(jnp.int32, (length, length), 0) >= lax.broadcasted_iota(jnp.int32, (length, length), 1)
    ).astype(BF16)
    high = log_decay.astype(BF16)
    middle = (log_decay - high.astype(F32)).astype(BF16)
    low = (log_decay - high.astype(F32) - middle.astype(F32)).astype(BF16)
    cum = jnp.dot(lower, high, preferred_element_type=F32)
    cum = cum + jnp.dot(lower, middle, preferred_element_type=F32)
    cum = cum + jnp.dot(lower, low, preferred_element_type=F32)
    step_out[...] = step
    cum_out[...] = cum
    parts = half_inputs(1 - row, normed, mix_weight, conv_weight, conv_bias, x_out)
    last = cum[length - 1 :]
    scales = (jnp.exp(last - cum) * step).astype(BF16)
    scales_out[...] = scales
    decay = spread(jnp.broadcast_to(jnp.exp(last), (8, HEADS)), spread_matrix())
    maps = mixed(maps_raw, conv_weight[:, E:], conv_bias[:, E:]).astype(F32)
    b_out[...] = maps[:, :NSTATE].astype(BF16)
    c_out[...] = maps[:, NSTATE:].astype(BF16)
    b_t = maps.T[:NSTATE].astype(BF16)
    b_t_out[...] = b_t
    state = half_state(1 - row, parts, scales, b_t)
    half = E // 2
    first = row == 0
    decay_out[...] = jnp.where(first, decay[:, :half], decay[:, half:])
    send_out[...] = wire(state, jnp.where(first, decay[:, half:], decay[:, :half]))


def rest_kernel(normed, scales, b_t, mix_weight, conv_weight, conv_bias, decay, x_out, keep_out):
    row = lax.axis_index("rows")
    parts = half_inputs(row, normed[...], mix_weight, conv_weight, conv_bias, x_out)
    keep_out[0:NSTATE, :] = half_state(row, parts, scales[...], b_t[...])
    keep_out[NSTATE : NSTATE + 8, :] = decay[...]


TILES = E // 2 // 128
MESSAGE = (TILES * NSTATE + 16, 128)


def wire(values, decay):
    high = decay.astype(BF16).astype(F32)
    place = lax.broadcasted_iota(jnp.int32, (8, 128), 0)
    rows = [jnp.zeros((8, 128), F32)] * 2
    for tile in range(TILES):
        lanes = slice(128 * tile, 128 * (tile + 1))
        for part, piece in enumerate((high, decay - high)):
            rows[part] = jnp.where(place == tile, piece[:, lanes], rows[part])
    columns = [values[:, 128 * tile : 128 * (tile + 1)] for tile in range(TILES)]
    return jnp.concatenate([*columns, *rows], axis=0).astype(BF16)


def unwire(message):
    columns = [message[NSTATE * tile : NSTATE * (tile + 1), :].astype(F32) for tile in range(TILES)]
    rows = message[TILES * NSTATE :, :].astype(F32)
    decay = rows[:8] + rows[8:]
    decays = [jnp.broadcast_to(decay[tile : tile + 1], (8, 128)) for tile in range(TILES)]
    return jnp.concatenate(columns, axis=1), jnp.concatenate(decays, axis=1)


def product(factors):
    total = factors[0]
    for factor in factors[1:]:
        total = total * factor
    return total


def folded(place, pieces):
    places = [place ^ step for step in range(len(pieces))]
    steps = range(len(pieces))
    one = jnp.ones_like(pieces[0][1])
    all_values, ahead_values = None, None
    for step in steps:
        after = [jnp.where(places[k] > places[step], pieces[k][1], one) for k in steps if k != step]
        between = [
            jnp.where((places[k] > places[step]) & (places[k] < place), pieces[k][1], one)
            for k in steps
            if k not in (0, step)
        ]
        term = product(after)[0:1] * pieces[step][0]
        all_values = term if step == 0 else all_values + term
        if step:
            weight = jnp.where(places[step] < place, product([one, *between]), 0.0)
            term = weight[0:1] * pieces[step][0]
            ahead_values = term if ahead_values is None else ahead_values + term
    all_decay = product([decay for _, decay in pieces])
    ahead_decay = product([jnp.where(places[k] < place, pieces[k][1], one) for k in steps if k])
    return (all_values, all_decay), (ahead_values, ahead_decay)


def read(summary):
    return summary[0:NSTATE, :], summary[NSTATE : NSTATE + 8, :]


def write(summary, piece):
    summary[0:NSTATE, :] = piece[0]
    summary[NSTATE : NSTATE + 8, :] = piece[1]


def chained(earlier, latter):
    return latter[1][0:1] * earlier[0] + latter[0], earlier[1] * latter[1]


def pair_kernel(keep, received, total_out, message_out):
    total, _ = folded(lax.axis_index("rows"), [read(keep), unwire(received)])
    write(total_out, total)
    message_out[...] = wire(*total)


def join_kernel(low, count, first, *refs):
    refs = list(refs)
    total = read(refs.pop(0))
    before = None if first else read(refs.pop(0))
    pieces = [total] + [unwire(refs.pop(0)) for _ in range(count - 1)]
    place = (lax.axis_index("cols") // low) & (count - 1)
    total, ahead = folded(place, pieces)
    before_out, message_out = refs[:2]
    write(before_out, ahead if first else chained(ahead, before))
    message_out[...] = wire(*total)
    write(refs[2], total)


def enter_kernel(low, count, first, *refs):
    refs = list(refs)
    total = read(refs.pop(0))
    before = None if first else read(refs.pop(0))
    pieces = [total] + [unwire(refs.pop(0)) for _ in range(count - 1)]
    keep, received, mine_out, theirs_out = refs
    _, ahead = folded((lax.axis_index("cols") // low) & (count - 1), pieces)
    if not first:
        ahead = chained(ahead, before)
    own, other = read(keep), unwire(received)
    upper = lax.axis_index("rows") == 1
    low_piece = tuple(jnp.where(upper, b, a) for a, b in zip(own, other))
    second = chained(ahead, low_piece)[0]
    mine_out[...] = jnp.where(upper, second, ahead[0]).astype(BF16)
    theirs_out[...] = jnp.where(upper, ahead[0], second).astype(BF16)


def gate_kernel(normed, gate_weight, local_mine, local_theirs, cum, own_out, factor_out):
    gate = jnp.dot(normed[...], gate_weight[...], preferred_element_type=F32)[:-LEAD].astype(BF16).astype(F32)
    gate = silu(gate)
    half = local_mine.shape[1]
    upper = lax.axis_index("rows") == 1
    own_out[:, :half] = jnp.where(upper, local_theirs[...], local_mine[...]) * gate[:, :half]
    own_out[:, half:] = jnp.where(upper, local_mine[...], local_theirs[...]) * gate[:, half:]
    factor_out[...] = spread(jnp.exp(cum[...]), spread_matrix()) * gate


def intra_kernel(flip, skip, x, b_mat, c_mat, step, cum, out):
    row = lax.axis_index("rows")
    which = 1 - row if flip else row
    heads = HEADS // 2
    upper = which == 1
    length = x.shape[0]
    half = length // 2
    scores = lax.dot_general(c_mat[...], b_mat[...], (((1,), (1,)), ((), ())), preferred_element_type=F32)
    causal = lax.broadcasted_iota(jnp.int32, (length, length), 0) >= lax.broadcasted_iota(
        jnp.int32, (length, length), 1
    )
    scores = jnp.where(causal, scores, 0.0)
    wide = jnp.zeros((length, 128 - heads), F32)
    cum_v = jnp.where(upper, cum[:, heads:], cum[:, :heads])
    cum_t = jnp.concatenate([cum_v, wide], axis=1).T
    step_t = jnp.concatenate([jnp.where(upper, step[:, heads:], step[:, :heads]), wide], axis=1).T
    for place in range(out.shape[1] // 128):
        pair = place
        lanes = slice(place * 128, (place + 1) * 128)
        x_pair = x[:, lanes].astype(F32)
        lane = lax.broadcasted_iota(jnp.int32, x_pair.shape, 1)
        top = bottom = None
        for member in range(2):
            head = 2 * pair + member
            column = cum_v[:, head : head + 1]
            cum_row = cum_t[head : head + 1, :]
            step_row = step_t[head : head + 1, :]

            def weights(rows, span):
                gap = jnp.minimum(column[rows] - cum_row[:, span], 0.0)
                return (scores[rows, span] * jnp.exp(gap) * step_row[:, span]).astype(BF16)

            inputs = jnp.where((lane < HDIM) == (member == 0), x_pair, 0.0).astype(BF16)
            upper_part = jnp.dot(
                weights(slice(0, half), slice(0, half)), inputs[:half], preferred_element_type=F32
            )
            lower_part = jnp.dot(
                weights(slice(half, length), slice(0, length)), inputs, preferred_element_type=F32
            )
            top = upper_part if top is None else top + upper_part
            bottom = lower_part if bottom is None else bottom + lower_part
        base = which * heads + 2 * pair
        direct = jnp.where(lane < HDIM, skip[base], skip[base + 1]) * x_pair
        out[0:half, lanes] = top + direct[:half]
        out[half:length, lanes] = bottom + direct[half:]


def half_hidden(lanes, state, own, factor, c_mat, out_gain):
    carried = jnp.dot(c_mat[...], state[...], preferred_element_type=F32)
    gated = own[:, lanes] + carried * factor[:, lanes]
    squares = jnp.sum(gated * gated, axis=-1, keepdims=True)
    return (gated * out_gain[:, lanes]).astype(BF16), squares


def first_kernel(mine, own, factor, c_mat, out_gain, out_weight, product_out, squares_out):
    half = own.shape[1] // 2
    lanes = pl.ds(pl.multiple_of(lax.axis_index("rows") * half, 128), half)
    hidden, squares = half_hidden(lanes, mine, own, factor, c_mat, out_gain)
    product = jnp.dot(hidden, out_weight[lanes, :], preferred_element_type=F32)
    product_out[...] = product
    squares_out[...] = jnp.broadcast_to(squares, squares_out.shape)


def finish_kernel(
    theirs, own, factor, c_mat, out_gain, out_weight, product, squares, embedded, out, result, sems
):
    which = 1 - lax.axis_index("rows")
    half = own.shape[1] // 2
    lanes = pl.ds(pl.multiple_of(which * half, 128), half)
    hidden, more = half_hidden(lanes, theirs, own, factor, c_mat, out_gain)
    scale = lax.rsqrt((squares[:, 0:1] + more) / own.shape[1] + 1e-05)
    chunk = result.shape[1]
    copies = []
    rest = jnp.dot(hidden, out_weight[lanes, :], preferred_element_type=F32)
    for place in range(result.shape[0]):
        rows = slice(place * chunk, (place + 1) * chunk)
        resid = embedded[rows, :].astype(F32)
        result[place] = ((product[rows, :] + rest[rows]) * scale[rows] + resid).astype(BF16)
        copies.append(pltpu.make_async_copy(result.at[place], out.at[rows, :], sems.at[place]))
        copies[-1].start()
    for copy in copies:
        copy.wait()


def swap(block, axis, bit):
    return lax.ppermute(block, axis, [(i, i ^ bit) for i in range(lax.axis_size(axis))])


def sending_order(side):
    return (*range(side // 2, side), *reversed(range(side // 2)))


def across(block, step):
    side = lax.axis_size("cols") // 2
    pairs = []
    for col in range(2 * side):
        for row in range(2):
            other = side * row + ((col % side) ^ step)
            pairs.append((2 * col + row, 2 * other + col // side))
    return lax.ppermute(block, ("cols", "rows"), pairs)


def embed_by_rows(pixels, patch_weight, patch_bias):
    col_count = lax.axis_size("cols")
    side = col_count // 2
    width = pixels.shape[2]
    partner = swap(pixels, "rows", 1)
    pixels = call(stage_kernel, (pixels,), shape(pixels.shape))
    block = shape((5 * KERNEL + 8, width))
    scratch = [pltpu.VMEM((CHAN, 2 * pixels.shape[1] + 64, width), BF16)]
    blocks = call(pack_kernel, (pixels, partner), [block] * side, scratch, limit=8)
    near, far = [None] * side, [None] * side
    for step in sending_order(side):
        near[step] = across(blocks[step], step)
        far[step] = swap(near[step], "rows", 1)
    came = near + far
    weight = patch_weight.reshape(3, 8, KERNEL, CHAN, D).transpose(2, 0, 3, 1, 4).reshape(KERNEL, WIN, D)
    weight = jnp.pad(weight, ((0, 0), (0, 128 - WIN), (0, 0))).reshape(KERNEL * 128, D)
    tokens = col_count * width // PATCH
    scratch = [
        pltpu.VMEM((tokens + LEAD, KERNEL * 128), BF16),
        pltpu.VMEM((len(neighbours()), tokens + 2 * LEAD, 128), F32),
        pltpu.VMEM((PATCH, 24, 128), F32),
    ]
    return call(
        embed_kernel, (*came, weight, patch_bias.reshape(1, -1)), shape((tokens + LEAD, D)), scratch,
        flops=2 * tokens * KERNEL * 128 * D, moved=6 << 20, limit=16,
    )


def extended(block, sides, width):
    for axis, dim in sides:
        count = lax.axis_size(axis)
        forward = [(i, i + 1) for i in range(count - 1)]
        backward = [(target, source) for source, target in forward]
        low = lax.ppermute(
            lax.slice_in_dim(block, block.shape[dim] - width, None, axis=dim), axis, forward
        )
        high = lax.ppermute(lax.slice_in_dim(block, 0, width, axis=dim), axis, backward)
        block = jnp.concatenate([low, block, high], axis=dim)
    return block


def shifted(block, axis, distance):
    devices = range(lax.axis_size(axis))
    route = [(i - distance, i) for i in devices if i - distance in devices]
    return lax.ppermute(block, axis, route)


def embed_by_blocks(pixels, patch_weight, patch_bias):
    padded = extended(pixels, (("cols", 2), ("rows", 1)), MARGIN)
    embed_grid = lax.conv_general_dilated(
        padded[None],
        patch_weight,
        (PATCH, PATCH),
        "VALID",
        dimension_numbers=("NCHW", "HWIO", "NHWC"),
        preferred_element_type=jnp.float32,
    )[0]
    embed_grid = (embed_grid + patch_bias).astype(jnp.bfloat16)
    row_local, col_local, feature_width = embed_grid.shape
    devices = lax.axis_size(("cols", "rows"))
    row_count = lax.axis_size("rows")
    col_count = lax.axis_size("cols")
    groups = col_count // row_local
    piece_len = col_local * feature_width // devices
    outgoing = embed_grid.reshape(row_local, devices, piece_len)
    spread = lax.all_to_all(outgoing, ("cols", "rows"), split_axis=1, concat_axis=1, tiled=True)
    spread = spread.reshape(row_local, groups, row_local, row_count, piece_len).transpose(
        3, 0, 1, 2, 4
    )
    landed = lax.all_to_all(
        spread.reshape(devices, row_local, piece_len),
        ("cols", "rows"),
        split_axis=0,
        concat_axis=0,
        tiled=True,
    )
    tokens = landed.transpose(1, 0, 2).reshape(row_local * col_local, feature_width)
    tail = shifted(tokens[tokens.shape[0] - LEAD :], ("cols", "rows"), 1)
    return jnp.concatenate([tokens, tail], axis=0)


def body(
    pixels,
    patch_weight,
    patch_bias,
    norm_gain,
    gate_weight,
    mix_weight,
    step_weight,
    step_bias,
    log_rate,
    conv_weight,
    conv_bias,
    skip_gain,
    out_gain,
    out_weight,
):
    col_count = lax.axis_size("cols")
    row_local = pixels.shape[1] // PATCH
    if col_count == row_local and lax.axis_size("rows") == 2:
        embedded = embed_by_rows(pixels, patch_weight, patch_bias)
    else:
        embedded = embed_by_blocks(pixels, patch_weight, patch_bias)
    length = embedded.shape[0] - LEAD
    line = lambda a: a.reshape(1, -1)
    mixed_width = mix_weight.shape[1]
    half = E // 2
    packed = NSTATE + 8
    conv = (conv_weight, line(conv_bias))
    normed, x_theirs, b_mat, c_mat, b_t, step, cum, scales, decay, send = call(
        mix_kernel,
        (embedded, line(norm_gain), mix_weight, step_weight.T, line(step_bias), line(log_rate), *conv),
        [
            shape((LEAD + length, D)), shape((length, half)), shape((length, NSTATE)), shape((length, NSTATE)),
            shape((NSTATE, length)), shape((length, HEADS), F32), shape((length, HEADS), F32),
            shape((length, HEADS)), shape((8, half), F32), shape(MESSAGE),
        ],
        flops=length * D * mixed_width, moved=4 << 20, limit=16,
    )
    came = swap(send, "rows", 1)
    summary, message = shape((packed, half), F32), shape(MESSAGE)
    x_mine, keep = call(
        rest_kernel, (normed, scales, b_t, mix_weight, *conv, decay), [shape((length, half)), summary],
        flops=length * D * mixed_width, moved=4 << 20, limit=16,
    )
    total, out = call(pair_kernel, (keep, came), [summary, message])
    locals_ = []
    for part in range(2):
        locals_.append(
            call(
                partial(intra_kernel, bool(part)), (skip_gain, (x_mine, x_theirs)[part], b_mat, c_mat, step, cum),
                shape((length, half), F32), scalars=1,
                flops=HEADS * length * length * 128, moved=2 << 20, limit=8,
            )
        )
    own, factor = call(
        gate_kernel, (normed, gate_weight, *locals_, cum), [shape((length, E), F32)] * 2,
        flops=2 * length * D * E, moved=4 << 20, limit=8,
    )
    groups, low = [], 1
    while low < col_count:
        count = min(4, col_count // low)
        groups.append((low, count))
        low *= count
    before = None
    for number, (low, count) in enumerate(groups):
        ending = number + 1 == len(groups)
        arrived = []
        for hop in range(1, count):
            arrived.append(swap(out, "cols", hop * low))
        first = before is None
        inputs = ([total] if first else [total, before]) + arrived
        if ending:
            entering = shape((NSTATE, half))
            mine, theirs = call(partial(enter_kernel, low, count, first), (*inputs, keep, came), [entering, entering])
        else:
            before, out, total = call(partial(join_kernel, low, count, first), inputs, [summary, message, summary])
    theirs = swap(theirs, "rows", 1)
    common = (own, factor, c_mat, line(out_gain), out_weight)
    partial_sum, squares = call(
        first_kernel, (mine, *common), [shape((length, D), F32), shape((length, 128), F32)],
        flops=length * D * E, moved=4 << 20, limit=8,
    )
    return call(
        finish_kernel, (theirs, *common, partial_sum, squares, embedded), shape((length, D)),
        [pltpu.VMEM((8, length // 8, D), BF16), pltpu.SemaphoreType.DMA((8,))],
        flops=length * D * E, moved=4 << 20, limit=8, outside=True,
    )


def solution(mesh):
    placed = (
        P(None, "rows", ("slides", "cols")),
        P(),
        P(),
        P(),
        P(),
        P(),
        P(),
        P(),
        P(),
        P(),
        P(),
        P(),
        P(),
        P(),
    )
    return jax.shard_map(
        body,
        mesh=mesh,
        in_specs=placed,
        out_specs=P(("slides", "cols", "rows"), None),
        check_vma=False,
    )
```
